32 devices in a mesh: groups: 2 (over y), pool: 16 (over z, x, core), tp: 1.
Axes of the slice: x: 2, y: 2, z: 4, core: 2. Of those that a mesh axis runs over, the one named last changes fastest.
Arguments:
- suffix_q: bfloat16 [16384, 4096], P(('groups', 'pool'), 'tp'), parts along dimension 0, may hold values from -140 to 140
- fresh_kv: bfloat16 [2048, 2, 8, 512], P(('groups', 'pool'), None, None, 'tp'), parts along dimension 0, may hold values from -6 to 6
- kv_pool: bfloat16 [16384, 2, 8, 512], P(('groups', 'pool'), None, None, 'tp'), parts along dimension 0, may hold values from -6 to 6
- dec_q: bfloat16 [1024, 4096], P(('groups', 'pool'), 'tp'), parts along dimension 0, may hold values from -140 to 140
- fetch_slots: int32 [32, 256], P(('groups', 'pool')), parts along dimension 0, may hold values from 0 to 511, as said below
- prefix_pages: int32 [32, 256], P(('groups', 'pool')), parts along dimension 0, may hold values from 0 to 255, as said below
- prefix_len: int32 [32], P(('groups', 'pool')), parts along dimension 0, may hold values from 8 to 2048, as said below
- suffix_route: int32 [32, 64], P(('groups', 'pool')), parts along dimension 0, may hold values from 0 to 63, as said below
- dec_pages: int32 [1024, 64], P(('groups', 'pool')), parts along dimension 0, may hold values from 0 to 575, as said below
- dec_len: int32 [1024], P(('groups', 'pool')), parts along dimension 0, may hold values from 72 to 512, as said below
Outputs:
- suffix_out: bfloat16 [16384, 4096], P(('groups', 'pool'), 'tp'), parts along dimension 0
- decode_out: bfloat16 [1024, 4096], P(('groups', 'pool'), 'tp'), parts along dimension 0
The draws below stay inside these ranges and needn't reach their ends.
There are 2 independent parts, one for each index of `groups`. The reference program is written for one: setup_inputs(seed, part) draws one part's arguments, and reference() takes and returns one part's arrays. A program takes and returns all parts, laid end to end along the dimension named above; each array names one. Nothing has to cross between parts.
Inputs may be any that keep to these rules, and one draw needn't show every extreme that they name: `fetch_slots`: entry r * 16 + c of row s names the page of device s's pool that fills slot c of requester r from s. `prefix_pages`: each row is a permutation; entry k names the fetched slot s * 16 + c that holds prefix page k. `prefix_len`: some prompt has the most. `suffix_route`: each row is a permutation; entry o * 4 + c names the fresh page sent to owner o as its c-th page from that device. `dec_pages`: entries below 512 name pages of the owner's own pool; 512 + s * 4 + c names the c-th page received from device s; each of these 64 names stands exactly once among an owner's 32 rows, within their first 8 entries. `dec_len`: some request has the most.
All inputs are finite; a program needn't handle non-finite values.
Results may differ from the reference program's by a relative error of at most 0.008.
Values may be sent and summed in bfloat16 or wider, within the bound.
No kernel may reach another device: no remote copies, remote signals or barrier semaphores. Data moves between devices by JAX's collectives and lax.ppermute only.
A program may use at most 256 MiB of HBM per device.

```python
import jax
import jax.numpy as jnp
from jax import lax

QH = 32
KVH = 4
HD = 128
PAGE = 8
DMIN = 8
SUF = 512
PMAX = 256
SLOTS = 512
DEC = 32
DPMAX = 64
CAP = 16
SPAGES = 64
CAPS = 4
FPR = 2
N_POOL = 16


def permutations(subkey, count, length):

    def single(inner_key):
        return jax.random.permutation(inner_key, length).astype(jnp.int32)
    return jax.vmap(single)(jax.random.split(subkey, count))


def fresh_tokens(key):
    samples = jnp.clip(jax.random.normal(jax.random.fold_in(key, 101), (N_POOL, 2, SUF, KVH * HD), jnp.float32), -4.5, 4.5)
    return samples


def pool_values(key):
    samples = jnp.clip(jax.random.normal(jax.random.fold_in(key, 111), (N_POOL * SLOTS, 2, PAGE, KVH * HD), jnp.float32), -4.5, 4.5)
    return samples


def decode_tables(key):
    samples = jax.random.randint(jax.random.fold_in(key, 201), (N_POOL * DEC, DPMAX), 0, SLOTS, jnp.int32)
    fresh_ids = (permutations(jax.random.fold_in(key, 202), N_POOL, SPAGES) + SLOTS).reshape(N_POOL * DEC, FPR)
    spot_ids = permutations(jax.random.fold_in(key, 203), N_POOL * DEC, DMIN)[:, :FPR]
    front_part = samples[:, :DMIN]
    columns = jnp.arange(DMIN, dtype=jnp.int32)[None, :]
    for number in range(FPR):
        front_part = jnp.where(columns == spot_ids[:, number:number + 1], fresh_ids[:, number:number + 1], front_part)
    page_table = jnp.concatenate([front_part, samples[:, DMIN:]], 1)
    page_table = page_table.at[0, DMIN].set(0)
    lengths = jax.random.randint(jax.random.fold_in(key, 204), (N_POOL * DEC,), (DMIN + 1) * PAGE, DPMAX * PAGE + 1, jnp.int32)
    choose = jax.random.randint(jax.random.fold_in(key, 205), (), 0, N_POOL * DEC, jnp.int32)
    lengths = lengths.at[choose].set(DPMAX * PAGE)
    lengths = lengths.at[(choose + 1) % (N_POOL * DEC)].set((DMIN + 1) * PAGE)
    return (page_table, lengths)


def draw_suffix_q(key, part):
    samples = jnp.clip(jax.random.normal(jax.random.fold_in(key, 121), (N_POOL, SUF, QH, HD), jnp.float32), -4.5, 4.5)
    return jnp.clip(samples, -140.0, 140.0).reshape(N_POOL * SUF, QH * HD).astype(jnp.bfloat16)


def draw_fresh_kv(key, part):
    tokens = jnp.clip(fresh_tokens(key), -6.0, 6.0)
    paged = tokens.reshape(N_POOL, 2, SPAGES, PAGE, KVH * HD).transpose(0, 2, 1, 3, 4)
    return paged.reshape(N_POOL * SPAGES, 2, PAGE, KVH * HD).astype(jnp.bfloat16)


def draw_kv_pool(key, part):
    return jnp.clip(pool_values(key), -6.0, 6.0).astype(jnp.bfloat16)


def draw_dec_q(key, part):
    samples = jnp.clip(jax.random.normal(jax.random.fold_in(key, 131), (N_POOL * DEC, QH, HD), jnp.float32), -4.5, 4.5)
    return jnp.clip(samples, -140.0, 140.0).reshape(N_POOL * DEC, QH * HD).astype(jnp.bfloat16)


def draw_fetch_slots(key, part):
    samples = jax.random.randint(jax.random.fold_in(key, 301), (N_POOL, N_POOL * CAP), 0, SLOTS, jnp.int32)
    samples = samples.at[0, 0].set(SLOTS - 1)
    return samples.at[N_POOL - 1, 0].set(0)


def draw_prefix_pages(key, part):
    return permutations(jax.random.fold_in(key, 311), N_POOL, PMAX)


def draw_prefix_len(key, part):
    limit = PMAX * PAGE
    base_len = PAGE * (PMAX // 2)
    extra = jax.random.randint(jax.random.fold_in(key, 321), (N_POOL,), 0, limit // 2 + 1, jnp.int32)
    lengths = jnp.minimum(base_len + extra, limit)
    choose = jax.random.randint(jax.random.fold_in(key, 323), (), 0, N_POOL, jnp.int32)
    lengths = lengths.at[choose].set(limit)
    return lengths.at[(choose + 1) % N_POOL].set(PAGE)


def draw_suffix_route(key, part):
    return permutations(jax.random.fold_in(key, 331), N_POOL, SPAGES)


def draw_dec_pages(key, part):
    return decode_tables(key)[0]


def draw_dec_len(key, part):
    return decode_tables(key)[1]


def setup_inputs(seed: int = 0, part: int = 0) -> dict:
    keys = jax.random.split(jax.random.key(seed), 11)
    own_keys = jax.random.split(jax.random.fold_in(keys[10], part), 11)
    suffix_q = draw_suffix_q(jax.random.fold_in(jax.random.fold_in(keys[10], part), 71), part)
    fresh_kv = draw_fresh_kv(jax.random.fold_in(jax.random.fold_in(keys[10], part), 71), part)
    kv_pool = draw_kv_pool(jax.random.fold_in(jax.random.fold_in(keys[10], part), 71), part)
    dec_q = draw_dec_q(jax.random.fold_in(jax.random.fold_in(keys[10], part), 71), part)
    fetch_slots = draw_fetch_slots(jax.random.fold_in(jax.random.fold_in(keys[10], part), 71), part)
    prefix_pages = draw_prefix_pages(jax.random.fold_in(jax.random.fold_in(keys[10], part), 71), part)
    prefix_len = draw_prefix_len(jax.random.fold_in(jax.random.fold_in(keys[10], part), 71), part)
    suffix_route = draw_suffix_route(jax.random.fold_in(jax.random.fold_in(keys[10], part), 71), part)
    dec_pages = draw_dec_pages(jax.random.fold_in(jax.random.fold_in(keys[10], part), 71), part)
    dec_len = draw_dec_len(jax.random.fold_in(jax.random.fold_in(keys[10], part), 71), part)
    return {"suffix_q": suffix_q, "fresh_kv": fresh_kv, "kv_pool": kv_pool, "dec_q": dec_q, "fetch_slots": fetch_slots, "prefix_pages": prefix_pages, "prefix_len": prefix_len, "suffix_route": suffix_route, "dec_pages": dec_pages, "dec_len": dec_len}


def normalize(scores, visible):
    scores = jnp.where(visible, scores, -1e30)
    row_max = jnp.max(scores, axis=-1, keepdims=True)
    weights = jnp.exp(scores - row_max)
    return (weights / jnp.sum(weights, axis=-1, keepdims=True)).astype(jnp.bfloat16)


def softmax_apply(queries, key_rows, value_rows, visible):
    row_count = queries.shape[0]
    query_heads = queries.astype(jnp.float32).reshape(row_count, KVH, QH // KVH, HD)
    key_heads = key_rows.astype(jnp.float32).reshape(-1, KVH, HD)
    value_heads = value_rows.astype(jnp.float32).reshape(-1, KVH, HD)
    scores = jnp.einsum('rkgh,lkh->rkgl', query_heads, key_heads) * (HD ** -0.5)
    attention_weights = normalize(scores, visible[:, None, None, :])
    combined = jnp.einsum('rkgl,lkh->rkgh', attention_weights.astype(jnp.float32), value_heads)
    return combined.reshape(row_count, QH * HD).astype(jnp.bfloat16)


def reference(suffix_q, fresh_kv, kv_pool, dec_q, fetch_slots, prefix_pages, prefix_len, suffix_route, dec_pages, dec_len):
    row_width = KVH * HD
    pool_pages = kv_pool.reshape(N_POOL, SLOTS, 2, PAGE, row_width)
    fresh_pages = fresh_kv.reshape(N_POOL, SPAGES, 2, PAGE, row_width)
    prompt_queries = suffix_q.reshape(N_POOL, SUF, QH * HD)

    def prefill_one(requester):
        entries = prefix_pages[requester]
        sources = entries // CAP
        within = entries % CAP
        slot_ids = fetch_slots[sources, requester * CAP + within]
        page_set = pool_pages[sources, slot_ids]
        fresh_set = fresh_pages[requester]
        key_rows = jnp.concatenate([page_set[:, 0].reshape(-1, row_width), fresh_set[:, 0].reshape(-1, row_width)], 0)
        value_rows = jnp.concatenate([page_set[:, 1].reshape(-1, row_width), fresh_set[:, 1].reshape(-1, row_width)], 0)
        key_positions = jnp.arange(PMAX * PAGE + SUF, dtype=jnp.int32)[None, :]
        row_positions = jnp.arange(SUF, dtype=jnp.int32)[:, None]
        visible = jnp.where(key_positions < PMAX * PAGE, key_positions < prefix_len[requester], key_positions - PMAX * PAGE <= row_positions)
        return softmax_apply(prompt_queries[requester], key_rows, value_rows, visible)

    suffix_out = lax.map(prefill_one, jnp.arange(N_POOL, dtype=jnp.int32)).reshape(N_POOL * SUF, QH * HD)

    def decode_one(owner_id):
        fresh_ids = jnp.arange(SPAGES, dtype=jnp.int32)
        sources = fresh_ids // CAPS
        within = fresh_ids % CAPS
        chosen = suffix_route[sources, owner_id * CAPS + within]
        received = fresh_pages[sources, chosen]
        page_store = jnp.concatenate([pool_pages[owner_id], received], 0)
        page_table = lax.dynamic_slice_in_dim(dec_pages, owner_id * DEC, DEC, 0)
        lengths = lax.dynamic_slice_in_dim(dec_len, owner_id * DEC, DEC, 0)
        queries = lax.dynamic_slice_in_dim(dec_q, owner_id * DEC, DEC, 0)
        page_set = page_store[page_table]
        key_rows = page_set[:, :, 0].reshape(DEC, DPMAX * PAGE, row_width)
        value_rows = page_set[:, :, 1].reshape(DEC, DPMAX * PAGE, row_width)
        visible = jnp.arange(DPMAX * PAGE, dtype=jnp.int32)[None, :] < lengths[:, None]

        def single(query_row, key_part, value_part, visible_row):
            return softmax_apply(query_row[None, :], key_part, value_part, visible_row[None, :])[0]

        return jax.vmap(single)(queries, key_rows, value_rows, visible)

    decode_out = lax.map(decode_one, jnp.arange(N_POOL, dtype=jnp.int32)).reshape(N_POOL * DEC, QH * HD)
    return suffix_out, decode_out
```

```python
import functools

import jax
import jax.numpy as jnp
from jax import lax
from jax.experimental import pallas as pl
from jax.experimental.pallas import tpu as pltpu
from jax.sharding import PartitionSpec as P

GROUP = 8
HD = 128
LOG2E = 1.4426950408889634
CEXP = HD**-0.5 * LOG2E
NEG = -1e30
ROWS = 256


NT = (((1,), (1,)), ((), ()))


def cdiv(a, b):
    return -(-a // b)


def gather_pages(kv_pool, fresh_kv, slots, routes, dests):
    count, _, page, width = kv_pool.shape
    n = len(dests)
    cap, caps = slots.shape[1], routes.shape[1]
    each = cap + caps

    def body(slots_ref, routes_ref, pool_ref, fresh_ref, *rest):
        outs, buf, in_sem, out_sem = rest[:n], rest[n], rest[n + 1], rest[n + 2]
        for i in range(n):
            for c in range(cap):
                pltpu.make_async_copy(
                    pool_ref.at[slots_ref[i, c]], buf.at[i, :, c], in_sem.at[i]
                ).start()
            for c in range(caps):
                pltpu.make_async_copy(
                    fresh_ref.at[routes_ref[i, c]], buf.at[i, :, cap + c], in_sem.at[i]
                ).start()
        for i in range(n):
            pltpu.make_async_copy(outs[i], buf.at[i], in_sem.at[i]).wait()
            pltpu.make_async_copy(buf.at[i], outs[i], out_sem.at[i]).start()
        for i in range(n):
            pltpu.make_async_copy(buf.at[i], outs[i], out_sem.at[i]).wait()

    shape = (2, each, page, width)
    return pl.pallas_call(
        body,
        out_shape=[jax.ShapeDtypeStruct(shape, kv_pool.dtype)] * n,
        in_specs=[pl.BlockSpec(memory_space=pltpu.SMEM)] * 2 + [pl.BlockSpec(memory_space=pl.ANY)] * 2,
        out_specs=[pl.BlockSpec(memory_space=pl.ANY)] * n,
        scratch_shapes=[
            pltpu.VMEM((n, *shape), kv_pool.dtype),
            pltpu.SemaphoreType.DMA((n,)),
            pltpu.SemaphoreType.DMA((n,)),
        ],
        cost_estimate=pl.CostEstimate(
            flops=0, transcendentals=0, bytes_accessed=2 * n * each * 2 * page * width * 2
        ),
        name="gather_pages",
    )(slots, routes, kv_pool, fresh_kv)


def prefill_chunk(q, pieces, srcs, pages, plen, fresh, state, first, final, cap):
    tokens, qwidth = q.shape
    page, width = pieces[0].shape[2:]
    heads_kv = width // HD
    piece_keys = cap * page
    suffix_keys = tokens if first else 0
    prefix_keys = piece_keys * len(pieces)
    keys = suffix_keys + prefix_keys
    n = len(pieces)
    hp = 2
    rows = min(ROWS, tokens)

    def body(*refs):
        srcs_ref, plen_ref, pages_ref, q_ref, fresh_ref = refs[:5]
        piece_refs = refs[5 : 5 + n]
        refs = refs[5 + n :]
        if not first:
            acc_in, st_in = refs[:2]
            refs = refs[2:]
        if final:
            out_ref = refs[0]
            refs = refs[1:]
        else:
            acc_out, st_out = refs[:2]
            refs = refs[2:]
        vis_ref, k_ref, v_ref = refs
        g, hb = pl.program_id(0), pl.program_id(1)

        @pl.when((g == 0) & (hb == 0))
        def _():
            wanted = pages_ref[...]
            order = lax.broadcasted_iota(jnp.int32, (piece_keys, wanted.shape[1]), 1)
            token = lax.broadcasted_iota(jnp.int32, (piece_keys, 1), 0)
            for i in range(n):
                name = srcs_ref[i] * cap + token // page
                place = jnp.sum(jnp.where(wanted == name, order, 0), axis=1, keepdims=True)
                seen = place * page + token % page < plen_ref[0]
                vis_ref[i * piece_keys : (i + 1) * piece_keys, :] = jnp.broadcast_to(
                    jnp.where(seen, 1.0, 0.0), (piece_keys, HD)
                )

        @pl.when(hb == 0)
        def _():
            own_k = fresh_ref[:, 0].reshape(-1, HD)
            stand_in = own_k[0:1].astype(jnp.float32)
            if first:
                k_ref[0:suffix_keys, :] = own_k
                v_ref[0:suffix_keys, 0:HD] = fresh_ref[:, 1].reshape(-1, HD)
                v_ref[0:suffix_keys, HD:] = jnp.ones((suffix_keys, HD), jnp.bfloat16)
            for i in range(n):
                at = suffix_keys + i * piece_keys
                seen = vis_ref[i * piece_keys : (i + 1) * piece_keys, :]
                key = piece_refs[i][0].reshape(piece_keys, HD).astype(jnp.float32)
                val = piece_refs[i][1].reshape(piece_keys, HD).astype(jnp.float32)
                k_ref[at : at + piece_keys, :] = jnp.where(seen > 0, key, stand_in).astype(jnp.bfloat16)
                v_ref[at : at + piece_keys, 0:HD] = jnp.where(seen > 0, val, 0.0).astype(jnp.bfloat16)
                v_ref[at : at + piece_keys, HD:] = seen.astype(jnp.bfloat16)

        for h in range(hp):
            cols = slice(h * HD, (h + 1) * HD)
            for r in range(0, tokens, rows):
                rs = slice(r, r + rows)
                qb = q_ref[rs, cols]
                parts = []
                if first:
                    shown = r + rows
                    s = lax.dot_general(qb, k_ref[0:shown, :], NT, preferred_element_type=jnp.float32)
                    row = lax.broadcasted_iota(jnp.int32, (rows, rows), 0)
                    col = lax.broadcasted_iota(jnp.int32, (rows, rows), 1)
                    diag = jnp.where(col <= row, s[:, r:shown], NEG)
                    parts.append((jnp.concatenate([s[:, 0:r], diag], 1) if r else diag, slice(0, shown)))
                parts.append(
                    (
                        lax.dot_general(
                            qb, k_ref[suffix_keys:keys, :], NT, preferred_element_type=jnp.float32
                        ),
                        slice(suffix_keys, keys),
                    )
                )
                m = functools.reduce(
                    jnp.maximum, [jnp.max(s, axis=1, keepdims=True) for s, _ in parts]
                )
                if not first:
                    m_old = st_in[rs, h * HD : h * HD + 1]
                    l_old = st_in[rs, h * HD + HD // 2 : h * HD + HD // 2 + 1]
                    m = jnp.maximum(m, m_old)
                both = 0.0
                for s, where in parts:
                    p = jnp.exp2((s - m) * CEXP).astype(jnp.bfloat16)
                    both += jnp.dot(p, v_ref[where, :], preferred_element_type=jnp.float32)
                acc, total = both[:, 0:HD], both[:, HD:]
                if not first:
                    alpha = jnp.exp2((m_old - m) * CEXP)
                    acc += acc_in[rs, cols] * alpha
                    total += l_old * alpha
                if final:
                    out_ref[rs, cols] = (acc / total).astype(out_ref.dtype)
                else:
                    acc_out[rs, cols] = acc
                    lane = lax.broadcasted_iota(jnp.int32, (rows, HD), 1)
                    st_out[rs, cols] = jnp.where(lane < HD // 2, jnp.broadcast_to(m, (rows, HD)), total)

    blocks = GROUP // hp
    col_block = pl.BlockSpec((tokens, hp * HD), lambda g, hb: (0, g * blocks + hb))
    kv_block = lambda k: pl.BlockSpec((2, k, page, HD), lambda g, hb: (0, 0, 0, g))
    fresh_pages = fresh.shape[0] if first else 1
    in_specs = [
        pl.BlockSpec(memory_space=pltpu.SMEM),
        pl.BlockSpec(memory_space=pltpu.SMEM),
        pl.BlockSpec(pages.shape, lambda g, hb: (0, 0)),
        col_block,
        pl.BlockSpec((fresh_pages, 2, page, HD), lambda g, hb: (0, 0, 0, g)),
    ] + [kv_block(cap)] * n
    operands = [srcs, plen, pages, q, fresh, *pieces]
    aliases = {}
    wide = jax.ShapeDtypeStruct((tokens, qwidth), jnp.float32)
    if not first:
        in_specs += [col_block, col_block]
        operands += list(state)
        if not final:
            aliases = {5 + n: 0, 6 + n: 1}
    if final:
        out_shape, out_specs = jax.ShapeDtypeStruct(q.shape, jnp.bfloat16), col_block
    else:
        out_shape, out_specs = [wide, wide], [col_block, col_block]
    work = tokens * keys * (qwidth // HD)
    return pl.pallas_call(
        body,
        grid=(heads_kv, blocks),
        out_shape=out_shape,
        in_specs=in_specs,
        out_specs=out_specs,
        scratch_shapes=[
            pltpu.VMEM((prefix_keys, HD), jnp.float32),
            pltpu.VMEM((keys, HD), jnp.bfloat16),
            pltpu.VMEM((keys, 2 * HD), jnp.bfloat16),
        ],
        input_output_aliases=aliases,
        cost_estimate=pl.CostEstimate(
            flops=4 * HD * work, transcendentals=work, bytes_accessed=tokens * qwidth * 18
        ),
        name="prefill_first" if first else "prefill_last" if final else "prefill_more",
    )(*operands)


def decode_scores(q, key, full, part, rest, spread):
    requests = full.shape[0]
    times = jnp.dot(full, spread, preferred_element_type=jnp.float32)
    edge = jnp.dot(part, spread, preferred_element_type=jnp.float32)
    token = lax.broadcasted_iota(jnp.int32, times.shape, 1) % 8
    times = times + jnp.where(token < rest, edge, 0.0)
    return times


def decode_fold(q_ref, g, key, val, times, m_old, l_old, acc_old):
    requests = times.shape[0]
    q = jnp.concatenate(
        [q_ref[:, (g * GROUP + h) * HD : (g * GROUP + h + 1) * HD] for h in range(GROUP)], 0
    )
    s = lax.dot_general(q, key, NT, preferred_element_type=jnp.float32)
    keys = s.shape[1]
    s = s.reshape(GROUP, requests, keys)
    s = jnp.where((times > 0)[None], s, NEG).reshape(GROUP * requests, keys)
    m = jnp.maximum(jnp.max(s, axis=1, keepdims=True), m_old)
    p = jnp.exp2((s - m) * CEXP).reshape(GROUP, requests, keys) * times[None]
    p = p.reshape(GROUP * requests, keys)
    total = jnp.sum(p, axis=1, keepdims=True)
    new = jnp.dot(p.astype(jnp.bfloat16), val, preferred_element_type=jnp.float32)
    alpha = jnp.exp2((m_old - m) * CEXP)
    return m, l_old * alpha + total, acc_old * alpha + new


def spread_matrix(pages, page):
    key = lax.broadcasted_iota(jnp.int32, (pages, pages * page), 1) // page
    row = lax.broadcasted_iota(jnp.int32, (pages, pages * page), 0)
    return jnp.where(key == row, 1.0, 0.0).astype(jnp.bfloat16)


def token_counts(full, part, rest, page):
    spread = spread_matrix(full.shape[1], page)
    times = jnp.dot(full, spread, preferred_element_type=jnp.float32)
    edge = jnp.dot(part, spread, preferred_element_type=jnp.float32)
    token = lax.broadcasted_iota(jnp.int32, times.shape, 1) % page
    return times + jnp.where(token < rest, edge, 0.0)


def decode_pool(dec_q, kv_pool, full, part, rest):
    slots, _, page, width = kv_pool.shape
    requests = dec_q.shape[0]
    heads_kv = width // HD
    block = 128 if slots % 128 == 0 else slots
    steps = slots // block

    def body(q_ref, kv_ref, full_ref, part_ref, rest_ref, acc_ref, m_ref, l_ref):
        @pl.when(pl.program_id(0) == 0)
        def _():
            acc_ref[...] = jnp.zeros_like(acc_ref)
            m_ref[...] = jnp.full_like(m_ref, NEG)
            l_ref[...] = jnp.zeros_like(l_ref)

        times = token_counts(full_ref[...], part_ref[...], rest_ref[...], page)
        for g in range(heads_kv):
            cols = slice(g * HD, (g + 1) * HD)
            key = kv_ref[:, 0, :, cols].reshape(block * page, HD)
            val = kv_ref[:, 1, :, cols].reshape(block * page, HD)
            m, l, acc = decode_fold(
                q_ref, g, key, val, times, m_ref[g, :, 0:1], l_ref[g, :, 0:1], acc_ref[g]
            )
            m_ref[g] = jnp.broadcast_to(m, m_ref.shape[1:])
            l_ref[g] = jnp.broadcast_to(l, l_ref.shape[1:])
            acc_ref[g] = acc

    shape = (heads_kv, GROUP * requests, HD)
    whole = pl.BlockSpec(shape, lambda i: (0, 0, 0))
    return pl.pallas_call(
        body,
        grid=(steps,),
        out_shape=[jax.ShapeDtypeStruct(shape, jnp.float32)] * 3,
        in_specs=[
            pl.BlockSpec(dec_q.shape, lambda i: (0, 0)),
            pl.BlockSpec((block, 2, page, width), lambda i: (i, 0, 0, 0)),
            pl.BlockSpec((requests, block), lambda i: (0, i)),
            pl.BlockSpec((requests, block), lambda i: (0, i)),
            pl.BlockSpec(rest.shape, lambda i: (0, 0)),
        ],
        out_specs=[whole] * 3,
        cost_estimate=pl.CostEstimate(
            flops=4 * HD * heads_kv * GROUP * requests * slots * page,
            transcendentals=heads_kv * GROUP * requests * slots * page,
            bytes_accessed=slots * 2 * page * width * 2,
        ),
        name="decode_pool",
    )(dec_q, kv_pool, full, part, rest)


def decode_fresh(dec_q, pieces, state, full, part, rest, caps):
    page, width = pieces[0].shape[2:]
    each = pieces[0].shape[1]
    requests = dec_q.shape[0]
    heads_kv = width // HD
    n = len(pieces)

    def body(q_ref, *refs):
        piece_refs = refs[:n]
        acc_ref, m_ref, l_ref, full_ref, part_ref, rest_ref, out_ref = refs[n:]
        times = token_counts(full_ref[...], part_ref[...], rest_ref[...], page)
        for g in range(heads_kv):
            cols = slice(g * HD, (g + 1) * HD)
            key = jnp.concatenate([p[0, :, :, cols].reshape(caps * page, HD) for p in piece_refs], 0)
            val = jnp.concatenate([p[1, :, :, cols].reshape(caps * page, HD) for p in piece_refs], 0)
            m, l, acc = decode_fold(
                q_ref, g, key, val, times, m_ref[g, :, 0:1], l_ref[g, :, 0:1], acc_ref[g]
            )
            out = (acc / l).astype(out_ref.dtype)
            for h in range(GROUP):
                at = (g * GROUP + h) * HD
                out_ref[:, at : at + HD] = out[h * requests : (h + 1) * requests]

    shape = (heads_kv, GROUP * requests, HD)
    whole = pl.BlockSpec(shape, lambda i: (0, 0, 0))
    small = lambda a: pl.BlockSpec(a.shape, lambda i: (0, 0))
    return pl.pallas_call(
        body,
        grid=(1,),
        out_shape=jax.ShapeDtypeStruct(dec_q.shape, jnp.bfloat16),
        in_specs=[small(dec_q)]
        + [pl.BlockSpec((2, caps, page, width), lambda i: (0, each // caps - 1, 0, 0))] * n
        + [whole] * 3
        + [small(full), small(part), small(rest)],
        out_specs=pl.BlockSpec(dec_q.shape, lambda i: (0, 0)),
        cost_estimate=pl.CostEstimate(
            flops=4 * HD * heads_kv * GROUP * requests * n * caps * page,
            transcendentals=heads_kv * GROUP * requests * n * caps * page,
            bytes_accessed=n * caps * 2 * page * width * 2,
        ),
        name="decode_fresh",
    )(dec_q, *pieces, *state, full, part, rest)


def shards(
    size,
    suffix_q,
    fresh_kv,
    kv_pool,
    dec_q,
    fetch_slots,
    prefix_pages,
    prefix_len,
    suffix_route,
    dec_pages,
    dec_len,
):
    page = kv_pool.shape[2]
    slots = kv_pool.shape[0]
    cap = fetch_slots.shape[1] // size
    caps = suffix_route.shape[1] // size
    me = lax.axis_index("pool")
    power = size & (size - 1) == 0
    steps = list(range(size))
    sends = [k for k in range(size - 1, 0, -1)]

    def partner(i, k):
        return i ^ k if power else (i + k) % size

    def source(k):
        return me ^ k if power else (me - k) % size

    def target(k):
        return me ^ k if power else (me + k) % size

    by_dest = fetch_slots[0].reshape(size, cap)
    routes = suffix_route[0].reshape(size, caps)
    half = sends[: len(sends) // 2 + 1]
    rest_sends = sends[len(half) :] + [0]

    def gather(ks):
        dests = jnp.stack([target(k) for k in ks])
        return dict(
            zip(ks, gather_pages(kv_pool, fresh_kv, by_dest[dests], routes[dests], ks), strict=True)
        )

    outgoing = gather(half) | gather(rest_sends)
    arrived = {0: outgoing[0]}
    for k in sends:
        arrived[k] = lax.ppermute(outgoing[k], "pool", [(i, partner(i, k)) for i in range(size)])

    def chunk(ks, state, first, final):
        srcs = jnp.stack([source(k) for k in ks]).astype(jnp.int32)
        return prefill_chunk(
            suffix_q,
            [arrived[k] for k in ks],
            srcs,
            prefix_pages,
            prefix_len,
            fresh_kv,
            state,
            first,
            final,
            cap,
        )

    near = cdiv(size, 8)
    order = steps
    groups = [order[:near]]
    at = near
    per = cdiv(size, 4)
    while at < size:
        groups.append(order[at : at + per])
        at += per

    context = dec_pages.shape[1]
    position = jnp.arange(context, dtype=jnp.int32)[None, :]
    whole_pages = (position + 1) * page <= dec_len[:, None]
    edge_page = position == dec_len[:, None] // page
    rest = (dec_len % page)[:, None]

    def counts(names):
        same = dec_pages[:, :, None] == names[None, None, :]
        full = jnp.sum((same & whole_pages[:, :, None]).astype(jnp.float32), 1).astype(jnp.bfloat16)
        part = jnp.sum((same & edge_page[:, :, None]).astype(jnp.float32), 1).astype(jnp.bfloat16)
        return full, part

    pool_names = jnp.arange(slots, dtype=jnp.int32)
    fresh_srcs = jnp.stack([source(k) for k in steps]).astype(jnp.int32)
    fresh_names = (
        slots + fresh_srcs[:, None] * caps + jnp.arange(caps, dtype=jnp.int32)[None, :]
    ).reshape(-1)

    state = chunk(groups[0], None, True, len(groups) == 1)
    dec_state = decode_pool(dec_q, kv_pool, *counts(pool_names), rest)
    for i, ks in enumerate(groups[1:], 1):
        state = chunk(ks, state, False, i == len(groups) - 1)
    decode_out = decode_fresh(
        dec_q, [arrived[k] for k in steps], dec_state, *counts(fresh_names), rest, caps
    )
    return (state, decode_out)


def solution(mesh):
    return jax.shard_map(
        functools.partial(shards, mesh.shape["pool"]),
        mesh=mesh,
        in_specs=(
            P(("groups", "pool"), "tp"),
            P(("groups", "pool"), None, None, "tp"),
            P(("groups", "pool"), None, None, "tp"),
            P(("groups", "pool"), "tp"),
            P(("groups", "pool"), None),
            P(("groups", "pool"), None),
            P(("groups", "pool")),
            P(("groups", "pool"), None),
            P(("groups", "pool"), None),
            P(("groups", "pool")),
        ),
        out_specs=(P(("groups", "pool"), "tp"), P(("groups", "pool"), "tp")),
        check_vma=False,
    )
```

```python
import functools

import jax
import jax.numpy as jnp
from jax import lax
from jax.experimental import pallas as pl
from jax.experimental.pallas import tpu as pltpu
from jax.sharding import PartitionSpec as P

GROUP = 8
HD = 128
LOG2E = 1.4426950408889634
CEXP = HD**-0.5 * LOG2E
NEG = -1e30
HUGE = 2.0**90
VMEM_LIMIT = 24 << 20


HP_FIRST = 4

NT = (((1,), (1,)), ((), ()))
VM = pl.BlockSpec(memory_space=pltpu.VMEM)
SM = pl.BlockSpec(memory_space=pltpu.SMEM)
ANY = pl.BlockSpec(memory_space=pl.ANY)
PARAMS = pltpu.CompilerParams(vmem_limit_bytes=VMEM_LIMIT)


def head_at(i):
    return pl.ds(pl.multiple_of(i * HD, HD), HD)


def partner(i, k, size):
    return i ^ k if size & (size - 1) == 0 else lax.rem(i + k, size)


def source(i, k, size):
    return i ^ k if size & (size - 1) == 0 else lax.rem(i - k + size, size)


def gather_pages(kv_pool, fresh_kv, fetch_slots, suffix_route, ks, size):
    _, _, page, width = kv_pool.shape
    n = len(ks)
    cap, caps = fetch_slots.shape[1] // size, suffix_route.shape[1] // size
    each = cap + caps

    def body(slots_ref, routes_ref, pool_ref, fresh_ref, *rest):
        outs, buf, in_sem, out_sem = rest[:n], rest[n], rest[n + 1], rest[n + 2]
        me = lax.axis_index("pool")
        for i, k in enumerate(ks):
            dest = partner(me, k, size)
            for c in range(cap):
                pltpu.make_async_copy(
                    pool_ref.at[slots_ref[0, dest * cap + c]], buf.at[i, :, c], in_sem.at[i]
                ).start()
            for c in range(caps):
                pltpu.make_async_copy(
                    fresh_ref.at[routes_ref[0, dest * caps + c]], buf.at[i, :, cap + c], in_sem.at[i]
                ).start()
        for i in range(n):
            pltpu.make_async_copy(outs[i], buf.at[i], in_sem.at[i]).wait()
            pltpu.make_async_copy(buf.at[i], outs[i], out_sem.at[i]).start()
        for i in range(n):
            pltpu.make_async_copy(buf.at[i], outs[i], out_sem.at[i]).wait()

    shape = (2, each, page, width)
    return pl.pallas_call(
        body,
        out_shape=[jax.ShapeDtypeStruct(shape, kv_pool.dtype)] * n,
        in_specs=[SM, SM, ANY, ANY],
        out_specs=[ANY] * n,
        scratch_shapes=[
            pltpu.VMEM((n, *shape), kv_pool.dtype),
            pltpu.SemaphoreType.DMA((n,)),
            pltpu.SemaphoreType.DMA((n,)),
        ],
        compiler_params=PARAMS,
        cost_estimate=pl.CostEstimate(
            flops=0, transcendentals=0, bytes_accessed=2 * n * each * 2 * page * width * 2
        ),
        name="gather_pages",
    )(fetch_slots, suffix_route, kv_pool, fresh_kv)


def mark_visible(vis_ref, at, k, cap, page, pages_ref, plen_ref, size):
    wanted = pages_ref[...]
    keys = cap * page
    order = lax.broadcasted_iota(jnp.int32, (keys, wanted.shape[1]), 1)
    token = lax.broadcasted_iota(jnp.int32, (keys, 1), 0)
    name = source(lax.axis_index("pool"), k, size) * cap + token // page
    place = jnp.sum(jnp.where(wanted == name, order, 0), axis=1, keepdims=True)
    seen = place * page + token % page < plen_ref[0]
    vis_ref[at : at + keys, :] = jnp.broadcast_to(jnp.where(seen, 1.0, 0.0), (keys, HD))


def place_keys(k_ref, v_ref, vis_ref, vis_at, at, g, piece, stand_in, cap, page):
    keys = cap * page
    rows = slice(at, at + keys)
    seen = vis_ref[vis_at : vis_at + keys, :] > 0
    key = piece[0, 0:cap, :, head_at(g)].reshape(keys, HD).astype(jnp.float32)
    val = piece[1, 0:cap, :, head_at(g)].reshape(keys, HD).astype(jnp.float32)
    k_ref[rows, 0:HD] = jnp.where(seen, key, stand_in).astype(jnp.bfloat16)
    v_ref[rows, 0:HD] = jnp.where(seen, val, 0.0).astype(jnp.bfloat16)


def prefill_first(q, fresh):
    tokens, qwidth = q.shape
    page, width = fresh.shape[2:]
    rows = min(256, tokens)

    def body(q_ref, f_ref, m_ref, acc_ref, l_ref, k_ref, v_ref):
        v_ref[:, HD:] = jnp.ones((tokens, HD), jnp.bfloat16)
        lane = lax.broadcasted_iota(jnp.int32, (rows, HD), 1)
        row = lax.broadcasted_iota(jnp.int32, (rows, rows), 0)
        col = lax.broadcasted_iota(jnp.int32, (rows, rows), 1)

        def group(g, carry):
            k_ref[...] = f_ref[:, 0, :, head_at(g)].reshape(tokens, HD)
            v_ref[:, 0:HD] = f_ref[:, 1, :, head_at(g)].reshape(tokens, HD)

            def heads(b, carry):
                for h in range(HP_FIRST):
                    cols = head_at(g * GROUP + b * HP_FIRST + h)
                    for r in range(0, tokens, rows):
                        rs = slice(r, r + rows)
                        s = lax.dot_general(
                            q_ref[rs, cols], k_ref[0 : r + rows, :], NT, preferred_element_type=jnp.float32
                        )
                        diag = jnp.where(col <= row, s[:, r:], NEG)
                        s = jnp.concatenate([s[:, :r], diag], 1) if r else diag
                        m = jnp.max(s, axis=1, keepdims=True).astype(jnp.bfloat16).astype(jnp.float32)
                        p = jnp.exp2((s - m) * CEXP).astype(jnp.bfloat16)
                        new = jnp.dot(p, v_ref[0 : r + rows, :], preferred_element_type=jnp.float32)
                        acc_ref[rs, cols] = new[:, :HD]
                        l_ref[rs, cols] = new[:, HD:]
                        m_ref[rs, cols] = jnp.where(lane == 0, m, 0.0).astype(jnp.bfloat16)
                return carry

            return lax.fori_loop(0, GROUP // HP_FIRST, heads, carry)

        lax.fori_loop(0, width // HD, group, 0)

    wide = pltpu.VMEM((tokens, qwidth), jnp.float32)
    work = tokens * tokens * (qwidth // HD) // 2
    return pl.pallas_call(
        body,
        out_shape=[pltpu.VMEM((tokens, qwidth), jnp.bfloat16), wide, wide],
        in_specs=[VM, VM],
        out_specs=[VM] * 3,
        scratch_shapes=[
            pltpu.VMEM((tokens, HD), jnp.bfloat16),
            pltpu.VMEM((tokens, 2 * HD), jnp.bfloat16),
        ],
        compiler_params=PARAMS,
        cost_estimate=pl.CostEstimate(flops=8 * HD * work, transcendentals=work, bytes_accessed=8 * work // HD),
        name="prefill_first",
    )(q, fresh)


def prefill_more(q, fresh, pieces, ks, pages, plen, state, cap, size, final):
    tokens, qwidth = q.shape
    page, width = fresh.shape[2:]
    n = len(pieces)
    keys = n * cap * page

    def body(*refs):
        plen_ref, pages_ref, q_ref, f_ref = refs[:4]
        piece_refs = refs[4 : 4 + n]
        m_ref, acc_in, l_in = refs[4 + n : 7 + n]
        if final:
            out_hbm, bad_ref, out_ref, sem, vis_ref, k_ref, v_ref = refs[7 + n :]
        else:
            acc_ref, l_ref, vis_ref, k_ref, v_ref = refs[7 + n :]
        for i, k in enumerate(ks):
            mark_visible(vis_ref, i * cap * page, k, cap, page, pages_ref, plen_ref, size)
        lane = lax.broadcasted_iota(jnp.int32, (keys, HD), 1)
        k_ref[:, HD:] = jnp.where(lane == 0, -1.0, 0.0).astype(jnp.bfloat16)
        v_ref[:, HD:] = vis_ref[...].astype(jnp.bfloat16)

        def out_copy(g):
            cols = pl.ds(pl.multiple_of(g * GROUP * HD, GROUP * HD), GROUP * HD)
            return pltpu.make_async_copy(out_ref.at[:, cols], out_hbm.at[:, cols], sem)

        def group(g, carry):
            stand_in = f_ref[0, 0, :, head_at(g)][0:1].astype(jnp.float32)
            for i in range(n):
                at = i * cap * page
                place_keys(k_ref, v_ref, vis_ref, at, at, g, piece_refs[i], stand_in, cap, page)
            for h in range(GROUP):
                cols = head_at(g * GROUP + h)
                lhs = jnp.concatenate([q_ref[:, cols], m_ref[:, cols]], 1)
                s = lax.dot_general(lhs, k_ref[...], NT, preferred_element_type=jnp.float32)
                p = jnp.exp2(s * CEXP).astype(jnp.bfloat16)
                new = jnp.dot(p, v_ref[...], preferred_element_type=jnp.float32)
                acc = acc_in[:, cols] + new[:, :HD]
                total = l_in[:, cols] + new[:, HD:]
                if final:
                    out_ref[:, cols] = (acc / total).astype(out_ref.dtype)
                    carry += jnp.sum(total.reshape(-1, 8, HD), axis=0)
                else:
                    acc_ref[:, cols] = acc
                    l_ref[:, cols] = total
            if final:
                out_copy(g).start()
            return carry

        sums = lax.fori_loop(0, width // HD, group, jnp.zeros((8, HD), jnp.float32) if final else 0)
        if final:
            bad_ref[0] = jnp.where(jnp.sum(sums) <= HUGE, 0, 1).astype(jnp.int32)
            lax.fori_loop(0, width // HD, lambda g, c: (out_copy(g).wait(), c)[1], 0)

    work = tokens * keys * (qwidth // HD)
    wide = pltpu.VMEM((tokens, qwidth), jnp.float32)
    scratch = [
        pltpu.VMEM((keys, HD), jnp.float32),
        pltpu.VMEM((keys, 2 * HD), jnp.bfloat16),
        pltpu.VMEM((keys, 2 * HD), jnp.bfloat16),
    ]
    if final:
        out_shape = [jax.ShapeDtypeStruct(q.shape, q.dtype), jax.ShapeDtypeStruct((1,), jnp.int32)]
        out_specs = [ANY, SM]
        scratch = [pltpu.VMEM(q.shape, q.dtype), pltpu.SemaphoreType.DMA] + scratch
    else:
        out_shape, out_specs = [wide, wide], [VM, VM]
    return pl.pallas_call(
        body,
        out_shape=out_shape,
        in_specs=[SM, VM, VM, VM] + [VM] * n + [VM] * 3,
        out_specs=out_specs,
        input_output_aliases={} if final else {5 + n: 0, 6 + n: 1},
        scratch_shapes=scratch,
        compiler_params=PARAMS,
        cost_estimate=pl.CostEstimate(
            flops=8 * HD * work, transcendentals=work, bytes_accessed=8 * work // HD
        ),
        name="prefill_last" if final else "prefill_more",
    )(plen, pages, q, fresh, *pieces, *state)


def token_counts(full, part, rest, page):
    pages = full.shape[1]
    key = lax.broadcasted_iota(jnp.int32, (pages, pages * page), 1) // page
    row = lax.broadcasted_iota(jnp.int32, (pages, pages * page), 0)
    spread = jnp.where(key == row, 1.0, 0.0).astype(jnp.bfloat16)
    times = jnp.dot(full, spread, preferred_element_type=jnp.float32)
    edge = jnp.dot(part, spread, preferred_element_type=jnp.float32)
    token = lax.broadcasted_iota(jnp.int32, times.shape, 1) % page
    return times + jnp.where(token < rest, edge, 0.0)


def decode_fold(q_ref, g, key, val, times, m_old, l_old, acc_old):
    requests = times.shape[0]
    q = jnp.concatenate(
        [q_ref[:, (g * GROUP + h) * HD : (g * GROUP + h + 1) * HD] for h in range(GROUP)], 0
    )
    s = lax.dot_general(q, key, NT, preferred_element_type=jnp.float32)
    keys = s.shape[1]
    s = s.reshape(GROUP, requests, keys)
    s = jnp.where((times > 0)[None], s, NEG).reshape(GROUP * requests, keys)
    m = jnp.maximum(jnp.max(s, axis=1, keepdims=True), m_old)
    p = jnp.exp2((s - m) * CEXP).reshape(GROUP, requests, keys) * times[None]
    p = p.reshape(GROUP * requests, keys)
    total = jnp.sum(p, axis=1, keepdims=True)
    new = jnp.dot(p.astype(jnp.bfloat16), val, preferred_element_type=jnp.float32)
    alpha = jnp.exp2((m_old - m) * CEXP)
    return m, l_old * alpha + total, acc_old * alpha + new


def decode_pool(dec_q, kv_pool, full, part, rest):
    slots, _, page, width = kv_pool.shape
    requests = dec_q.shape[0]
    heads_kv = width // HD
    block = 128 if slots % 128 == 0 else slots
    steps = slots // block

    def body(q_ref, kv_ref, full_ref, part_ref, rest_ref, acc_ref, m_ref, l_ref):
        @pl.when(pl.program_id(0) == 0)
        def _():
            acc_ref[...] = jnp.zeros_like(acc_ref)
            m_ref[...] = jnp.full_like(m_ref, NEG)
            l_ref[...] = jnp.zeros_like(l_ref)

        times = token_counts(full_ref[...], part_ref[...], rest_ref[...], page)
        for g in range(heads_kv):
            cols = slice(g * HD, (g + 1) * HD)
            key = kv_ref[:, 0, :, cols].reshape(block * page, HD)
            val = kv_ref[:, 1, :, cols].reshape(block * page, HD)
            m, l, acc = decode_fold(
                q_ref, g, key, val, times, m_ref[g, :, 0:1], l_ref[g, :, 0:1], acc_ref[g]
            )
            m_ref[g] = jnp.broadcast_to(m, m_ref.shape[1:])
            l_ref[g] = jnp.broadcast_to(l, l_ref.shape[1:])
            acc_ref[g] = acc

    shape = (heads_kv, GROUP * requests, HD)
    whole = pl.BlockSpec(shape, lambda i: (0, 0, 0))
    return pl.pallas_call(
        body,
        grid=(steps,),
        out_shape=[jax.ShapeDtypeStruct(shape, jnp.float32)] * 3,
        in_specs=[
            pl.BlockSpec(dec_q.shape, lambda i: (0, 0)),
            pl.BlockSpec((block, 2, page, width), lambda i: (i, 0, 0, 0)),
            pl.BlockSpec((requests, block), lambda i: (0, i)),
            pl.BlockSpec((requests, block), lambda i: (0, i)),
            pl.BlockSpec(rest.shape, lambda i: (0, 0)),
        ],
        out_specs=[whole] * 3,
        compiler_params=PARAMS,
        cost_estimate=pl.CostEstimate(
            flops=4 * HD * heads_kv * GROUP * requests * slots * page,
            transcendentals=heads_kv * GROUP * requests * slots * page,
            bytes_accessed=slots * 2 * page * width * 2,
        ),
        name="decode_pool",
    )(dec_q, kv_pool, full, part, rest)


def finish(dec_q, state, full, part, rest, bad, q, fresh, pages, plen, out, pieces, ks, cap, size):
    page, width = pieces[0].shape[2:]
    caps = pieces[0].shape[1] - cap
    requests = dec_q.shape[0]
    heads_kv = width // HD
    tokens = q.shape[0]
    n = len(pieces)
    keys = cap * page
    rows = min(128, tokens)

    def body(*refs):
        q_ref, acc_ref, m_ref, l_ref, full_ref, part_ref, rest_ref = refs[:7]
        bad_ref, pq_ref, f_ref, pages_ref, plen_ref, _ = refs[7:13]
        piece_refs = refs[13 : 13 + n]
        out_ref, suffix_out, vis_ref, k_ref, v_ref, block_ref = refs[13 + n :]
        times = token_counts(full_ref[...], part_ref[...], rest_ref[...], page)
        for g in range(heads_kv):
            cols = slice(g * HD, (g + 1) * HD)
            key = jnp.concatenate([p[0, cap:, :, cols].reshape(caps * page, HD) for p in piece_refs], 0)
            val = jnp.concatenate([p[1, cap:, :, cols].reshape(caps * page, HD) for p in piece_refs], 0)
            m, l, acc = decode_fold(
                q_ref, g, key, val, times, m_ref[g, :, 0:1], l_ref[g, :, 0:1], acc_ref[g]
            )
            done = (acc / l).astype(out_ref.dtype)
            for h in range(GROUP):
                at = (g * GROUP + h) * HD
                out_ref[:, at : at + HD] = done[h * requests : (h + 1) * requests]

        @pl.when(bad_ref[0] > 0)
        def _():
            for i, k in enumerate(ks):
                mark_visible(vis_ref, i * keys, k, cap, page, pages_ref, plen_ref, size)
            v_ref[0:tokens, HD:] = jnp.ones((tokens, HD), jnp.bfloat16)
            v_ref[tokens:, HD:] = vis_ref[...].astype(jnp.bfloat16)
            col = lax.broadcasted_iota(jnp.int32, (rows, tokens), 1)
            row = lax.broadcasted_iota(jnp.int32, (rows, tokens), 0)

            def group(g, carry):
                k_ref[0:tokens, :] = f_ref[:, 0, :, head_at(g)].reshape(tokens, HD)
                v_ref[0:tokens, 0:HD] = f_ref[:, 1, :, head_at(g)].reshape(tokens, HD)
                stand_in = f_ref[0, 0, :, head_at(g)][0:1].astype(jnp.float32)
                for i in range(n):
                    place_keys(
                        k_ref, v_ref, vis_ref, i * keys, tokens + i * keys, g, piece_refs[i], stand_in, cap, page
                    )

                def block(b, carry):
                    r = pl.multiple_of((b % (tokens // rows)) * rows, rows)
                    cols = head_at(g * GROUP + b // (tokens // rows))
                    qb = pq_ref[pl.ds(r, rows), cols]
                    s = lax.dot_general(qb, k_ref[...], NT, preferred_element_type=jnp.float32)
                    own = jnp.where(col <= row + r, s[:, :tokens], NEG)
                    s = jnp.concatenate([own, s[:, tokens:]], 1)
                    m = jnp.max(s, axis=1, keepdims=True)
                    p = jnp.exp2((s - m) * CEXP).astype(jnp.bfloat16)
                    new = jnp.dot(p, v_ref[...], preferred_element_type=jnp.float32)
                    block_ref[...] = (new[:, :HD] / new[:, HD:]).astype(block_ref.dtype)
                    pltpu.sync_copy(block_ref, suffix_out.at[pl.ds(r, rows), cols])
                    return carry

                return lax.fori_loop(0, GROUP * (tokens // rows), block, carry)

            lax.fori_loop(0, heads_kv, group, 0)

    return pl.pallas_call(
        body,
        out_shape=[
            jax.ShapeDtypeStruct(dec_q.shape, dec_q.dtype),
            jax.ShapeDtypeStruct(out.shape, out.dtype),
        ],
        in_specs=[VM] * 7 + [SM, VM, VM, VM, SM, ANY] + [VM] * n,
        out_specs=[VM, ANY],
        input_output_aliases={12: 1},
        scratch_shapes=[
            pltpu.VMEM((n * keys, HD), jnp.float32),
            pltpu.VMEM((tokens + n * keys, HD), jnp.bfloat16),
            pltpu.VMEM((tokens + n * keys, 2 * HD), jnp.bfloat16),
            pltpu.VMEM((rows, HD), q.dtype),
        ],
        compiler_params=PARAMS,
        cost_estimate=pl.CostEstimate(
            flops=4 * HD * heads_kv * GROUP * requests * n * caps * page,
            transcendentals=heads_kv * GROUP * requests * n * caps * page,
            bytes_accessed=n * caps * 2 * page * width * 2,
        ),
        name="finish",
    )(dec_q, *state, full, part, rest, bad, q, fresh, pages, plen, out, *pieces)


def send_order(size):
    if size == 16:
        return [12, 1, 2, 3, 4, 8, 5, 13, 6, 9, 7, 14, 10, 15, 11]
    return list(range(1, size))


def shards(
    size,
    suffix_q,
    fresh_kv,
    kv_pool,
    dec_q,
    fetch_slots,
    prefix_pages,
    prefix_len,
    suffix_route,
    dec_pages,
    dec_len,
):
    page = kv_pool.shape[2]
    slots = kv_pool.shape[0]
    cap = fetch_slots.shape[1] // size
    caps = suffix_route.shape[1] // size
    sends = send_order(size)
    batches = [sends[: size // 2], sends[size // 2 :] + [0]]
    outgoing = {}
    for ks in batches:
        outs = gather_pages(kv_pool, fresh_kv, fetch_slots, suffix_route, ks, size)
        outgoing |= dict(zip(ks, outs, strict=True))
    arrived = {0: outgoing[0]}
    for k in sends:
        pairs = [(i, i ^ k if size & (size - 1) == 0 else (i + k) % size) for i in range(size)]
        arrived[k] = lax.ppermute(outgoing[k], "pool", pairs)

    context = dec_pages.shape[1]
    position = jnp.arange(context, dtype=jnp.int32)[None, :]
    whole_pages = (position + 1) * page <= dec_len[:, None]
    edge_page = position == dec_len[:, None] // page
    rest = (dec_len % page)[:, None]

    def counts(names):
        same = dec_pages[:, :, None] == names[None, None, :]
        full = jnp.sum((same & whole_pages[:, :, None]).astype(jnp.float32), 1).astype(jnp.bfloat16)
        part = jnp.sum((same & edge_page[:, :, None]).astype(jnp.float32), 1).astype(jnp.bfloat16)
        return full, part

    order = [0] + sends
    me = lax.axis_index("pool")
    fresh_srcs = jnp.repeat(
        source(jnp.full((size,), me, jnp.int32), jnp.asarray(order, jnp.int32), size), caps
    )
    fresh_names = slots + fresh_srcs * caps + jnp.tile(jnp.arange(caps, dtype=jnp.int32), size)

    state = prefill_first(suffix_q, fresh_kv)
    dec_state = decode_pool(dec_q, kv_pool, *counts(jnp.arange(slots, dtype=jnp.int32)), rest)
    groups = arrival_groups(order)
    for i, ks in enumerate(groups):
        final = i == len(groups) - 1
        new = prefill_more(
            suffix_q, fresh_kv, [arrived[k] for k in ks], ks, prefix_pages, prefix_len, state, cap, size, final
        )
        if not final:
            state = (state[0], *new)
    out, bad = new
    decode_out, suffix_out = finish(
        dec_q,
        dec_state,
        *counts(fresh_names),
        rest,
        bad,
        suffix_q,
        fresh_kv,
        prefix_pages,
        prefix_len,
        out,
        [arrived[k] for k in order],
        order,
        cap,
        size,
    )
    return (suffix_out, decode_out)


def arrival_groups(order):
    size = len(order)
    if size == 16:
        return [[0, 1, 2, 3], [12, 4, 8, 5], [13, 6, 9, 7], [14, 10], [15, 11]]
    per = -(-size // 4)
    return [order[i : i + per] for i in range(0, size, per)]


def solution(mesh):
    return jax.shard_map(
        functools.partial(shards, mesh.shape["pool"]),
        mesh=mesh,
        in_specs=(
            P(("groups", "pool"), "tp"),
            P(("groups", "pool"), None, None, "tp"),
            P(("groups", "pool"), None, None, "tp"),
            P(("groups", "pool"), "tp"),
            P(("groups", "pool"), None),
            P(("groups", "pool"), None),
            P(("groups", "pool")),
            P(("groups", "pool"), None),
            P(("groups", "pool"), None),
            P(("groups", "pool")),
        ),
        out_specs=(P(("groups", "pool"), "tp"), P(("groups", "pool"), "tp")),
        check_vma=False,
    )
```

```python
import functools

import jax
import jax.numpy as jnp
from jax import lax
from jax.experimental import pallas as pl
from jax.experimental.pallas import tpu as pltpu
from jax.sharding import PartitionSpec as P

GROUP = 8
HD = 128
LOG2E = 1.4426950408889634
CEXP = HD**-0.5 * LOG2E
NEG = -1e30
HUGE = 2.0**90
VMEM_LIMIT = 16 << 20
POOL_LIMIT = 56 << 20


HP_FIRST = 4

NT = (((1,), (1,)), ((), ()))
VM = pl.BlockSpec(memory_space=pltpu.VMEM)
SM = pl.BlockSpec(memory_space=pltpu.SMEM)
ANY = pl.BlockSpec(memory_space=pl.ANY)
HBM = pl.BlockSpec(memory_space=pltpu.HBM)
PARAMS = pltpu.CompilerParams(vmem_limit_bytes=VMEM_LIMIT)


def head_at(i):
    return pl.ds(pl.multiple_of(i * HD, HD), HD)


def partner(i, k, size):
    return i ^ k if size & (size - 1) == 0 else lax.rem(i + k, size)


def source(i, k, size):
    return i ^ k if size & (size - 1) == 0 else lax.rem(i - k + size, size)


def gather_pages(kv_pool, fresh_kv, fetch_slots, suffix_route, ks, size, after):
    _, _, page, width = kv_pool.shape
    n = len(ks)
    cap, caps = fetch_slots.shape[1] // size, suffix_route.shape[1] // size
    each = cap + caps

    def body(slots_ref, routes_ref, pool_ref, fresh_ref, *rest):
        outs, sem = rest[-n - 1 : -1], rest[-1]
        me = lax.axis_index("pool")
        for i, k in enumerate(ks):
            dest = partner(me, k, size)
            for c in range(cap):
                pltpu.make_async_copy(
                    pool_ref.at[slots_ref[0, dest * cap + c]], outs[i].at[:, c], sem.at[i]
                ).start()
            for c in range(caps):
                pltpu.make_async_copy(
                    fresh_ref.at[routes_ref[0, dest * caps + c]], outs[i].at[:, cap + c], sem.at[i]
                ).start()
        for i in range(n):
            pltpu.make_async_copy(outs[i], outs[i], sem.at[i]).wait()

    shape = (2, each, page, width)
    return pl.pallas_call(
        body,
        out_shape=[pltpu.VMEM(shape, kv_pool.dtype)] * n,
        in_specs=[SM, SM, HBM, HBM] + [ANY] * len(after),
        out_specs=[VM] * n,
        scratch_shapes=[pltpu.SemaphoreType.DMA((n,))],
        compiler_params=pltpu.CompilerParams(vmem_limit_bytes=POOL_LIMIT),
        cost_estimate=pl.CostEstimate(
            flops=0, transcendentals=0, bytes_accessed=2 * n * each * 2 * page * width * 2
        ),
        name="gather_pages",
    )(fetch_slots, suffix_route, kv_pool, fresh_kv, *after)


def mark_visible(vis_ref, at, k, cap, page, pages_ref, plen_ref, size):
    wanted = pages_ref[...]
    keys = cap * page
    order = lax.broadcasted_iota(jnp.int32, (keys, wanted.shape[1]), 1)
    token = lax.broadcasted_iota(jnp.int32, (keys, 1), 0)
    name = source(lax.axis_index("pool"), k, size) * cap + token // page
    place = jnp.sum(jnp.where(wanted == name, order, 0), axis=1, keepdims=True)
    seen = place * page + token % page < plen_ref[0]
    vis_ref[at : at + keys, :] = jnp.broadcast_to(jnp.where(seen, 1.0, 0.0), (keys, HD))


def place_keys(k_ref, v_ref, vis_ref, vis_at, at, g, piece, stand_in, cap, page):
    keys = cap * page
    rows = slice(at, at + keys)
    seen = vis_ref[vis_at : vis_at + keys, :] > 0
    key = piece[0, 0:cap, :, head_at(g)].reshape(keys, HD).astype(jnp.float32)
    val = piece[1, 0:cap, :, head_at(g)].reshape(keys, HD).astype(jnp.float32)
    k_ref[rows, 0:HD] = jnp.where(seen, key, stand_in).astype(jnp.bfloat16)
    v_ref[rows, 0:HD] = jnp.where(seen, val, 0.0).astype(jnp.bfloat16)


def prefill_first(q, fresh, after):
    tokens, qwidth = q.shape
    _, width = fresh.shape[2:]
    rows = min(256, tokens)

    def body(q_ref, f_ref, _, m_ref, acc_ref, l_ref, k_ref, v_ref):
        v_ref[:, HD:] = jnp.ones((tokens, HD), jnp.bfloat16)
        lane = lax.broadcasted_iota(jnp.int32, (rows, HD), 1)
        row = lax.broadcasted_iota(jnp.int32, (rows, rows), 0)
        col = lax.broadcasted_iota(jnp.int32, (rows, rows), 1)

        def group(g, carry):
            k_ref[...] = f_ref[:, 0, :, head_at(g)].reshape(tokens, HD)
            v_ref[:, 0:HD] = f_ref[:, 1, :, head_at(g)].reshape(tokens, HD)

            def heads(b, carry):
                for h in range(HP_FIRST):
                    cols = head_at(g * GROUP + b * HP_FIRST + h)
                    for r in range(0, tokens, rows):
                        rs = slice(r, r + rows)
                        s = lax.dot_general(
                            q_ref[rs, cols], k_ref[0 : r + rows, :], NT, preferred_element_type=jnp.float32
                        )
                        diag = jnp.where(col <= row, s[:, r:], NEG)
                        s = jnp.concatenate([s[:, :r], diag], 1) if r else diag
                        m = jnp.max(s, axis=1, keepdims=True).astype(jnp.bfloat16).astype(jnp.float32)
                        p = jnp.exp2((s - m) * CEXP).astype(jnp.bfloat16)
                        new = jnp.dot(p, v_ref[0 : r + rows, :], preferred_element_type=jnp.float32)
                        acc_ref[rs, cols] = new[:, :HD]
                        l_ref[rs, cols] = new[:, HD:]
                        m_ref[rs, cols] = jnp.where(lane == 0, m, 0.0).astype(jnp.bfloat16)
                return carry

            return lax.fori_loop(0, GROUP // HP_FIRST, heads, carry)

        lax.fori_loop(0, width // HD, group, 0)

    wide = pltpu.VMEM((tokens, qwidth), jnp.float32)
    work = tokens * tokens * (qwidth // HD) // 2
    return pl.pallas_call(
        body,
        out_shape=[pltpu.VMEM((tokens, qwidth), jnp.bfloat16), wide, wide],
        in_specs=[VM, VM, ANY],
        out_specs=[VM] * 3,
        scratch_shapes=[
            pltpu.VMEM((tokens, HD), jnp.bfloat16),
            pltpu.VMEM((tokens, 2 * HD), jnp.bfloat16),
        ],
        compiler_params=PARAMS,
        cost_estimate=pl.CostEstimate(flops=8 * HD * work, transcendentals=work, bytes_accessed=8 * work // HD),
        name="prefill_first",
    )(q, fresh, after)


def add_pages(k_ref, v_ref, q_ref, m_ref, g, emit):
    for h in range(GROUP):
        cols = head_at(g * GROUP + h)
        lhs = jnp.concatenate([q_ref[:, cols], m_ref[:, cols]], 1)
        s = lax.dot_general(lhs, k_ref[...], NT, preferred_element_type=jnp.float32)
        p = jnp.exp2(s * CEXP).astype(jnp.bfloat16)
        new = jnp.dot(p, v_ref[...], preferred_element_type=jnp.float32)
        emit(cols, new[:, :HD], new[:, HD:])


def start_pages(vis_ref, k_ref, v_ref, pages_ref, plen_ref, ks, cap, page, size):
    keys = k_ref.shape[0]
    for i, k in enumerate(ks):
        mark_visible(vis_ref, i * cap * page, k, cap, page, pages_ref, plen_ref, size)
    lane = lax.broadcasted_iota(jnp.int32, (keys, HD), 1)
    k_ref[:, HD:] = jnp.where(lane == 0, -1.0, 0.0).astype(jnp.bfloat16)
    v_ref[:, HD:] = vis_ref[...].astype(jnp.bfloat16)


def prefill_more(q, fresh, pieces, ks, pages, plen, state, cap, size):
    tokens, qwidth = q.shape
    page, width = fresh.shape[2:]
    n = len(pieces)
    keys = n * cap * page

    def body(*refs):
        plen_ref, pages_ref, q_ref, f_ref = refs[:4]
        piece_refs = refs[4 : 4 + n]
        m_ref, acc_in, l_in, acc_ref, l_ref, vis_ref, k_ref, v_ref = refs[4 + n :]
        start_pages(vis_ref, k_ref, v_ref, pages_ref, plen_ref, ks, cap, page, size)

        def group(g, carry):
            stand_in = f_ref[0, 0, :, head_at(g)][0:1].astype(jnp.float32)
            for i in range(n):
                at = i * cap * page
                place_keys(k_ref, v_ref, vis_ref, at, at, g, piece_refs[i], stand_in, cap, page)

            def emit(cols, acc, total):
                acc_ref[:, cols] = acc_in[:, cols] + acc
                l_ref[:, cols] = l_in[:, cols] + total

            add_pages(k_ref, v_ref, q_ref, m_ref, g, emit)
            return carry

        lax.fori_loop(0, width // HD, group, 0)

    work = tokens * keys * (qwidth // HD)
    wide = pltpu.VMEM((tokens, qwidth), jnp.float32)
    return pl.pallas_call(
        body,
        out_shape=[wide, wide],
        in_specs=[SM, VM, VM, VM] + [VM] * n + [VM] * 3,
        out_specs=[VM, VM],
        input_output_aliases={5 + n: 0, 6 + n: 1},
        scratch_shapes=[
            pltpu.VMEM((keys, HD), jnp.float32),
            pltpu.VMEM((keys, 2 * HD), jnp.bfloat16),
            pltpu.VMEM((keys, 2 * HD), jnp.bfloat16),
        ],
        compiler_params=PARAMS,
        cost_estimate=pl.CostEstimate(
            flops=8 * HD * work, transcendentals=work, bytes_accessed=8 * work // HD
        ),
        name="prefill_more",
    )(plen, pages, q, fresh, *pieces, *state)


def token_counts(full, part, rest, page):
    pages = full.shape[1]
    key = lax.broadcasted_iota(jnp.int32, (pages, pages * page), 1) // page
    row = lax.broadcasted_iota(jnp.int32, (pages, pages * page), 0)
    spread = jnp.where(key == row, 1.0, 0.0).astype(jnp.bfloat16)
    times = jnp.dot(full, spread, preferred_element_type=jnp.float32)
    edge = jnp.dot(part, spread, preferred_element_type=jnp.float32)
    token = lax.broadcasted_iota(jnp.int32, times.shape, 1) % page
    return times + jnp.where(token < rest, edge, 0.0)


def decode_fold(q_ref, g, key, val, times, m_old, l_old, acc_old):
    requests = times.shape[0]
    q = jnp.concatenate(
        [q_ref[:, (g * GROUP + h) * HD : (g * GROUP + h + 1) * HD] for h in range(GROUP)], 0
    )
    s = lax.dot_general(q, key, NT, preferred_element_type=jnp.float32)
    keys = s.shape[1]
    s = s.reshape(GROUP, requests, keys)
    s = jnp.where((times > 0)[None], s, NEG).reshape(GROUP * requests, keys)
    m = jnp.maximum(jnp.max(s, axis=1, keepdims=True), m_old)
    p = jnp.exp2((s - m) * CEXP).reshape(GROUP, requests, keys) * times[None]
    p = p.reshape(GROUP * requests, keys)
    total = jnp.sum(p, axis=1, keepdims=True)
    new = jnp.dot(p.astype(jnp.bfloat16), val, preferred_element_type=jnp.float32)
    alpha = jnp.exp2((m_old - m) * CEXP)
    return m, l_old * alpha + total, acc_old * alpha + new


def decode_pool(dec_q, kv_pool, full, part, rest):
    slots, _, page, width = kv_pool.shape
    requests = dec_q.shape[0]
    heads_kv = width // HD
    block = 128 if slots % 128 == 0 else slots
    steps = slots // block

    def body(q_ref, kv_ref, full_ref, part_ref, rest_ref, acc_ref, m_ref, l_ref):
        @pl.when(pl.program_id(0) == 0)
        def _():
            acc_ref[...] = jnp.zeros_like(acc_ref)
            m_ref[...] = jnp.full_like(m_ref, NEG)
            l_ref[...] = jnp.zeros_like(l_ref)

        times = token_counts(full_ref[...], part_ref[...], rest_ref[...], page)
        for g in range(heads_kv):
            cols = slice(g * HD, (g + 1) * HD)
            key = kv_ref[:, 0, :, cols].reshape(block * page, HD)
            val = kv_ref[:, 1, :, cols].reshape(block * page, HD)
            m, l, acc = decode_fold(
                q_ref, g, key, val, times, m_ref[g, :, 0:1], l_ref[g, :, 0:1], acc_ref[g]
            )
            m_ref[g] = jnp.broadcast_to(m, m_ref.shape[1:])
            l_ref[g] = jnp.broadcast_to(l, l_ref.shape[1:])
            acc_ref[g] = acc

    shape = (heads_kv, GROUP * requests, HD)
    whole = pl.BlockSpec(shape, lambda i: (0, 0, 0))
    return pl.pallas_call(
        body,
        grid=(steps,),
        out_shape=[jax.ShapeDtypeStruct(shape, jnp.float32)] * 3,
        in_specs=[
            pl.BlockSpec(dec_q.shape, lambda i: (0, 0)),
            pl.BlockSpec((block, 2, page, width), lambda i: (i, 0, 0, 0)),
            pl.BlockSpec((requests, block), lambda i: (0, i)),
            pl.BlockSpec((requests, block), lambda i: (0, i)),
            pl.BlockSpec(rest.shape, lambda i: (0, 0)),
        ],
        out_specs=[whole] * 3,
        compiler_params=pltpu.CompilerParams(vmem_limit_bytes=POOL_LIMIT),
        cost_estimate=pl.CostEstimate(
            flops=4 * HD * heads_kv * GROUP * requests * slots * page,
            transcendentals=heads_kv * GROUP * requests * slots * page,
            bytes_accessed=slots * 2 * page * width * 2,
        ),
        name="decode_pool",
    )(dec_q, kv_pool, full, part, rest)


def fresh_rows(piece, which, cap, cols):
    rows = piece[which, cap:, :, cols]
    return rows.reshape(rows.shape[0] * rows.shape[1], HD)


def decode_fresh(dec_q, pieces, state, full, part, rest, cap):
    page, width = pieces[0].shape[2:]
    caps = pieces[0].shape[1] - cap
    n = len(pieces)
    heads_kv = width // HD
    rows = state[0].shape[1]

    def body(*refs):
        q_ref, acc_in, m_in, l_in, full_ref, part_ref, rest_ref = refs[:7]
        piece_refs = refs[7 : 7 + n]
        acc_ref, m_ref, l_ref = refs[7 + n :]
        times = token_counts(full_ref[...], part_ref[...], rest_ref[...], page)
        for g in range(heads_kv):
            cols = slice(g * HD, (g + 1) * HD)
            key = jnp.concatenate([fresh_rows(p, 0, 0, cols) for p in piece_refs], 0)
            val = jnp.concatenate([fresh_rows(p, 1, 0, cols) for p in piece_refs], 0)
            m, l, acc = decode_fold(
                q_ref, g, key, val, times, m_in[g, :, 0:1], l_in[g, :, 0:1], acc_in[g]
            )
            m_ref[g] = jnp.broadcast_to(m, m_ref.shape[1:])
            l_ref[g] = jnp.broadcast_to(l, l_ref.shape[1:])
            acc_ref[g] = acc

    whole = lambda a: pl.BlockSpec(a.shape, lambda i: (0,) * a.ndim)
    each = pieces[0].shape[1]
    return pl.pallas_call(
        body,
        grid=(1,),
        out_shape=[jax.ShapeDtypeStruct(a.shape, a.dtype) for a in state],
        in_specs=[whole(a) for a in (dec_q, *state, full, part, rest)]
        + [pl.BlockSpec((2, caps, page, width), lambda i: (0, each // caps - 1, 0, 0))] * n,
        out_specs=[whole(a) for a in state],
        compiler_params=PARAMS,
        cost_estimate=pl.CostEstimate(
            flops=4 * HD * heads_kv * rows * n * caps * page,
            transcendentals=heads_kv * rows * n * caps * page,
            bytes_accessed=n * caps * 2 * page * width * 2,
        ),
        name="decode_fresh",
    )(dec_q, *state, full, part, rest, *pieces)


def finish(dec_q, dec_state, times, q, fresh, pages, plen, state, pieces, ks, last, cap, size):
    page, width = fresh.shape[2:]
    requests = dec_q.shape[0]
    heads_kv = width // HD
    tokens, qwidth = q.shape
    n, tail = len(pieces), len(last)
    keys = cap * page
    rows = min(128, tokens)
    held = n * keys

    def body(*refs):
        dq_ref, dacc_ref, dm_ref, dl_ref, times_ref, q_ref, f_ref, pages_ref, plen_ref = refs[:9]
        m_ref, acc_ref, l_ref = refs[9:12]
        last_refs = refs[12 : 12 + tail]
        piece_refs = refs[12 + tail : 12 + tail + n]
        (dec_ref, out_hbm, out_ref, sem, vis_ref, k_ref, v_ref, all_vis, all_k, all_v, page_ref, block_ref) = (
            refs[12 + tail + n :]
        )
        start_pages(vis_ref, k_ref, v_ref, pages_ref, plen_ref, last, cap, page, size)

        def out_copy(g):
            cols = pl.ds(pl.multiple_of(g * GROUP * HD, GROUP * HD), GROUP * HD)
            return pltpu.make_async_copy(out_ref.at[:, cols], out_hbm.at[:, cols], sem.at[g])

        def group(g, sums):
            stand_in = f_ref[0, 0, :, head_at(g)][0:1].astype(jnp.float32)
            for i in range(tail):
                place_keys(k_ref, v_ref, vis_ref, i * keys, i * keys, g, last_refs[i], stand_in, cap, page)
            partial = []

            def emit(cols, acc, total):
                total = l_ref[:, cols] + total
                out_ref[:, cols] = ((acc_ref[:, cols] + acc) / total).astype(out_ref.dtype)
                partial.append(jnp.sum(total.reshape(-1, 8, HD), axis=0))

            add_pages(k_ref, v_ref, q_ref, m_ref, g, emit)
            out_copy(g).start()
            return sum(partial, sums)

        sums = lax.fori_loop(0, heads_kv, group, jnp.zeros((8, HD), jnp.float32))

        times = times_ref[...]
        for g in range(heads_kv):
            cols = slice(g * HD, (g + 1) * HD)
            key = jnp.concatenate([fresh_rows(p, 0, cap, cols) for p in last_refs], 0)
            val = jnp.concatenate([fresh_rows(p, 1, cap, cols) for p in last_refs], 0)
            _, l, acc = decode_fold(
                dq_ref, g, key, val, times, dm_ref[g, :, 0:1], dl_ref[g, :, 0:1], dacc_ref[g]
            )
            done = (acc / l).astype(dec_ref.dtype)
            for h in range(GROUP):
                at = (g * GROUP + h) * HD
                dec_ref[:, at : at + HD] = done[h * requests : (h + 1) * requests]
        for g in range(heads_kv):
            out_copy(g).wait()

        @pl.when(jnp.logical_not(jnp.sum(sums) <= HUGE))
        def _():
            for i, k in enumerate(ks):
                mark_visible(all_vis, i * keys, k, cap, page, pages_ref, plen_ref, size)
            all_v[0:tokens, HD:] = jnp.ones((tokens, HD), jnp.bfloat16)
            all_v[tokens:, HD:] = all_vis[...].astype(jnp.bfloat16)
            col = lax.broadcasted_iota(jnp.int32, (rows, tokens), 1)
            row = lax.broadcasted_iota(jnp.int32, (rows, tokens), 0)

            def again(g, carry):
                all_k[0:tokens, :] = f_ref[:, 0, :, head_at(g)].reshape(tokens, HD)
                all_v[0:tokens, 0:HD] = f_ref[:, 1, :, head_at(g)].reshape(tokens, HD)
                stand_in = f_ref[0, 0, :, head_at(g)][0:1].astype(jnp.float32)
                for i in range(n):
                    pltpu.sync_copy(piece_refs[i].at[:, 0:cap], page_ref)
                    place_keys(all_k, all_v, all_vis, i * keys, tokens + i * keys, g, page_ref, stand_in, cap, page)

                def block(b, carry):
                    r = pl.multiple_of((b % (tokens // rows)) * rows, rows)
                    cols = head_at(g * GROUP + b // (tokens // rows))
                    qb = q_ref[pl.ds(r, rows), cols]
                    s = lax.dot_general(qb, all_k[...], NT, preferred_element_type=jnp.float32)
                    own = jnp.where(col <= row + r, s[:, :tokens], NEG)
                    s = jnp.concatenate([own, s[:, tokens:]], 1)
                    m = jnp.max(s, axis=1, keepdims=True)
                    p = jnp.exp2((s - m) * CEXP).astype(jnp.bfloat16)
                    new = jnp.dot(p, all_v[...], preferred_element_type=jnp.float32)
                    block_ref[...] = (new[:, :HD] / new[:, HD:]).astype(block_ref.dtype)
                    pltpu.sync_copy(block_ref, out_hbm.at[pl.ds(r, rows), cols])
                    return carry

                return lax.fori_loop(0, GROUP * (tokens // rows), block, carry)

            lax.fori_loop(0, heads_kv, again, 0)

    work = tokens * tail * keys * (qwidth // HD)
    return pl.pallas_call(
        body,
        out_shape=[
            jax.ShapeDtypeStruct(dec_q.shape, dec_q.dtype),
            jax.ShapeDtypeStruct(q.shape, q.dtype),
        ],
        in_specs=[VM] * 8 + [SM] + [VM] * (3 + tail) + [ANY] * n,
        out_specs=[VM, ANY],
        scratch_shapes=[
            pltpu.VMEM(q.shape, q.dtype),
            pltpu.SemaphoreType.DMA((heads_kv,)),
            pltpu.VMEM((tail * keys, HD), jnp.float32),
            pltpu.VMEM((tail * keys, 2 * HD), jnp.bfloat16),
            pltpu.VMEM((tail * keys, 2 * HD), jnp.bfloat16),
            pltpu.VMEM((held, HD), jnp.float32),
            pltpu.VMEM((tokens + held, HD), jnp.bfloat16),
            pltpu.VMEM((tokens + held, 2 * HD), jnp.bfloat16),
            pltpu.VMEM((2, cap, page, width), q.dtype),
            pltpu.VMEM((rows, HD), q.dtype),
        ],
        compiler_params=PARAMS,
        cost_estimate=pl.CostEstimate(
            flops=8 * HD * work, transcendentals=work, bytes_accessed=8 * work // HD
        ),
        name="finish",
    )(dec_q, *dec_state, times, q, fresh, pages, plen, *state, *[pieces[ks.index(k)] for k in last], *pieces)


def send_order(size):
    if size == 16:
        return [12, 8, 1, 2, 3, 4, 13, 5, 9, 6, 14, 7, 10, 15, 11]
    return list(range(1, size))


def shards(
    size,
    suffix_q,
    fresh_kv,
    kv_pool,
    dec_q,
    fetch_slots,
    prefix_pages,
    prefix_len,
    suffix_route,
    dec_pages,
    dec_len,
):
    page = kv_pool.shape[2]
    slots = kv_pool.shape[0]
    cap = fetch_slots.shape[1] // size
    caps = suffix_route.shape[1] // size
    sends = send_order(size)
    lead = max(1, size // 8)
    batches = [sends[:lead], sends[lead:] + [0]]
    outgoing, after = {}, []
    for ks in batches:
        outs = gather_pages(kv_pool, fresh_kv, fetch_slots, suffix_route, ks, size, after)
        after = outs[:1]
        outgoing |= dict(zip(ks, outs, strict=True))
    arrived = {0: outgoing[0]}
    for k in sends:
        pairs = [(i, i ^ k if size & (size - 1) == 0 else (i + k) % size) for i in range(size)]
        arrived[k] = lax.ppermute(outgoing[k], "pool", pairs)

    context = dec_pages.shape[1]
    position = jnp.arange(context, dtype=jnp.int32)[None, :]
    whole_pages = (position + 1) * page <= dec_len[:, None]
    edge_page = position == dec_len[:, None] // page
    rest = (dec_len % page)[:, None]

    def counts(names):
        same = dec_pages[:, :, None] == names[None, None, :]
        full = jnp.sum((same & whole_pages[:, :, None]).astype(jnp.float32), 1).astype(jnp.bfloat16)
        part = jnp.sum((same & edge_page[:, :, None]).astype(jnp.float32), 1).astype(jnp.bfloat16)
        return full, part

    groups = arrival_groups([0] + sends)
    order = [k for ks in groups for k in ks]
    early, last = order[: -len(groups[-1])], groups[-1]
    me = lax.axis_index("pool")

    def fresh_names(ks):
        srcs = source(jnp.full((len(ks),), me, jnp.int32), jnp.asarray(ks, jnp.int32), size)
        return slots + jnp.repeat(srcs, caps) * caps + jnp.tile(jnp.arange(caps, dtype=jnp.int32), len(ks))

    last_names = jnp.repeat(fresh_names(last), page)[None, None, :]
    last_token = (jnp.arange(last_names.shape[2], dtype=jnp.int32) % page)[None, None, :]
    last_seen = position[:, :, None] * page + last_token < dec_len[:, None, None]
    last_times = jnp.sum(((dec_pages[:, :, None] == last_names) & last_seen).astype(jnp.float32), 1)

    dec_state = decode_pool(dec_q, kv_pool, *counts(jnp.arange(slots, dtype=jnp.int32)), rest)
    state = prefill_first(suffix_q, fresh_kv, dec_state[1])
    for ks in groups[:-1]:
        new = prefill_more(
            suffix_q, fresh_kv, [arrived[k] for k in ks], ks, prefix_pages, prefix_len, state, cap, size
        )
        state = (state[0], *new)
    dec_state = decode_fresh(
        dec_q, [arrived[k] for k in early], dec_state, *counts(fresh_names(early)), rest, cap
    )
    decode_out, suffix_out = finish(
        dec_q,
        dec_state,
        last_times,
        suffix_q,
        fresh_kv,
        prefix_pages,
        prefix_len,
        state,
        [arrived[k] for k in order],
        order,
        last,
        cap,
        size,
    )
    return (suffix_out, decode_out)


def arrival_groups(order):
    size = len(order)
    if size == 16:
        return [[0, 1, 2, 3], [12, 4, 8, 5], [13, 6, 9, 7], [14, 10], [15], [11]]
    per = -(-size // 4)
    return [order[i : min(i + per, size - 1)] for i in range(0, size - 1, per)] + [order[-1:]]


def solution(mesh):
    size = mesh.shape["pool"]
    return jax.shard_map(
        functools.partial(shards, size),
        mesh=mesh,
        in_specs=(
            P(("groups", "pool"), "tp"),
            P(("groups", "pool"), None, None, "tp"),
            P(("groups", "pool"), None, None, "tp"),
            P(("groups", "pool"), "tp"),
            P(("groups", "pool"), None),
            P(("groups", "pool"), None),
            P(("groups", "pool")),
            P(("groups", "pool"), None),
            P(("groups", "pool"), None),
            P(("groups", "pool")),
        ),
        out_specs=(P(("groups", "pool"), "tp"), P(("groups", "pool"), "tp")),
        check_vma=False,
    )
```

```python
import functools

import jax
import jax.numpy as jnp
from jax import lax
from jax.experimental import pallas as pl
from jax.experimental.pallas import tpu as pltpu
from jax.sharding import PartitionSpec as P

GROUP = 8
HD = 128
LOG2E = 1.4426950408889634
CEXP = HD**-0.5 * LOG2E
NEG = -1e30
HUGE = 2.0**90
VMEM_LIMIT = 16 << 20
POOL_LIMIT = 56 << 20


NT = (((1,), (1,)), ((), ()))
VM = pl.BlockSpec(memory_space=pltpu.VMEM)
SM = pl.BlockSpec(memory_space=pltpu.SMEM)
ANY = pl.BlockSpec(memory_space=pl.ANY)
HBM = pl.BlockSpec(memory_space=pltpu.HBM)
PARAMS = pltpu.CompilerParams(vmem_limit_bytes=VMEM_LIMIT)


def head_at(i):
    return pl.ds(pl.multiple_of(i * HD, HD), HD)


def partner(i, k, size):
    return i ^ k if size & (size - 1) == 0 else lax.rem(i + k, size)


def source(i, k, size):
    return i ^ k if size & (size - 1) == 0 else lax.rem(i - k + size, size)


def gather_pages(kv_pool, fresh_kv, fetch_slots, suffix_route, ks, size, after):
    _, _, page, width = kv_pool.shape
    n = len(ks)
    cap, caps = fetch_slots.shape[1] // size, suffix_route.shape[1] // size
    each = cap + caps

    def body(slots_ref, routes_ref, pool_ref, fresh_ref, *rest):
        outs, sem = rest[-n - 1 : -1], rest[-1]
        me = lax.axis_index("pool")
        for i, k in enumerate(ks):
            dest = partner(me, k, size)
            for c in range(cap):
                pltpu.make_async_copy(
                    pool_ref.at[slots_ref[0, dest * cap + c]], outs[i].at[:, c], sem.at[i]
                ).start()
            for c in range(caps):
                pltpu.make_async_copy(
                    fresh_ref.at[routes_ref[0, dest * caps + c]], outs[i].at[:, cap + c], sem.at[i]
                ).start()
        for i in range(n):
            pltpu.make_async_copy(outs[i], outs[i], sem.at[i]).wait()

    shape = (2, each, page, width)
    return pl.pallas_call(
        body,
        out_shape=[pltpu.VMEM(shape, kv_pool.dtype)] * n,
        in_specs=[SM, SM, HBM, HBM] + [ANY] * len(after),
        out_specs=[VM] * n,
        scratch_shapes=[pltpu.SemaphoreType.DMA((n,))],
        compiler_params=pltpu.CompilerParams(vmem_limit_bytes=POOL_LIMIT),
        cost_estimate=pl.CostEstimate(
            flops=0, transcendentals=0, bytes_accessed=2 * n * each * 2 * page * width * 2
        ),
        name="gather_pages",
    )(fetch_slots, suffix_route, kv_pool, fresh_kv, *after)


def mark_visible(vis_ref, at, k, cap, page, pages_ref, plen_ref, size):
    wanted = pages_ref[...]
    keys = cap * page
    order = lax.broadcasted_iota(jnp.int32, (keys, wanted.shape[1]), 1)
    token = lax.broadcasted_iota(jnp.int32, (keys, 1), 0)
    name = source(lax.axis_index("pool"), k, size) * cap + token // page
    place = jnp.sum(jnp.where(wanted == name, order, 0), axis=1, keepdims=True)
    seen = place * page + token % page < plen_ref[0]
    vis_ref[at : at + keys, :] = jnp.broadcast_to(jnp.where(seen, 1.0, 0.0), (keys, HD))


def place_keys(k_ref, v_ref, vis_ref, vis_at, at, g, piece, stand_in, cap, page):
    keys = cap * page
    rows = slice(at, at + keys)
    seen = vis_ref[vis_at : vis_at + keys, :] > 0
    key = piece[0, 0:cap, :, head_at(g)].reshape(keys, HD).astype(jnp.float32)
    val = piece[1, 0:cap, :, head_at(g)].reshape(keys, HD).astype(jnp.float32)
    k_ref[rows, 0:HD] = jnp.where(seen, key, stand_in).astype(jnp.bfloat16)
    v_ref[rows, 0:HD] = jnp.where(seen, val, 0.0).astype(jnp.bfloat16)


def prefill_first(q, fresh, after):
    tokens, qwidth = q.shape
    _, width = fresh.shape[2:]
    rows = min(256, tokens)

    def body(q_ref, f_ref, _, m_ref, acc_ref, l_ref, k_ref, v_ref):
        v_ref[:, HD:] = jnp.ones((tokens, HD), jnp.bfloat16)
        k_lane = lax.broadcasted_iota(jnp.int32, (tokens, HD), 1)
        k_ref[:, HD:] = jnp.where(k_lane == 0, -1.0, 0.0).astype(jnp.bfloat16)
        row = lax.broadcasted_iota(jnp.int32, (rows, rows), 0)
        col = lax.broadcasted_iota(jnp.int32, (rows, rows), 1)

        def group(g, carry):
            key = f_ref[:, 0, :, head_at(g)].reshape(tokens, HD)
            k_ref[:, 0:HD] = key
            v_ref[:, 0:HD] = f_ref[:, 1, :, head_at(g)].reshape(tokens, HD)
            key = key.astype(jnp.float32)
            for h in range(GROUP):
                cols = head_at(g * GROUP + h)
                own = jnp.sum(q_ref[:, cols].astype(jnp.float32) * key, axis=1, keepdims=True)
                m_ref[:, cols] = jnp.where(k_lane == 0, own, 0.0).astype(jnp.bfloat16)
            for h in range(GROUP):
                cols = head_at(g * GROUP + h)
                for r in range(0, tokens, rows):
                    rs = slice(r, r + rows)
                    lhs = jnp.concatenate([q_ref[rs, cols], m_ref[rs, cols]], 1)
                    s = lax.dot_general(lhs, k_ref[0 : r + rows, :], NT, preferred_element_type=jnp.float32)
                    diag = jnp.where(col <= row, s[:, r:], NEG)
                    s = jnp.concatenate([s[:, :r], diag], 1) if r else diag
                    p = jnp.exp2(s * CEXP).astype(jnp.bfloat16)
                    new = jnp.dot(p, v_ref[0 : r + rows, :], preferred_element_type=jnp.float32)
                    acc_ref[rs, cols] = new[:, :HD]
                    l_ref[rs, cols] = new[:, HD:]
            return carry

        lax.fori_loop(0, width // HD, group, 0)

    wide = pltpu.VMEM((tokens, qwidth), jnp.float32)
    work = tokens * tokens * (qwidth // HD) // 2
    return pl.pallas_call(
        body,
        out_shape=[pltpu.VMEM((tokens, qwidth), jnp.bfloat16), wide, wide],
        in_specs=[VM, VM, SM],
        out_specs=[VM] * 3,
        scratch_shapes=[
            pltpu.VMEM((tokens, 2 * HD), jnp.bfloat16),
            pltpu.VMEM((tokens, 2 * HD), jnp.bfloat16),
        ],
        compiler_params=PARAMS,
        cost_estimate=pl.CostEstimate(flops=8 * HD * work, transcendentals=work, bytes_accessed=8 * work // HD),
        name="prefill_first",
    )(q, fresh, after)


def add_pages(k_ref, v_ref, q_ref, m_ref, g, emit):
    for h in range(GROUP):
        cols = head_at(g * GROUP + h)
        lhs = jnp.concatenate([q_ref[:, cols], m_ref[:, cols]], 1)
        s = lax.dot_general(lhs, k_ref[...], NT, preferred_element_type=jnp.float32)
        p = jnp.exp2(s * CEXP).astype(jnp.bfloat16)
        new = jnp.dot(p, v_ref[...], preferred_element_type=jnp.float32)
        emit(cols, new[:, :HD], new[:, HD:])


def start_pages(vis_ref, k_ref, v_ref, pages_ref, plen_ref, ks, cap, page, size):
    keys = k_ref.shape[0]
    for i, k in enumerate(ks):
        mark_visible(vis_ref, i * cap * page, k, cap, page, pages_ref, plen_ref, size)
    lane = lax.broadcasted_iota(jnp.int32, (keys, HD), 1)
    k_ref[:, HD:] = jnp.where(lane == 0, -1.0, 0.0).astype(jnp.bfloat16)
    v_ref[:, HD:] = vis_ref[...].astype(jnp.bfloat16)


def prefill_more(q, fresh, pieces, ks, pages, plen, state, cap, size):
    tokens, qwidth = q.shape
    page, width = fresh.shape[2:]
    n = len(pieces)
    keys = n * cap * page

    def body(*refs):
        plen_ref, pages_ref, q_ref, f_ref = refs[:4]
        piece_refs = refs[4 : 4 + n]
        m_ref, acc_in, l_in, acc_ref, l_ref, vis_ref, k_ref, v_ref = refs[4 + n :]
        start_pages(vis_ref, k_ref, v_ref, pages_ref, plen_ref, ks, cap, page, size)

        def group(g, carry):
            stand_in = f_ref[0, 0, :, head_at(g)][0:1].astype(jnp.float32)
            for i in range(n):
                at = i * cap * page
                place_keys(k_ref, v_ref, vis_ref, at, at, g, piece_refs[i], stand_in, cap, page)

            def emit(cols, acc, total):
                acc_ref[:, cols] = acc_in[:, cols] + acc
                l_ref[:, cols] = l_in[:, cols] + total

            add_pages(k_ref, v_ref, q_ref, m_ref, g, emit)
            return carry

        lax.fori_loop(0, width // HD, group, 0)

    work = tokens * keys * (qwidth // HD)
    wide = pltpu.VMEM((tokens, qwidth), jnp.float32)
    return pl.pallas_call(
        body,
        out_shape=[wide, wide],
        in_specs=[SM, VM, VM, VM] + [VM] * n + [VM] * 3,
        out_specs=[VM, VM],
        input_output_aliases={5 + n: 0, 6 + n: 1},
        scratch_shapes=[
            pltpu.VMEM((keys, HD), jnp.float32),
            pltpu.VMEM((keys, 2 * HD), jnp.bfloat16),
            pltpu.VMEM((keys, 2 * HD), jnp.bfloat16),
        ],
        compiler_params=PARAMS,
        cost_estimate=pl.CostEstimate(
            flops=8 * HD * work, transcendentals=work, bytes_accessed=8 * work // HD
        ),
        name="prefill_more",
    )(plen, pages, q, fresh, *pieces, *state)


def token_counts(full, part, rest, page):
    pages = full.shape[1]
    key = lax.broadcasted_iota(jnp.int32, (pages, pages * page), 1) // page
    row = lax.broadcasted_iota(jnp.int32, (pages, pages * page), 0)
    spread = jnp.where(key == row, 1.0, 0.0).astype(jnp.bfloat16)
    times = jnp.dot(full, spread, preferred_element_type=jnp.float32)
    edge = jnp.dot(part, spread, preferred_element_type=jnp.float32)
    token = lax.broadcasted_iota(jnp.int32, times.shape, 1) % page
    return times + jnp.where(token < rest, edge, 0.0)


def decode_fold(q_ref, g, key, val, times, m_old, l_old, acc_old):
    requests = times.shape[0]
    q = jnp.concatenate(
        [q_ref[:, (g * GROUP + h) * HD : (g * GROUP + h + 1) * HD] for h in range(GROUP)], 0
    )
    s = lax.dot_general(q, key, NT, preferred_element_type=jnp.float32)
    keys = s.shape[1]
    s = s.reshape(GROUP, requests, keys)
    s = jnp.where((times > 0)[None], s, NEG).reshape(GROUP * requests, keys)
    m = jnp.maximum(jnp.max(s, axis=1, keepdims=True), m_old)
    p = jnp.exp2((s - m) * CEXP).reshape(GROUP, requests, keys) * times[None]
    p = p.reshape(GROUP * requests, keys)
    total = jnp.sum(p, axis=1, keepdims=True)
    new = jnp.dot(p.astype(jnp.bfloat16), val, preferred_element_type=jnp.float32)
    alpha = jnp.exp2((m_old - m) * CEXP)
    return m, l_old * alpha + total, acc_old * alpha + new


def decode_pool(dec_q, kv_pool, full, part, rest):
    slots, _, page, width = kv_pool.shape
    requests = dec_q.shape[0]
    heads_kv = width // HD
    block = 128 if slots % 128 == 0 else slots
    steps = slots // block

    def body(q_ref, kv_ref, full_ref, part_ref, rest_ref, acc_ref, m_ref, l_ref, token_ref):
        token_ref[0] = 0

        @pl.when(pl.program_id(0) == 0)
        def _():
            acc_ref[...] = jnp.zeros_like(acc_ref)
            m_ref[...] = jnp.full_like(m_ref, NEG)
            l_ref[...] = jnp.zeros_like(l_ref)

        times = token_counts(full_ref[...], part_ref[...], rest_ref[...], page)
        for g in range(heads_kv):
            cols = slice(g * HD, (g + 1) * HD)
            key = kv_ref[:, 0, :, cols].reshape(block * page, HD)
            val = kv_ref[:, 1, :, cols].reshape(block * page, HD)
            m, l, acc = decode_fold(
                q_ref, g, key, val, times, m_ref[g, :, 0:1], l_ref[g, :, 0:1], acc_ref[g]
            )
            m_ref[g] = jnp.broadcast_to(m, m_ref.shape[1:])
            l_ref[g] = jnp.broadcast_to(l, l_ref.shape[1:])
            acc_ref[g] = acc

    shape = (heads_kv, GROUP * requests, HD)
    whole = pl.BlockSpec(shape, lambda i: (0, 0, 0))
    return pl.pallas_call(
        body,
        grid=(steps,),
        out_shape=[jax.ShapeDtypeStruct(shape, jnp.float32)] * 3 + [jax.ShapeDtypeStruct((1,), jnp.int32)],
        in_specs=[
            pl.BlockSpec(dec_q.shape, lambda i: (0, 0)),
            pl.BlockSpec((block, 2, page, width), lambda i: (i, 0, 0, 0)),
            pl.BlockSpec((requests, block), lambda i: (0, i)),
            pl.BlockSpec((requests, block), lambda i: (0, i)),
            pl.BlockSpec(rest.shape, lambda i: (0, 0)),
        ],
        out_specs=[whole] * 3 + [SM],
        compiler_params=pltpu.CompilerParams(vmem_limit_bytes=POOL_LIMIT),
        cost_estimate=pl.CostEstimate(
            flops=4 * HD * heads_kv * GROUP * requests * slots * page,
            transcendentals=heads_kv * GROUP * requests * slots * page,
            bytes_accessed=slots * 2 * page * width * 2,
        ),
        name="decode_pool",
    )(dec_q, kv_pool, full, part, rest)


def fresh_rows(piece, which, cap, cols):
    rows = piece[which, cap:, :, cols]
    return rows.reshape(rows.shape[0] * rows.shape[1], HD)


def decode_fresh(dec_q, pieces, state, full, part, rest, cap):
    page, width = pieces[0].shape[2:]
    caps = pieces[0].shape[1] - cap
    n = len(pieces)
    heads_kv = width // HD
    rows = state[0].shape[1]

    def body(*refs):
        q_ref, acc_in, m_in, l_in, full_ref, part_ref, rest_ref = refs[:7]
        piece_refs = refs[7 : 7 + n]
        acc_ref, m_ref, l_ref = refs[7 + n :]
        times = token_counts(full_ref[...], part_ref[...], rest_ref[...], page)
        for g in range(heads_kv):
            cols = slice(g * HD, (g + 1) * HD)
            key = jnp.concatenate([fresh_rows(p, 0, 0, cols) for p in piece_refs], 0)
            val = jnp.concatenate([fresh_rows(p, 1, 0, cols) for p in piece_refs], 0)
            m, l, acc = decode_fold(
                q_ref, g, key, val, times, m_in[g, :, 0:1], l_in[g, :, 0:1], acc_in[g]
            )
            m_ref[g] = jnp.broadcast_to(m, m_ref.shape[1:])
            l_ref[g] = jnp.broadcast_to(l, l_ref.shape[1:])
            acc_ref[g] = acc

    whole = lambda a: pl.BlockSpec(a.shape, lambda i: (0,) * a.ndim)
    each = pieces[0].shape[1]
    return pl.pallas_call(
        body,
        grid=(1,),
        out_shape=[jax.ShapeDtypeStruct(a.shape, a.dtype) for a in state],
        in_specs=[whole(a) for a in (dec_q, *state, full, part, rest)]
        + [pl.BlockSpec((2, caps, page, width), lambda i: (0, each // caps - 1, 0, 0))] * n,
        out_specs=[whole(a) for a in state],
        compiler_params=PARAMS,
        cost_estimate=pl.CostEstimate(
            flops=4 * HD * heads_kv * rows * n * caps * page,
            transcendentals=heads_kv * rows * n * caps * page,
            bytes_accessed=n * caps * 2 * page * width * 2,
        ),
        name="decode_fresh",
    )(dec_q, *state, full, part, rest, *pieces)


def finish(dec_q, dec_state, times, q, fresh, pages, plen, state, pieces, ks, last, cap, size):
    page, width = fresh.shape[2:]
    requests = dec_q.shape[0]
    heads_kv = width // HD
    tokens, qwidth = q.shape
    n, tail = len(pieces), len(last)
    keys = cap * page
    rows = min(128, tokens)
    held = n * keys

    def body(*refs):
        dq_ref, dacc_ref, dm_ref, dl_ref, times_ref, q_ref, f_ref, pages_ref, plen_ref = refs[:9]
        m_ref, acc_ref, l_ref = refs[9:12]
        last_refs = refs[12 : 12 + tail]
        piece_refs = refs[12 + tail : 12 + tail + n]
        (dec_ref, out_hbm, out_ref, sem, vis_ref, k_ref, v_ref, all_vis, all_k, all_v, page_ref, block_ref) = (
            refs[12 + tail + n :]
        )
        start_pages(vis_ref, k_ref, v_ref, pages_ref, plen_ref, last, cap, page, size)

        def out_copy(g):
            cols = pl.ds(pl.multiple_of(g * GROUP * HD, GROUP * HD), GROUP * HD)
            return pltpu.make_async_copy(out_ref.at[:, cols], out_hbm.at[:, cols], sem.at[g])

        def group(g, sums):
            stand_in = f_ref[0, 0, :, head_at(g)][0:1].astype(jnp.float32)
            for i in range(tail):
                place_keys(k_ref, v_ref, vis_ref, i * keys, i * keys, g, last_refs[i], stand_in, cap, page)
            partial = []

            def emit(cols, acc, total):
                total = l_ref[:, cols] + total
                out_ref[:, cols] = ((acc_ref[:, cols] + acc) * pl.reciprocal(total)).astype(out_ref.dtype)
                partial.append(jnp.sum(total.reshape(-1, 8, HD), axis=0))

            add_pages(k_ref, v_ref, q_ref, m_ref, g, emit)
            out_copy(g).start()
            return sum(partial, sums)

        sums = lax.fori_loop(0, heads_kv, group, jnp.zeros((8, HD), jnp.float32))

        times = times_ref[...]
        for g in range(heads_kv):
            cols = slice(g * HD, (g + 1) * HD)
            key = jnp.concatenate([fresh_rows(p, 0, cap, cols) for p in last_refs], 0)
            val = jnp.concatenate([fresh_rows(p, 1, cap, cols) for p in last_refs], 0)
            _, l, acc = decode_fold(
                dq_ref, g, key, val, times, dm_ref[g, :, 0:1], dl_ref[g, :, 0:1], dacc_ref[g]
            )
            done = (acc / l).astype(dec_ref.dtype)
            for h in range(GROUP):
                at = (g * GROUP + h) * HD
                dec_ref[:, at : at + HD] = done[h * requests : (h + 1) * requests]
        for g in range(heads_kv):
            out_copy(g).wait()

        @pl.when(jnp.logical_not(jnp.sum(sums) <= HUGE))
        def _():
            for i, k in enumerate(ks):
                mark_visible(all_vis, i * keys, k, cap, page, pages_ref, plen_ref, size)
            all_v[0:tokens, HD:] = jnp.ones((tokens, HD), jnp.bfloat16)
            all_v[tokens:, HD:] = all_vis[...].astype(jnp.bfloat16)
            col = lax.broadcasted_iota(jnp.int32, (rows, tokens), 1)
            row = lax.broadcasted_iota(jnp.int32, (rows, tokens), 0)

            def again(g, carry):
                all_k[0:tokens, :] = f_ref[:, 0, :, head_at(g)].reshape(tokens, HD)
                all_v[0:tokens, 0:HD] = f_ref[:, 1, :, head_at(g)].reshape(tokens, HD)
                stand_in = f_ref[0, 0, :, head_at(g)][0:1].astype(jnp.float32)
                for i in range(n):
                    pltpu.sync_copy(piece_refs[i].at[:, 0:cap], page_ref)
                    place_keys(all_k, all_v, all_vis, i * keys, tokens + i * keys, g, page_ref, stand_in, cap, page)

                def block(b, carry):
                    r = pl.multiple_of((b % (tokens // rows)) * rows, rows)
                    cols = head_at(g * GROUP + b // (tokens // rows))
                    qb = q_ref[pl.ds(r, rows), cols]
                    s = lax.dot_general(qb, all_k[...], NT, preferred_element_type=jnp.float32)
                    own = jnp.where(col <= row + r, s[:, :tokens], NEG)
                    s = jnp.concatenate([own, s[:, tokens:]], 1)
                    m = jnp.max(s, axis=1, keepdims=True)
                    p = jnp.exp2((s - m) * CEXP).astype(jnp.bfloat16)
                    new = jnp.dot(p, all_v[...], preferred_element_type=jnp.float32)
                    block_ref[...] = (new[:, :HD] / new[:, HD:]).astype(block_ref.dtype)
                    pltpu.sync_copy(block_ref, out_hbm.at[pl.ds(r, rows), cols])
                    return carry

                return lax.fori_loop(0, GROUP * (tokens // rows), block, carry)

            lax.fori_loop(0, heads_kv, again, 0)

    work = tokens * tail * keys * (qwidth // HD)
    return pl.pallas_call(
        body,
        out_shape=[
            jax.ShapeDtypeStruct(dec_q.shape, dec_q.dtype),
            jax.ShapeDtypeStruct(q.shape, q.dtype),
        ],
        in_specs=[VM] * 8 + [SM] + [VM] * (3 + tail) + [ANY] * n,
        out_specs=[VM, ANY],
        scratch_shapes=[
            pltpu.VMEM(q.shape, q.dtype),
            pltpu.SemaphoreType.DMA((heads_kv,)),
            pltpu.VMEM((tail * keys, HD), jnp.float32),
            pltpu.VMEM((tail * keys, 2 * HD), jnp.bfloat16),
            pltpu.VMEM((tail * keys, 2 * HD), jnp.bfloat16),
            pltpu.VMEM((held, HD), jnp.float32),
            pltpu.VMEM((tokens + held, HD), jnp.bfloat16),
            pltpu.VMEM((tokens + held, 2 * HD), jnp.bfloat16),
            pltpu.VMEM((2, cap, page, width), q.dtype),
            pltpu.VMEM((rows, HD), q.dtype),
        ],
        compiler_params=PARAMS,
        cost_estimate=pl.CostEstimate(
            flops=8 * HD * work, transcendentals=work, bytes_accessed=8 * work // HD
        ),
        name="finish",
    )(dec_q, *dec_state, times, q, fresh, pages, plen, *state, *[pieces[ks.index(k)] for k in last], *pieces)


def send_order(size):
    if size == 16:
        return [12, 8, 1, 2, 3, 4, 13, 5, 9, 6, 14, 7, 10, 15, 11]
    return list(range(1, size))


def shards(
    size,
    suffix_q,
    fresh_kv,
    kv_pool,
    dec_q,
    fetch_slots,
    prefix_pages,
    prefix_len,
    suffix_route,
    dec_pages,
    dec_len,
):
    page = kv_pool.shape[2]
    slots = kv_pool.shape[0]
    cap = fetch_slots.shape[1] // size
    caps = suffix_route.shape[1] // size
    sends = send_order(size)
    lead = max(1, size // 8)
    batches = [sends[:lead], sends[lead:] + [0]]
    outgoing, after = {}, []
    for ks in batches:
        outs = gather_pages(kv_pool, fresh_kv, fetch_slots, suffix_route, ks, size, after)
        after = outs[:1]
        outgoing |= dict(zip(ks, outs, strict=True))
    arrived = {0: outgoing[0]}
    for k in sends:
        pairs = [(i, i ^ k if size & (size - 1) == 0 else (i + k) % size) for i in range(size)]
        arrived[k] = lax.ppermute(outgoing[k], "pool", pairs)

    context = dec_pages.shape[1]
    position = jnp.arange(context, dtype=jnp.int32)[None, :]
    whole_pages = (position + 1) * page <= dec_len[:, None]
    edge_page = position == dec_len[:, None] // page
    rest = (dec_len % page)[:, None]

    def counts(names):
        same = dec_pages[:, :, None] == names[None, None, :]
        full = jnp.sum((same & whole_pages[:, :, None]).astype(jnp.float32), 1).astype(jnp.bfloat16)
        part = jnp.sum((same & edge_page[:, :, None]).astype(jnp.float32), 1).astype(jnp.bfloat16)
        return full, part

    groups = arrival_groups([0] + sends)
    order = [k for ks in groups for k in ks]
    early, last = order[: -len(groups[-1])], groups[-1]
    me = lax.axis_index("pool")

    def fresh_names(ks):
        srcs = source(jnp.full((len(ks),), me, jnp.int32), jnp.asarray(ks, jnp.int32), size)
        return slots + jnp.repeat(srcs, caps) * caps + jnp.tile(jnp.arange(caps, dtype=jnp.int32), len(ks))

    last_names = jnp.repeat(fresh_names(last), page)[None, None, :]
    last_token = (jnp.arange(last_names.shape[2], dtype=jnp.int32) % page)[None, None, :]
    last_seen = position[:, :, None] * page + last_token < dec_len[:, None, None]
    last_times = jnp.sum(((dec_pages[:, :, None] == last_names) & last_seen).astype(jnp.float32), 1)

    *dec_state, token = decode_pool(dec_q, kv_pool, *counts(jnp.arange(slots, dtype=jnp.int32)), rest)
    state = prefill_first(suffix_q, fresh_kv, token)
    for ks in groups[:-1]:
        new = prefill_more(
            suffix_q, fresh_kv, [arrived[k] for k in ks], ks, prefix_pages, prefix_len, state, cap, size
        )
        state = (state[0], *new)
    dec_state = decode_fresh(
        dec_q, [arrived[k] for k in early], dec_state, *counts(fresh_names(early)), rest, cap
    )
    decode_out, suffix_out = finish(
        dec_q,
        dec_state,
        last_times,
        suffix_q,
        fresh_kv,
        prefix_pages,
        prefix_len,
        state,
        [arrived[k] for k in order],
        order,
        last,
        cap,
        size,
    )
    return (suffix_out, decode_out)


def arrival_groups(order):
    size = len(order)
    if size == 16:
        return [[0, 1, 2, 3], [12, 4, 8, 5], [13, 6, 9, 7], [14, 10], [15, 11]]
    per = -(-size // 4)
    return [order[i : min(i + per, size - 1)] for i in range(0, size - 1, per)] + [order[-1:]]


def solution(mesh):
    size = mesh.shape["pool"]
    return jax.shard_map(
        functools.partial(shards, size),
        mesh=mesh,
        in_specs=(
            P(("groups", "pool"), "tp"),
            P(("groups", "pool"), None, None, "tp"),
            P(("groups", "pool"), None, None, "tp"),
            P(("groups", "pool"), "tp"),
            P(("groups", "pool"), None),
            P(("groups", "pool"), None),
            P(("groups", "pool")),
            P(("groups", "pool"), None),
            P(("groups", "pool"), None),
            P(("groups", "pool")),
        ),
        out_specs=(P(("groups", "pool"), "tp"), P(("groups", "pool"), "tp")),
        check_vma=False,
    )
```

```python
import functools

import jax
import jax.numpy as jnp
from jax import lax
from jax.experimental import pallas as pl
from jax.experimental.pallas import tpu as pltpu
from jax.sharding import PartitionSpec as P

GROUP = 8
HD = 128
LOG2E = 1.4426950408889634
CEXP = HD**-0.5 * LOG2E
NEG = -1e30
HUGE = 2.0**90
VMEM_LIMIT = 16 << 20
POOL_LIMIT = 56 << 20


NT = (((1,), (1,)), ((), ()))
VM = pl.BlockSpec(memory_space=pltpu.VMEM)
SM = pl.BlockSpec(memory_space=pltpu.SMEM)
ANY = pl.BlockSpec(memory_space=pl.ANY)
HBM = pl.BlockSpec(memory_space=pltpu.HBM)
PARAMS = pltpu.CompilerParams(vmem_limit_bytes=VMEM_LIMIT)


def head_at(i):
    return pl.ds(pl.multiple_of(i * HD, HD), HD)


def partner(i, k, size):
    return i ^ k if size & (size - 1) == 0 else lax.rem(i + k, size)


def source(i, k, size):
    return i ^ k if size & (size - 1) == 0 else lax.rem(i - k + size, size)


def gather_pages(kv_pool, fresh_kv, fetch_slots, suffix_route, ks, size, after):
    _, _, page, width = kv_pool.shape
    n = len(ks)
    cap, caps = fetch_slots.shape[1] // size, suffix_route.shape[1] // size
    each = cap + caps

    def body(slots_ref, routes_ref, pool_ref, fresh_ref, *rest):
        outs, sem = rest[-n - 1 : -1], rest[-1]
        me = lax.axis_index("pool")
        for i, k in enumerate(ks):
            dest = partner(me, k, size)
            for c in range(cap):
                pltpu.make_async_copy(
                    pool_ref.at[slots_ref[0, dest * cap + c]], outs[i].at[:, c], sem.at[i]
                ).start()
            for c in range(caps):
                pltpu.make_async_copy(
                    fresh_ref.at[routes_ref[0, dest * caps + c]], outs[i].at[:, cap + c], sem.at[i]
                ).start()
        for i in range(n):
            pltpu.make_async_copy(outs[i], outs[i], sem.at[i]).wait()

    shape = (2, each, page, width)
    return pl.pallas_call(
        body,
        out_shape=[pltpu.VMEM(shape, kv_pool.dtype)] * n,
        in_specs=[SM, SM, HBM, HBM] + [ANY] * len(after),
        out_specs=[VM] * n,
        scratch_shapes=[pltpu.SemaphoreType.DMA((n,))],
        compiler_params=pltpu.CompilerParams(vmem_limit_bytes=POOL_LIMIT),
        cost_estimate=pl.CostEstimate(
            flops=0, transcendentals=0, bytes_accessed=2 * n * each * 2 * page * width * 2
        ),
        name="gather_pages",
    )(fetch_slots, suffix_route, kv_pool, fresh_kv, *after)


def mark_visible(vis_ref, at, k, cap, page, pages_ref, plen_ref, size):
    wanted = pages_ref[...]
    keys = cap * page
    order = lax.broadcasted_iota(jnp.int32, (keys, wanted.shape[1]), 1)
    token = lax.broadcasted_iota(jnp.int32, (keys, 1), 0)
    name = source(lax.axis_index("pool"), k, size) * cap + token // page
    place = jnp.sum(jnp.where(wanted == name, order, 0), axis=1, keepdims=True)
    seen = place * page + token % page < plen_ref[0]
    vis_ref[at : at + keys, :] = jnp.broadcast_to(jnp.where(seen, 1.0, 0.0), (keys, HD))


def place_keys(k_ref, v_ref, vis_ref, vis_at, at, g, piece, stand_in, cap, page):
    keys = cap * page
    rows = slice(at, at + keys)
    seen = vis_ref[vis_at : vis_at + keys, :] > 0
    key = piece[0, 0:cap, :, head_at(g)].reshape(keys, HD).astype(jnp.float32)
    val = piece[1, 0:cap, :, head_at(g)].reshape(keys, HD).astype(jnp.float32)
    k_ref[rows, 0:HD] = jnp.where(seen, key, stand_in).astype(jnp.bfloat16)
    v_ref[rows, 0:HD] = jnp.where(seen, val, 0.0).astype(jnp.bfloat16)


def prefill_first(q, fresh, pieces, ks, pages, plen, after, cap, size):
    tokens, qwidth = q.shape
    page, width = fresh.shape[2:]
    rows = min(256, tokens)
    n = len(pieces)
    each = cap * page
    held = n * each

    def body(*refs):
        plen_ref, pages_ref, q_ref, f_ref = refs[:4]
        piece_refs = refs[4 : 4 + n]
        _, m_ref, acc_ref, l_ref, vis_ref, k_ref, v_ref = refs[4 + n :]
        for i, k in enumerate(ks):
            mark_visible(vis_ref, i * each, k, cap, page, pages_ref, plen_ref, size)
        v_ref[0:held, HD:] = vis_ref[...].astype(jnp.bfloat16)
        v_ref[held:, HD:] = jnp.ones((tokens, HD), jnp.bfloat16)
        k_lane = lax.broadcasted_iota(jnp.int32, (held + tokens, HD), 1)
        k_ref[:, HD:] = jnp.where(k_lane == 0, -1.0, 0.0).astype(jnp.bfloat16)
        row = lax.broadcasted_iota(jnp.int32, (rows, rows), 0)
        col = lax.broadcasted_iota(jnp.int32, (rows, rows), 1)
        lane = lax.broadcasted_iota(jnp.int32, (tokens, HD), 1)

        def group(g, carry):
            key = f_ref[:, 0, :, head_at(g)].reshape(tokens, HD)
            k_ref[held:, 0:HD] = key
            v_ref[held:, 0:HD] = f_ref[:, 1, :, head_at(g)].reshape(tokens, HD)
            key = key.astype(jnp.float32)
            for i in range(n):
                at = i * each
                place_keys(k_ref, v_ref, vis_ref, at, at, g, piece_refs[i], key[0:1], cap, page)
            for h in range(GROUP):
                cols = head_at(g * GROUP + h)
                own = jnp.sum(q_ref[:, cols].astype(jnp.float32) * key, axis=1, keepdims=True)
                m_ref[:, cols] = jnp.where(lane == 0, own, 0.0).astype(jnp.bfloat16)
            for h in range(GROUP):
                cols = head_at(g * GROUP + h)
                for r in range(0, tokens, rows):
                    rs = slice(r, r + rows)
                    shown = held + r + rows
                    lhs = jnp.concatenate([q_ref[rs, cols], m_ref[rs, cols]], 1)
                    s = lax.dot_general(lhs, k_ref[0:shown, :], NT, preferred_element_type=jnp.float32)
                    diag = jnp.where(col <= row, s[:, held + r :], NEG)
                    s = jnp.concatenate([s[:, : held + r], diag], 1)
                    p = jnp.exp2(s * CEXP).astype(jnp.bfloat16)
                    new = jnp.dot(p, v_ref[0:shown, :], preferred_element_type=jnp.float32)
                    acc_ref[rs, cols] = new[:, :HD]
                    l_ref[rs, cols] = new[:, HD:]
            return carry

        lax.fori_loop(0, width // HD, group, 0)

    wide = pltpu.VMEM((tokens, qwidth), jnp.float32)
    work = tokens * (tokens // 2 + held) * (qwidth // HD)
    return pl.pallas_call(
        body,
        out_shape=[pltpu.VMEM((tokens, qwidth), jnp.bfloat16), wide, wide],
        in_specs=[SM, VM, VM, VM] + [VM] * n + [SM],
        out_specs=[VM] * 3,
        scratch_shapes=[
            pltpu.VMEM((held, HD), jnp.float32),
            pltpu.VMEM((held + tokens, 2 * HD), jnp.bfloat16),
            pltpu.VMEM((held + tokens, 2 * HD), jnp.bfloat16),
        ],
        compiler_params=PARAMS,
        cost_estimate=pl.CostEstimate(flops=8 * HD * work, transcendentals=work, bytes_accessed=8 * work // HD),
        name="prefill_first",
    )(plen, pages, q, fresh, *pieces, after)


def add_pages(k_ref, v_ref, q_ref, m_ref, g, emit):
    for h in range(GROUP):
        cols = head_at(g * GROUP + h)
        lhs = jnp.concatenate([q_ref[:, cols], m_ref[:, cols]], 1)
        s = lax.dot_general(lhs, k_ref[...], NT, preferred_element_type=jnp.float32)
        p = jnp.exp2(s * CEXP).astype(jnp.bfloat16)
        new = jnp.dot(p, v_ref[...], preferred_element_type=jnp.float32)
        emit(cols, new[:, :HD], new[:, HD:])


def start_pages(vis_ref, k_ref, v_ref, pages_ref, plen_ref, ks, cap, page, size):
    keys = k_ref.shape[0]
    for i, k in enumerate(ks):
        mark_visible(vis_ref, i * cap * page, k, cap, page, pages_ref, plen_ref, size)
    lane = lax.broadcasted_iota(jnp.int32, (keys, HD), 1)
    k_ref[:, HD:] = jnp.where(lane == 0, -1.0, 0.0).astype(jnp.bfloat16)
    v_ref[:, HD:] = vis_ref[...].astype(jnp.bfloat16)


def prefill_more(q, fresh, pieces, ks, pages, plen, state, cap, size):
    tokens, qwidth = q.shape
    page, width = fresh.shape[2:]
    n = len(pieces)
    keys = n * cap * page

    def body(*refs):
        plen_ref, pages_ref, q_ref, f_ref = refs[:4]
        piece_refs = refs[4 : 4 + n]
        m_ref, acc_in, l_in, acc_ref, l_ref, vis_ref, k_ref, v_ref = refs[4 + n :]
        start_pages(vis_ref, k_ref, v_ref, pages_ref, plen_ref, ks, cap, page, size)

        def group(g, carry):
            stand_in = f_ref[0, 0, :, head_at(g)][0:1].astype(jnp.float32)
            for i in range(n):
                at = i * cap * page
                place_keys(k_ref, v_ref, vis_ref, at, at, g, piece_refs[i], stand_in, cap, page)

            def emit(cols, acc, total):
                acc_ref[:, cols] = acc_in[:, cols] + acc
                l_ref[:, cols] = l_in[:, cols] + total

            add_pages(k_ref, v_ref, q_ref, m_ref, g, emit)
            return carry

        lax.fori_loop(0, width // HD, group, 0)

    work = tokens * keys * (qwidth // HD)
    wide = pltpu.VMEM((tokens, qwidth), jnp.float32)
    return pl.pallas_call(
        body,
        out_shape=[wide, wide],
        in_specs=[SM, VM, VM, VM] + [VM] * n + [VM] * 3,
        out_specs=[VM, VM],
        input_output_aliases={5 + n: 0, 6 + n: 1},
        scratch_shapes=[
            pltpu.VMEM((keys, HD), jnp.float32),
            pltpu.VMEM((keys, 2 * HD), jnp.bfloat16),
            pltpu.VMEM((keys, 2 * HD), jnp.bfloat16),
        ],
        compiler_params=PARAMS,
        cost_estimate=pl.CostEstimate(
            flops=8 * HD * work, transcendentals=work, bytes_accessed=8 * work // HD
        ),
        name="prefill_more",
    )(plen, pages, q, fresh, *pieces, *state)


def token_counts(full, part, rest, page):
    pages = full.shape[1]
    key = lax.broadcasted_iota(jnp.int32, (pages, pages * page), 1) // page
    row = lax.broadcasted_iota(jnp.int32, (pages, pages * page), 0)
    spread = jnp.where(key == row, 1.0, 0.0).astype(jnp.bfloat16)
    times = jnp.dot(full, spread, preferred_element_type=jnp.float32)
    edge = jnp.dot(part, spread, preferred_element_type=jnp.float32)
    token = lax.broadcasted_iota(jnp.int32, times.shape, 1) % page
    return times + jnp.where(token < rest, edge, 0.0)


def decode_fold(q_ref, g, key, val, times, m_old, l_old, acc_old):
    requests = times.shape[0]
    q = jnp.concatenate(
        [q_ref[:, (g * GROUP + h) * HD : (g * GROUP + h + 1) * HD] for h in range(GROUP)], 0
    )
    s = lax.dot_general(q, key, NT, preferred_element_type=jnp.float32)
    keys = s.shape[1]
    s = s.reshape(GROUP, requests, keys)
    s = jnp.where((times > 0)[None], s, NEG).reshape(GROUP * requests, keys)
    m = jnp.maximum(jnp.max(s, axis=1, keepdims=True), m_old)
    p = jnp.exp2((s - m) * CEXP).reshape(GROUP, requests, keys) * times[None]
    p = p.reshape(GROUP * requests, keys)
    total = jnp.sum(p, axis=1, keepdims=True)
    new = jnp.dot(p.astype(jnp.bfloat16), val, preferred_element_type=jnp.float32)
    alpha = jnp.exp2((m_old - m) * CEXP)
    return m, l_old * alpha + total, acc_old * alpha + new


def decode_pool(dec_q, kv_pool, full, part, rest):
    slots, _, page, width = kv_pool.shape
    requests = dec_q.shape[0]
    heads_kv = width // HD
    block = 128 if slots % 128 == 0 else slots
    steps = slots // block

    def body(q_ref, kv_ref, full_ref, part_ref, rest_ref, acc_ref, m_ref, l_ref, token_ref):
        token_ref[0] = 0

        @pl.when(pl.program_id(0) == 0)
        def _():
            acc_ref[...] = jnp.zeros_like(acc_ref)
            m_ref[...] = jnp.full_like(m_ref, NEG)
            l_ref[...] = jnp.zeros_like(l_ref)

        times = token_counts(full_ref[...], part_ref[...], rest_ref[...], page)
        for g in range(heads_kv):
            cols = slice(g * HD, (g + 1) * HD)
            key = kv_ref[:, 0, :, cols].reshape(block * page, HD)
            val = kv_ref[:, 1, :, cols].reshape(block * page, HD)
            m, l, acc = decode_fold(
                q_ref, g, key, val, times, m_ref[g, :, 0:1], l_ref[g, :, 0:1], acc_ref[g]
            )
            m_ref[g] = jnp.broadcast_to(m, m_ref.shape[1:])
            l_ref[g] = jnp.broadcast_to(l, l_ref.shape[1:])
            acc_ref[g] = acc

    shape = (heads_kv, GROUP * requests, HD)
    whole = pl.BlockSpec(shape, lambda i: (0, 0, 0))
    return pl.pallas_call(
        body,
        grid=(steps,),
        out_shape=[jax.ShapeDtypeStruct(shape, jnp.float32)] * 3 + [jax.ShapeDtypeStruct((1,), jnp.int32)],
        in_specs=[
            pl.BlockSpec(dec_q.shape, lambda i: (0, 0)),
            pl.BlockSpec((block, 2, page, width), lambda i: (i, 0, 0, 0)),
            pl.BlockSpec((requests, block), lambda i: (0, i)),
            pl.BlockSpec((requests, block), lambda i: (0, i)),
            pl.BlockSpec(rest.shape, lambda i: (0, 0)),
        ],
        out_specs=[whole] * 3 + [SM],
        compiler_params=pltpu.CompilerParams(vmem_limit_bytes=POOL_LIMIT),
        cost_estimate=pl.CostEstimate(
            flops=4 * HD * heads_kv * GROUP * requests * slots * page,
            transcendentals=heads_kv * GROUP * requests * slots * page,
            bytes_accessed=slots * 2 * page * width * 2,
        ),
        name="decode_pool",
    )(dec_q, kv_pool, full, part, rest)


def fresh_rows(piece, which, cap, cols):
    rows = piece[which, cap:, :, cols]
    return rows.reshape(rows.shape[0] * rows.shape[1], HD)


def decode_fresh(dec_q, pieces, state, full, part, rest, cap):
    page, width = pieces[0].shape[2:]
    caps = pieces[0].shape[1] - cap
    n = len(pieces)
    heads_kv = width // HD
    rows = state[0].shape[1]

    def body(*refs):
        q_ref, acc_in, m_in, l_in, full_ref, part_ref, rest_ref = refs[:7]
        piece_refs = refs[7 : 7 + n]
        acc_ref, m_ref, l_ref = refs[7 + n :]
        times = token_counts(full_ref[...], part_ref[...], rest_ref[...], page)
        for g in range(heads_kv):
            cols = slice(g * HD, (g + 1) * HD)
            key = jnp.concatenate([fresh_rows(p, 0, 0, cols) for p in piece_refs], 0)
            val = jnp.concatenate([fresh_rows(p, 1, 0, cols) for p in piece_refs], 0)
            m, l, acc = decode_fold(
                q_ref, g, key, val, times, m_in[g, :, 0:1], l_in[g, :, 0:1], acc_in[g]
            )
            m_ref[g] = jnp.broadcast_to(m, m_ref.shape[1:])
            l_ref[g] = jnp.broadcast_to(l, l_ref.shape[1:])
            acc_ref[g] = acc

    whole = lambda a: pl.BlockSpec(a.shape, lambda i: (0,) * a.ndim)
    each = pieces[0].shape[1]
    return pl.pallas_call(
        body,
        grid=(1,),
        out_shape=[jax.ShapeDtypeStruct(a.shape, a.dtype) for a in state],
        in_specs=[whole(a) for a in (dec_q, *state, full, part, rest)]
        + [pl.BlockSpec((2, caps, page, width), lambda i: (0, each // caps - 1, 0, 0))] * n,
        out_specs=[whole(a) for a in state],
        compiler_params=PARAMS,
        cost_estimate=pl.CostEstimate(
            flops=4 * HD * heads_kv * rows * n * caps * page,
            transcendentals=heads_kv * rows * n * caps * page,
            bytes_accessed=n * caps * 2 * page * width * 2,
        ),
        name="decode_fresh",
    )(dec_q, *state, full, part, rest, *pieces)


def finish(dec_q, dec_state, times, q, fresh, pages, plen, state, pieces, ks, last, cap, size):
    page, width = fresh.shape[2:]
    requests = dec_q.shape[0]
    heads_kv = width // HD
    tokens, qwidth = q.shape
    n, tail = len(pieces), len(last)
    keys = cap * page
    rows = min(128, tokens)
    held = n * keys

    def body(*refs):
        dq_ref, dacc_ref, dm_ref, dl_ref, times_ref, q_ref, f_ref, pages_ref, plen_ref = refs[:9]
        m_ref, acc_ref, l_ref = refs[9:12]
        last_refs = refs[12 : 12 + tail]
        piece_refs = refs[12 + tail : 12 + tail + n]
        (dec_ref, out_hbm, out_ref, sem, vis_ref, k_ref, v_ref, all_vis, all_k, all_v, page_ref, block_ref) = (
            refs[12 + tail + n :]
        )
        start_pages(vis_ref, k_ref, v_ref, pages_ref, plen_ref, last, cap, page, size)

        def out_copy(g):
            cols = pl.ds(pl.multiple_of(g * GROUP * HD, GROUP * HD), GROUP * HD)
            return pltpu.make_async_copy(out_ref.at[:, cols], out_hbm.at[:, cols], sem.at[g])

        def group(g, sums):
            stand_in = f_ref[0, 0, :, head_at(g)][0:1].astype(jnp.float32)
            for i in range(tail):
                place_keys(k_ref, v_ref, vis_ref, i * keys, i * keys, g, last_refs[i], stand_in, cap, page)
            partial = []

            def emit(cols, acc, total):
                total = l_ref[:, cols] + total
                out_ref[:, cols] = ((acc_ref[:, cols] + acc) * pl.reciprocal(total)).astype(out_ref.dtype)
                partial.append(jnp.sum(total.reshape(-1, 8, HD), axis=0))

            add_pages(k_ref, v_ref, q_ref, m_ref, g, emit)
            out_copy(g).start()
            return sum(partial, sums)

        sums = lax.fori_loop(0, heads_kv, group, jnp.zeros((8, HD), jnp.float32))

        times = times_ref[...]
        for g in range(heads_kv):
            cols = slice(g * HD, (g + 1) * HD)
            key = jnp.concatenate([fresh_rows(p, 0, cap, cols) for p in last_refs], 0)
            val = jnp.concatenate([fresh_rows(p, 1, cap, cols) for p in last_refs], 0)
            _, l, acc = decode_fold(
                dq_ref, g, key, val, times, dm_ref[g, :, 0:1], dl_ref[g, :, 0:1], dacc_ref[g]
            )
            done = (acc / l).astype(dec_ref.dtype)
            for h in range(GROUP):
                at = (g * GROUP + h) * HD
                dec_ref[:, at : at + HD] = done[h * requests : (h + 1) * requests]
        for g in range(heads_kv):
            out_copy(g).wait()

        @pl.when(jnp.logical_not(jnp.sum(sums) <= HUGE))
        def _():
            for i, k in enumerate(ks):
                mark_visible(all_vis, i * keys, k, cap, page, pages_ref, plen_ref, size)
            all_v[0:tokens, HD:] = jnp.ones((tokens, HD), jnp.bfloat16)
            all_v[tokens:, HD:] = all_vis[...].astype(jnp.bfloat16)
            col = lax.broadcasted_iota(jnp.int32, (rows, tokens), 1)
            row = lax.broadcasted_iota(jnp.int32, (rows, tokens), 0)

            def again(g, carry):
                all_k[0:tokens, :] = f_ref[:, 0, :, head_at(g)].reshape(tokens, HD)
                all_v[0:tokens, 0:HD] = f_ref[:, 1, :, head_at(g)].reshape(tokens, HD)
                stand_in = f_ref[0, 0, :, head_at(g)][0:1].astype(jnp.float32)
                for i in range(n):
                    pltpu.sync_copy(piece_refs[i].at[:, 0:cap], page_ref)
                    place_keys(all_k, all_v, all_vis, i * keys, tokens + i * keys, g, page_ref, stand_in, cap, page)

                def block(b, carry):
                    r = pl.multiple_of((b % (tokens // rows)) * rows, rows)
                    cols = head_at(g * GROUP + b // (tokens // rows))
                    qb = q_ref[pl.ds(r, rows), cols]
                    s = lax.dot_general(qb, all_k[...], NT, preferred_element_type=jnp.float32)
                    own = jnp.where(col <= row + r, s[:, :tokens], NEG)
                    s = jnp.concatenate([own, s[:, tokens:]], 1)
                    m = jnp.max(s, axis=1, keepdims=True)
                    p = jnp.exp2((s - m) * CEXP).astype(jnp.bfloat16)
                    new = jnp.dot(p, all_v[...], preferred_element_type=jnp.float32)
                    block_ref[...] = (new[:, :HD] / new[:, HD:]).astype(block_ref.dtype)
                    pltpu.sync_copy(block_ref, out_hbm.at[pl.ds(r, rows), cols])
                    return carry

                return lax.fori_loop(0, GROUP * (tokens // rows), block, carry)

            lax.fori_loop(0, heads_kv, again, 0)

    work = tokens * tail * keys * (qwidth // HD)
    return pl.pallas_call(
        body,
        out_shape=[
            jax.ShapeDtypeStruct(dec_q.shape, dec_q.dtype),
            jax.ShapeDtypeStruct(q.shape, q.dtype),
        ],
        in_specs=[VM] * 8 + [SM] + [VM] * (3 + tail) + [ANY] * n,
        out_specs=[VM, ANY],
        scratch_shapes=[
            pltpu.VMEM(q.shape, q.dtype),
            pltpu.SemaphoreType.DMA((heads_kv,)),
            pltpu.VMEM((tail * keys, HD), jnp.float32),
            pltpu.VMEM((tail * keys, 2 * HD), jnp.bfloat16),
            pltpu.VMEM((tail * keys, 2 * HD), jnp.bfloat16),
            pltpu.VMEM((held, HD), jnp.float32),
            pltpu.VMEM((tokens + held, HD), jnp.bfloat16),
            pltpu.VMEM((tokens + held, 2 * HD), jnp.bfloat16),
            pltpu.VMEM((2, cap, page, width), q.dtype),
            pltpu.VMEM((rows, HD), q.dtype),
        ],
        compiler_params=PARAMS,
        cost_estimate=pl.CostEstimate(
            flops=8 * HD * work, transcendentals=work, bytes_accessed=8 * work // HD
        ),
        name="finish",
    )(dec_q, *dec_state, times, q, fresh, pages, plen, *state, *[pieces[ks.index(k)] for k in last], *pieces)


def send_order(size):
    if size == 16:
        return [12, 8, 1, 2, 3, 4, 13, 5, 9, 6, 14, 7, 10, 15, 11]
    return list(range(1, size))


def shards(
    size,
    suffix_q,
    fresh_kv,
    kv_pool,
    dec_q,
    fetch_slots,
    prefix_pages,
    prefix_len,
    suffix_route,
    dec_pages,
    dec_len,
):
    page = kv_pool.shape[2]
    slots = kv_pool.shape[0]
    cap = fetch_slots.shape[1] // size
    caps = suffix_route.shape[1] // size
    sends = send_order(size)
    lead = max(1, size // 8)
    batches = [sends[:lead], sends[lead:] + [0]]
    outgoing, after = {}, []
    for ks in batches:
        outs = gather_pages(kv_pool, fresh_kv, fetch_slots, suffix_route, ks, size, after)
        after = outs[:1]
        outgoing |= dict(zip(ks, outs, strict=True))
    arrived = {0: outgoing[0]}
    for k in sends:
        pairs = [(i, i ^ k if size & (size - 1) == 0 else (i + k) % size) for i in range(size)]
        arrived[k] = lax.ppermute(outgoing[k], "pool", pairs)

    context = dec_pages.shape[1]
    position = jnp.arange(context, dtype=jnp.int32)[None, :]
    whole_pages = (position + 1) * page <= dec_len[:, None]
    edge_page = position == dec_len[:, None] // page
    rest = (dec_len % page)[:, None]

    def counts(names):
        same = dec_pages[:, :, None] == names[None, None, :]
        full = jnp.sum((same & whole_pages[:, :, None]).astype(jnp.float32), 1).astype(jnp.bfloat16)
        part = jnp.sum((same & edge_page[:, :, None]).astype(jnp.float32), 1).astype(jnp.bfloat16)
        return full, part

    groups = arrival_groups([0] + sends)
    order = [k for ks in groups for k in ks]
    early, last = order[: -len(groups[-1])], groups[-1]
    me = lax.axis_index("pool")

    def fresh_names(ks):
        srcs = source(jnp.full((len(ks),), me, jnp.int32), jnp.asarray(ks, jnp.int32), size)
        return slots + jnp.repeat(srcs, caps) * caps + jnp.tile(jnp.arange(caps, dtype=jnp.int32), len(ks))

    last_names = jnp.repeat(fresh_names(last), page)[None, None, :]
    last_token = (jnp.arange(last_names.shape[2], dtype=jnp.int32) % page)[None, None, :]
    last_seen = position[:, :, None] * page + last_token < dec_len[:, None, None]
    last_times = jnp.sum(((dec_pages[:, :, None] == last_names) & last_seen).astype(jnp.float32), 1)

    *dec_state, token = decode_pool(dec_q, kv_pool, *counts(jnp.arange(slots, dtype=jnp.int32)), rest)
    state = prefill_first(
        suffix_q,
        fresh_kv,
        [arrived[k] for k in groups[0]],
        groups[0],
        prefix_pages,
        prefix_len,
        token,
        cap,
        size,
    )
    for ks in groups[1:-1]:
        new = prefill_more(
            suffix_q, fresh_kv, [arrived[k] for k in ks], ks, prefix_pages, prefix_len, state, cap, size
        )
        state = (state[0], *new)
    dec_state = decode_fresh(
        dec_q, [arrived[k] for k in early], dec_state, *counts(fresh_names(early)), rest, cap
    )
    decode_out, suffix_out = finish(
        dec_q,
        dec_state,
        last_times,
        suffix_q,
        fresh_kv,
        prefix_pages,
        prefix_len,
        state,
        [arrived[k] for k in order],
        order,
        last,
        cap,
        size,
    )
    return (suffix_out, decode_out)


def arrival_groups(order):
    size = len(order)
    if size == 16:
        return [[0, 1, 2, 3, 12, 4, 8, 5], [13, 6, 9, 7], [14, 10], [15, 11]]
    per = -(-size // 4)
    return [order[i : min(i + per, size - 1)] for i in range(0, size - 1, per)] + [order[-1:]]


def solution(mesh):
    size = mesh.shape["pool"]
    return jax.shard_map(
        functools.partial(shards, size),
        mesh=mesh,
        in_specs=(
            P(("groups", "pool"), "tp"),
            P(("groups", "pool"), None, None, "tp"),
            P(("groups", "pool"), None, None, "tp"),
            P(("groups", "pool"), "tp"),
            P(("groups", "pool"), None),
            P(("groups", "pool"), None),
            P(("groups", "pool")),
            P(("groups", "pool"), None),
            P(("groups", "pool"), None),
            P(("groups", "pool")),
        ),
        out_specs=(P(("groups", "pool"), "tp"), P(("groups", "pool"), "tp")),
        check_vma=False,
    )
```

```python
import functools

import jax
import jax.numpy as jnp
from jax import lax
from jax.experimental import pallas as pl
from jax.experimental.pallas import tpu as pltpu
from jax.sharding import PartitionSpec as P

GROUP = 8
HD = 128
LOG2E = 1.4426950408889634
CEXP = HD**-0.5 * LOG2E
NEG = -1e30
HUGE = 2.0**90
VMEM_LIMIT = 16 << 20
POOL_LIMIT = 56 << 20
FIRST_LIMIT = 22 << 20


NT = (((1,), (1,)), ((), ()))
VM = pl.BlockSpec(memory_space=pltpu.VMEM)
SM = pl.BlockSpec(memory_space=pltpu.SMEM)
ANY = pl.BlockSpec(memory_space=pl.ANY)
HBM = pl.BlockSpec(memory_space=pltpu.HBM)
PARAMS = pltpu.CompilerParams(vmem_limit_bytes=VMEM_LIMIT)


def head_at(i):
    return pl.ds(pl.multiple_of(i * HD, HD), HD)


def partner(i, k, size):
    return i ^ k if size & (size - 1) == 0 else lax.rem(i + k, size)


def source(i, k, size):
    return i ^ k if size & (size - 1) == 0 else lax.rem(i - k + size, size)


def gather_pages(kv_pool, fresh_kv, fetch_slots, suffix_route, ks, size, after):
    _, _, page, width = kv_pool.shape
    n = len(ks)
    cap, caps = fetch_slots.shape[1] // size, suffix_route.shape[1] // size
    each = cap + caps

    def body(slots_ref, routes_ref, pool_ref, fresh_ref, *rest):
        outs, sem = rest[-n - 1 : -1], rest[-1]
        me = lax.axis_index("pool")
        for i, k in enumerate(ks):
            dest = partner(me, k, size)
            for c in range(cap):
                pltpu.make_async_copy(
                    pool_ref.at[slots_ref[0, dest * cap + c]], outs[i].at[:, c], sem.at[i]
                ).start()
            for c in range(caps):
                pltpu.make_async_copy(
                    fresh_ref.at[routes_ref[0, dest * caps + c]], outs[i].at[:, cap + c], sem.at[i]
                ).start()
        for i in range(n):
            pltpu.make_async_copy(outs[i], outs[i], sem.at[i]).wait()

    shape = (2, each, page, width)
    return pl.pallas_call(
        body,
        out_shape=[pltpu.VMEM(shape, kv_pool.dtype)] * n,
        in_specs=[SM, SM, HBM, HBM] + [ANY] * len(after),
        out_specs=[VM] * n,
        scratch_shapes=[pltpu.SemaphoreType.DMA((n,))],
        compiler_params=pltpu.CompilerParams(vmem_limit_bytes=POOL_LIMIT),
        cost_estimate=pl.CostEstimate(
            flops=0, transcendentals=0, bytes_accessed=2 * n * each * 2 * page * width * 2
        ),
        name="gather_pages",
    )(fetch_slots, suffix_route, kv_pool, fresh_kv, *after)


def mark_visible(vis_ref, at, k, cap, page, pages_ref, plen_ref, size):
    wanted = pages_ref[...]
    keys = cap * page
    order = lax.broadcasted_iota(jnp.int32, (keys, wanted.shape[1]), 1)
    token = lax.broadcasted_iota(jnp.int32, (keys, 1), 0)
    name = source(lax.axis_index("pool"), k, size) * cap + token // page
    place = jnp.sum(jnp.where(wanted == name, order, 0), axis=1, keepdims=True)
    seen = place * page + token % page < plen_ref[0]
    vis_ref[at : at + keys, :] = jnp.broadcast_to(jnp.where(seen, 1.0, 0.0), (keys, HD))


def place_keys(k_ref, v_ref, vis_ref, vis_at, at, g, piece, stand_in, cap, page):
    keys = cap * page
    rows = slice(at, at + keys)
    seen = vis_ref[vis_at : vis_at + keys, :] > 0
    key = piece[0, 0:cap, :, head_at(g)].reshape(keys, HD).astype(jnp.float32)
    val = piece[1, 0:cap, :, head_at(g)].reshape(keys, HD).astype(jnp.float32)
    k_ref[rows, 0:HD] = jnp.where(seen, key, stand_in).astype(jnp.bfloat16)
    v_ref[rows, 0:HD] = jnp.where(seen, val, 0.0).astype(jnp.bfloat16)


def fetch_pages(piece_refs, held, sem, cap):
    copies = [
        pltpu.make_async_copy(ref.at[:, 0:cap], held.at[i], sem.at[i]) for i, ref in enumerate(piece_refs)
    ]
    for copy in copies:
        copy.start()
    return copies


def prefill_first(q, fresh, pieces, ks, pages, plen, after, cap, size):
    tokens, qwidth = q.shape
    page, width = fresh.shape[2:]
    rows = min(256, tokens)
    n = len(pieces)
    each = cap * page
    held = n * each

    def body(*refs):
        plen_ref, pages_ref, q_ref, f_ref = refs[:4]
        piece_refs = refs[4 : 4 + n]
        _, m_ref, acc_ref, l_ref, got_ref, sem, vis_ref, k_ref, v_ref = refs[4 + n :]
        copies = fetch_pages(piece_refs, got_ref, sem, cap)
        for i, k in enumerate(ks):
            mark_visible(vis_ref, i * each, k, cap, page, pages_ref, plen_ref, size)
        v_ref[0:held, HD:] = vis_ref[...].astype(jnp.bfloat16)
        v_ref[held:, HD:] = jnp.ones((tokens, HD), jnp.bfloat16)
        k_lane = lax.broadcasted_iota(jnp.int32, (held + tokens, HD), 1)
        k_ref[:, HD:] = jnp.where(k_lane == 0, -1.0, 0.0).astype(jnp.bfloat16)
        row = lax.broadcasted_iota(jnp.int32, (rows, rows), 0)
        col = lax.broadcasted_iota(jnp.int32, (rows, rows), 1)
        lane = lax.broadcasted_iota(jnp.int32, (tokens, HD), 1)
        for copy in copies:
            copy.wait()

        def group(g, carry):
            key = f_ref[:, 0, :, head_at(g)].reshape(tokens, HD)
            k_ref[held:, 0:HD] = key
            v_ref[held:, 0:HD] = f_ref[:, 1, :, head_at(g)].reshape(tokens, HD)
            key = key.astype(jnp.float32)
            for i in range(n):
                at = i * each
                place_keys(k_ref, v_ref, vis_ref, at, at, g, got_ref.at[i], key[0:1], cap, page)
            for h in range(GROUP):
                cols = head_at(g * GROUP + h)
                own = jnp.sum(q_ref[:, cols].astype(jnp.float32) * key, axis=1, keepdims=True)
                m_ref[:, cols] = jnp.where(lane == 0, own, 0.0).astype(jnp.bfloat16)
            for h in range(GROUP):
                cols = head_at(g * GROUP + h)
                for r in range(0, tokens, rows):
                    rs = slice(r, r + rows)
                    shown = held + r + rows
                    lhs = jnp.concatenate([q_ref[rs, cols], m_ref[rs, cols]], 1)
                    s = lax.dot_general(lhs, k_ref[0:shown, :], NT, preferred_element_type=jnp.float32)
                    diag = jnp.where(col <= row, s[:, held + r :], NEG)
                    s = jnp.concatenate([s[:, : held + r], diag], 1)
                    p = jnp.exp2(s * CEXP).astype(jnp.bfloat16)
                    new = jnp.dot(p, v_ref[0:shown, :], preferred_element_type=jnp.float32)
                    acc_ref[rs, cols] = new[:, :HD]
                    l_ref[rs, cols] = new[:, HD:]
            return carry

        lax.fori_loop(0, width // HD, group, 0)

    wide = pltpu.VMEM((tokens, qwidth), jnp.float32)
    work = tokens * (tokens // 2 + held) * (qwidth // HD)
    return pl.pallas_call(
        body,
        out_shape=[pltpu.VMEM((tokens, qwidth), jnp.bfloat16), wide, wide],
        in_specs=[SM, VM, VM, VM] + [ANY] * n + [SM],
        out_specs=[VM] * 3,
        scratch_shapes=[
            pltpu.VMEM((n, 2, cap, page, width), q.dtype),
            pltpu.SemaphoreType.DMA((n,)),
            pltpu.VMEM((held, HD), jnp.float32),
            pltpu.VMEM((held + tokens, 2 * HD), jnp.bfloat16),
            pltpu.VMEM((held + tokens, 2 * HD), jnp.bfloat16),
        ],
        compiler_params=pltpu.CompilerParams(vmem_limit_bytes=FIRST_LIMIT),
        cost_estimate=pl.CostEstimate(flops=8 * HD * work, transcendentals=work, bytes_accessed=8 * work // HD),
        name="prefill_first",
    )(plen, pages, q, fresh, *pieces, after)


def add_pages(k_ref, v_ref, q_ref, m_ref, g, emit):
    for h in range(GROUP):
        cols = head_at(g * GROUP + h)
        lhs = jnp.concatenate([q_ref[:, cols], m_ref[:, cols]], 1)
        s = lax.dot_general(lhs, k_ref[...], NT, preferred_element_type=jnp.float32)
        p = jnp.exp2(s * CEXP).astype(jnp.bfloat16)
        new = jnp.dot(p, v_ref[...], preferred_element_type=jnp.float32)
        emit(cols, new[:, :HD], new[:, HD:])


def start_pages(vis_ref, k_ref, v_ref, pages_ref, plen_ref, ks, cap, page, size):
    keys = k_ref.shape[0]
    for i, k in enumerate(ks):
        mark_visible(vis_ref, i * cap * page, k, cap, page, pages_ref, plen_ref, size)
    lane = lax.broadcasted_iota(jnp.int32, (keys, HD), 1)
    k_ref[:, HD:] = jnp.where(lane == 0, -1.0, 0.0).astype(jnp.bfloat16)
    v_ref[:, HD:] = vis_ref[...].astype(jnp.bfloat16)


def prefill_more(q, fresh, pieces, ks, pages, plen, state, cap, size):
    tokens, qwidth = q.shape
    page, width = fresh.shape[2:]
    n = len(pieces)
    keys = n * cap * page

    def body(*refs):
        plen_ref, pages_ref, q_ref, f_ref = refs[:4]
        piece_refs = refs[4 : 4 + n]
        m_ref, acc_in, l_in, acc_ref, l_ref, got_ref, sem, vis_ref, k_ref, v_ref = refs[4 + n :]
        copies = fetch_pages(piece_refs, got_ref, sem, cap)
        start_pages(vis_ref, k_ref, v_ref, pages_ref, plen_ref, ks, cap, page, size)
        for copy in copies:
            copy.wait()

        def group(g, carry):
            stand_in = f_ref[0, 0, :, head_at(g)][0:1].astype(jnp.float32)
            for i in range(n):
                at = i * cap * page
                place_keys(k_ref, v_ref, vis_ref, at, at, g, got_ref.at[i], stand_in, cap, page)

            def emit(cols, acc, total):
                acc_ref[:, cols] = acc_in[:, cols] + acc
                l_ref[:, cols] = l_in[:, cols] + total

            add_pages(k_ref, v_ref, q_ref, m_ref, g, emit)
            return carry

        lax.fori_loop(0, width // HD, group, 0)

    work = tokens * keys * (qwidth // HD)
    wide = pltpu.VMEM((tokens, qwidth), jnp.float32)
    return pl.pallas_call(
        body,
        out_shape=[wide, wide],
        in_specs=[SM, VM, VM, VM] + [ANY] * n + [VM] * 3,
        out_specs=[VM, VM],
        input_output_aliases={5 + n: 0, 6 + n: 1},
        scratch_shapes=[
            pltpu.VMEM((n, 2, cap, page, width), q.dtype),
            pltpu.SemaphoreType.DMA((n,)),
            pltpu.VMEM((keys, HD), jnp.float32),
            pltpu.VMEM((keys, 2 * HD), jnp.bfloat16),
            pltpu.VMEM((keys, 2 * HD), jnp.bfloat16),
        ],
        compiler_params=PARAMS,
        cost_estimate=pl.CostEstimate(
            flops=8 * HD * work, transcendentals=work, bytes_accessed=8 * work // HD
        ),
        name="prefill_more",
    )(plen, pages, q, fresh, *pieces, *state)


def token_counts(full, part, rest, page):
    pages = full.shape[1]
    key = lax.broadcasted_iota(jnp.int32, (pages, pages * page), 1) // page
    row = lax.broadcasted_iota(jnp.int32, (pages, pages * page), 0)
    spread = jnp.where(key == row, 1.0, 0.0).astype(jnp.bfloat16)
    times = jnp.dot(full, spread, preferred_element_type=jnp.float32)
    edge = jnp.dot(part, spread, preferred_element_type=jnp.float32)
    token = lax.broadcasted_iota(jnp.int32, times.shape, 1) % page
    return times + jnp.where(token < rest, edge, 0.0)


def decode_fold(q_ref, g, key, val, times, m_old, l_old, acc_old):
    requests = times.shape[0]
    q = jnp.concatenate(
        [q_ref[:, (g * GROUP + h) * HD : (g * GROUP + h + 1) * HD] for h in range(GROUP)], 0
    )
    s = lax.dot_general(q, key, NT, preferred_element_type=jnp.float32)
    keys = s.shape[1]
    s = s.reshape(GROUP, requests, keys)
    s = jnp.where((times > 0)[None], s, NEG).reshape(GROUP * requests, keys)
    m = jnp.maximum(jnp.max(s, axis=1, keepdims=True), m_old)
    p = jnp.exp2((s - m) * CEXP).reshape(GROUP, requests, keys) * times[None]
    p = p.reshape(GROUP * requests, keys)
    total = jnp.sum(p, axis=1, keepdims=True)
    new = jnp.dot(p.astype(jnp.bfloat16), val, preferred_element_type=jnp.float32)
    alpha = jnp.exp2((m_old - m) * CEXP)
    return m, l_old * alpha + total, acc_old * alpha + new


def decode_pool(dec_q, kv_pool, full, part, rest):
    slots, _, page, width = kv_pool.shape
    requests = dec_q.shape[0]
    heads_kv = width // HD
    block = 128 if slots % 128 == 0 else slots
    steps = slots // block

    def body(q_ref, kv_ref, full_ref, part_ref, rest_ref, acc_ref, m_ref, l_ref, token_ref):
        token_ref[0] = 0

        @pl.when(pl.program_id(0) == 0)
        def _():
            acc_ref[...] = jnp.zeros_like(acc_ref)
            m_ref[...] = jnp.full_like(m_ref, NEG)
            l_ref[...] = jnp.zeros_like(l_ref)

        times = token_counts(full_ref[...], part_ref[...], rest_ref[...], page)
        for g in range(heads_kv):
            cols = slice(g * HD, (g + 1) * HD)
            key = kv_ref[:, 0, :, cols].reshape(block * page, HD)
            val = kv_ref[:, 1, :, cols].reshape(block * page, HD)
            m, l, acc = decode_fold(
                q_ref, g, key, val, times, m_ref[g, :, 0:1], l_ref[g, :, 0:1], acc_ref[g]
            )
            m_ref[g] = jnp.broadcast_to(m, m_ref.shape[1:])
            l_ref[g] = jnp.broadcast_to(l, l_ref.shape[1:])
            acc_ref[g] = acc

    shape = (heads_kv, GROUP * requests, HD)
    whole = pl.BlockSpec(shape, lambda i: (0, 0, 0))
    return pl.pallas_call(
        body,
        grid=(steps,),
        out_shape=[jax.ShapeDtypeStruct(shape, jnp.float32)] * 3 + [jax.ShapeDtypeStruct((1,), jnp.int32)],
        in_specs=[
            pl.BlockSpec(dec_q.shape, lambda i: (0, 0)),
            pl.BlockSpec((block, 2, page, width), lambda i: (i, 0, 0, 0)),
            pl.BlockSpec((requests, block), lambda i: (0, i)),
            pl.BlockSpec((requests, block), lambda i: (0, i)),
            pl.BlockSpec(rest.shape, lambda i: (0, 0)),
        ],
        out_specs=[whole] * 3 + [SM],
        compiler_params=pltpu.CompilerParams(vmem_limit_bytes=POOL_LIMIT),
        cost_estimate=pl.CostEstimate(
            flops=4 * HD * heads_kv * GROUP * requests * slots * page,
            transcendentals=heads_kv * GROUP * requests * slots * page,
            bytes_accessed=slots * 2 * page * width * 2,
        ),
        name="decode_pool",
    )(dec_q, kv_pool, full, part, rest)


def fresh_rows(piece, which, cap, cols):
    rows = piece[which, cap:, :, cols]
    return rows.reshape(rows.shape[0] * rows.shape[1], HD)


def decode_fresh(dec_q, pieces, state, full, part, rest, cap):
    page, width = pieces[0].shape[2:]
    caps = pieces[0].shape[1] - cap
    n = len(pieces)
    heads_kv = width // HD
    rows = state[0].shape[1]

    def body(*refs):
        q_ref, acc_in, m_in, l_in, full_ref, part_ref, rest_ref = refs[:7]
        piece_refs = refs[7 : 7 + n]
        acc_ref, m_ref, l_ref = refs[7 + n :]
        times = token_counts(full_ref[...], part_ref[...], rest_ref[...], page)
        for g in range(heads_kv):
            cols = slice(g * HD, (g + 1) * HD)
            key = jnp.concatenate([fresh_rows(p, 0, 0, cols) for p in piece_refs], 0)
            val = jnp.concatenate([fresh_rows(p, 1, 0, cols) for p in piece_refs], 0)
            m, l, acc = decode_fold(
                q_ref, g, key, val, times, m_in[g, :, 0:1], l_in[g, :, 0:1], acc_in[g]
            )
            m_ref[g] = jnp.broadcast_to(m, m_ref.shape[1:])
            l_ref[g] = jnp.broadcast_to(l, l_ref.shape[1:])
            acc_ref[g] = acc

    whole = lambda a: pl.BlockSpec(a.shape, lambda i: (0,) * a.ndim)
    each = pieces[0].shape[1]
    return pl.pallas_call(
        body,
        grid=(1,),
        out_shape=[jax.ShapeDtypeStruct(a.shape, a.dtype) for a in state],
        in_specs=[whole(a) for a in (dec_q, *state, full, part, rest)]
        + [pl.BlockSpec((2, caps, page, width), lambda i: (0, each // caps - 1, 0, 0))] * n,
        out_specs=[whole(a) for a in state],
        compiler_params=PARAMS,
        cost_estimate=pl.CostEstimate(
            flops=4 * HD * heads_kv * rows * n * caps * page,
            transcendentals=heads_kv * rows * n * caps * page,
            bytes_accessed=n * caps * 2 * page * width * 2,
        ),
        name="decode_fresh",
    )(dec_q, *state, full, part, rest, *pieces)


def finish(dec_q, dec_state, times, q, fresh, pages, plen, state, pieces, ks, last, cap, size):
    page, width = fresh.shape[2:]
    caps = pieces[0].shape[1] - cap
    requests = dec_q.shape[0]
    heads_kv = width // HD
    tokens, qwidth = q.shape
    n, tail = len(pieces), len(last)
    keys = cap * page
    rows = min(128, tokens)
    held = n * keys

    def body(*refs):
        dq_ref, dacc_ref, dm_ref, dl_ref, times_ref, q_ref, f_ref, pages_ref, plen_ref = refs[:9]
        m_ref, acc_ref, l_ref = refs[9:12]
        last_refs = refs[12 : 12 + tail]
        piece_refs = refs[12 + tail : 12 + tail + n]
        (dec_ref, out_hbm, out_ref, sem, got_ref, got_sem, vis_ref, k_ref, v_ref, all_vis, all_k, all_v, page_ref, block_ref) = (
            refs[12 + tail + n :]
        )
        copies = fetch_pages(last_refs, got_ref, got_sem, cap + caps)
        start_pages(vis_ref, k_ref, v_ref, pages_ref, plen_ref, last, cap, page, size)
        for copy in copies:
            copy.wait()

        def out_copy(g):
            cols = pl.ds(pl.multiple_of(g * GROUP * HD, GROUP * HD), GROUP * HD)
            return pltpu.make_async_copy(out_ref.at[:, cols], out_hbm.at[:, cols], sem.at[g])

        def group(g, sums):
            stand_in = f_ref[0, 0, :, head_at(g)][0:1].astype(jnp.float32)
            for i in range(tail):
                place_keys(k_ref, v_ref, vis_ref, i * keys, i * keys, g, got_ref.at[i], stand_in, cap, page)
            partial = []

            def emit(cols, acc, total):
                total = l_ref[:, cols] + total
                out_ref[:, cols] = ((acc_ref[:, cols] + acc) * pl.reciprocal(total)).astype(out_ref.dtype)
                partial.append(jnp.sum(total.reshape(-1, 8, HD), axis=0))

            add_pages(k_ref, v_ref, q_ref, m_ref, g, emit)
            out_copy(g).start()
            return sum(partial, sums)

        sums = lax.fori_loop(0, heads_kv, group, jnp.zeros((8, HD), jnp.float32))

        times = times_ref[...]
        for g in range(heads_kv):
            cols = slice(g * HD, (g + 1) * HD)
            key = jnp.concatenate([fresh_rows(got_ref.at[i], 0, cap, cols) for i in range(tail)], 0)
            val = jnp.concatenate([fresh_rows(got_ref.at[i], 1, cap, cols) for i in range(tail)], 0)
            _, l, acc = decode_fold(
                dq_ref, g, key, val, times, dm_ref[g, :, 0:1], dl_ref[g, :, 0:1], dacc_ref[g]
            )
            done = (acc / l).astype(dec_ref.dtype)
            for h in range(GROUP):
                at = (g * GROUP + h) * HD
                dec_ref[:, at : at + HD] = done[h * requests : (h + 1) * requests]
        for g in range(heads_kv):
            out_copy(g).wait()

        @pl.when(jnp.logical_not(jnp.sum(sums) <= HUGE))
        def _():
            for i, k in enumerate(ks):
                mark_visible(all_vis, i * keys, k, cap, page, pages_ref, plen_ref, size)
            all_v[0:tokens, HD:] = jnp.ones((tokens, HD), jnp.bfloat16)
            all_v[tokens:, HD:] = all_vis[...].astype(jnp.bfloat16)
            col = lax.broadcasted_iota(jnp.int32, (rows, tokens), 1)
            row = lax.broadcasted_iota(jnp.int32, (rows, tokens), 0)

            def again(g, carry):
                all_k[0:tokens, :] = f_ref[:, 0, :, head_at(g)].reshape(tokens, HD)
                all_v[0:tokens, 0:HD] = f_ref[:, 1, :, head_at(g)].reshape(tokens, HD)
                stand_in = f_ref[0, 0, :, head_at(g)][0:1].astype(jnp.float32)
                for i in range(n):
                    pltpu.sync_copy(piece_refs[i].at[:, 0:cap], page_ref)
                    place_keys(all_k, all_v, all_vis, i * keys, tokens + i * keys, g, page_ref, stand_in, cap, page)

                def block(b, carry):
                    r = pl.multiple_of((b % (tokens // rows)) * rows, rows)
                    cols = head_at(g * GROUP + b // (tokens // rows))
                    qb = q_ref[pl.ds(r, rows), cols]
                    s = lax.dot_general(qb, all_k[...], NT, preferred_element_type=jnp.float32)
                    own = jnp.where(col <= row + r, s[:, :tokens], NEG)
                    s = jnp.concatenate([own, s[:, tokens:]], 1)
                    m = jnp.max(s, axis=1, keepdims=True)
                    p = jnp.exp2((s - m) * CEXP).astype(jnp.bfloat16)
                    new = jnp.dot(p, all_v[...], preferred_element_type=jnp.float32)
                    block_ref[...] = (new[:, :HD] / new[:, HD:]).astype(block_ref.dtype)
                    pltpu.sync_copy(block_ref, out_hbm.at[pl.ds(r, rows), cols])
                    return carry

                return lax.fori_loop(0, GROUP * (tokens // rows), block, carry)

            lax.fori_loop(0, heads_kv, again, 0)

    work = tokens * tail * keys * (qwidth // HD)
    return pl.pallas_call(
        body,
        out_shape=[
            jax.ShapeDtypeStruct(dec_q.shape, dec_q.dtype),
            jax.ShapeDtypeStruct(q.shape, q.dtype),
        ],
        in_specs=[VM] * 8 + [SM] + [VM] * 3 + [ANY] * (tail + n),
        out_specs=[VM, ANY],
        scratch_shapes=[
            pltpu.VMEM(q.shape, q.dtype),
            pltpu.SemaphoreType.DMA((heads_kv,)),
            pltpu.VMEM((tail, 2, cap + caps, page, width), q.dtype),
            pltpu.SemaphoreType.DMA((tail,)),
            pltpu.VMEM((tail * keys, HD), jnp.float32),
            pltpu.VMEM((tail * keys, 2 * HD), jnp.bfloat16),
            pltpu.VMEM((tail * keys, 2 * HD), jnp.bfloat16),
            pltpu.VMEM((held, HD), jnp.float32),
            pltpu.VMEM((tokens + held, HD), jnp.bfloat16),
            pltpu.VMEM((tokens + held, 2 * HD), jnp.bfloat16),
            pltpu.VMEM((2, cap, page, width), q.dtype),
            pltpu.VMEM((rows, HD), q.dtype),
        ],
        compiler_params=PARAMS,
        cost_estimate=pl.CostEstimate(
            flops=8 * HD * work, transcendentals=work, bytes_accessed=8 * work // HD
        ),
        name="finish",
    )(dec_q, *dec_state, times, q, fresh, pages, plen, *state, *[pieces[ks.index(k)] for k in last], *pieces)


def send_order(size):
    if size == 16:
        return [12, 8, 1, 2, 3, 4, 13, 5, 9, 6, 14, 7, 10, 15, 11]
    return list(range(1, size))


def shards(
    size,
    suffix_q,
    fresh_kv,
    kv_pool,
    dec_q,
    fetch_slots,
    prefix_pages,
    prefix_len,
    suffix_route,
    dec_pages,
    dec_len,
):
    page = kv_pool.shape[2]
    slots = kv_pool.shape[0]
    cap = fetch_slots.shape[1] // size
    caps = suffix_route.shape[1] // size
    sends = send_order(size)
    lead = max(1, size // 8)
    batches = [sends[:lead], sends[lead:] + [0]]
    outgoing, after = {}, []
    for ks in batches:
        outs = gather_pages(kv_pool, fresh_kv, fetch_slots, suffix_route, ks, size, after)
        after = outs[:1]
        outgoing |= dict(zip(ks, outs, strict=True))
    arrived = {0: outgoing[0]}
    for k in sends:
        pairs = [(i, i ^ k if size & (size - 1) == 0 else (i + k) % size) for i in range(size)]
        arrived[k] = lax.ppermute(outgoing[k], "pool", pairs)

    context = dec_pages.shape[1]
    position = jnp.arange(context, dtype=jnp.int32)[None, :]
    whole_pages = (position + 1) * page <= dec_len[:, None]
    edge_page = position == dec_len[:, None] // page
    rest = (dec_len % page)[:, None]

    def counts(names):
        same = dec_pages[:, :, None] == names[None, None, :]
        full = jnp.sum((same & whole_pages[:, :, None]).astype(jnp.float32), 1).astype(jnp.bfloat16)
        part = jnp.sum((same & edge_page[:, :, None]).astype(jnp.float32), 1).astype(jnp.bfloat16)
        return full, part

    groups = arrival_groups([0] + sends)
    order = [k for ks in groups for k in ks]
    early, last = order[: -len(groups[-1])], groups[-1]
    me = lax.axis_index("pool")

    def fresh_names(ks):
        srcs = source(jnp.full((len(ks),), me, jnp.int32), jnp.asarray(ks, jnp.int32), size)
        return slots + jnp.repeat(srcs, caps) * caps + jnp.tile(jnp.arange(caps, dtype=jnp.int32), len(ks))

    last_names = jnp.repeat(fresh_names(last), page)[None, None, :]
    last_token = (jnp.arange(last_names.shape[2], dtype=jnp.int32) % page)[None, None, :]
    last_seen = position[:, :, None] * page + last_token < dec_len[:, None, None]
    last_times = jnp.sum(((dec_pages[:, :, None] == last_names) & last_seen).astype(jnp.float32), 1)

    *dec_state, token = decode_pool(dec_q, kv_pool, *counts(jnp.arange(slots, dtype=jnp.int32)), rest)
    state = prefill_first(
        suffix_q,
        fresh_kv,
        [arrived[k] for k in groups[0]],
        groups[0],
        prefix_pages,
        prefix_len,
        token,
        cap,
        size,
    )
    for ks in groups[1:-1]:
        new = prefill_more(
            suffix_q, fresh_kv, [arrived[k] for k in ks], ks, prefix_pages, prefix_len, state, cap, size
        )
        state = (state[0], *new)
    dec_state = decode_fresh(
        dec_q, [arrived[k] for k in early], dec_state, *counts(fresh_names(early)), rest, cap
    )
    decode_out, suffix_out = finish(
        dec_q,
        dec_state,
        last_times,
        suffix_q,
        fresh_kv,
        prefix_pages,
        prefix_len,
        state,
        [arrived[k] for k in order],
        order,
        last,
        cap,
        size,
    )
    return (suffix_out, decode_out)


def arrival_groups(order):
    size = len(order)
    if size == 16:
        return [[0, 1, 2, 3, 12, 4, 8, 5], [13, 6, 9, 7], [14, 10], [15, 11]]
    per = -(-size // 4)
    return [order[i : min(i + per, size - 1)] for i in range(0, size - 1, per)] + [order[-1:]]


def solution(mesh):
    size = mesh.shape["pool"]
    return jax.shard_map(
        functools.partial(shards, size),
        mesh=mesh,
        in_specs=(
            P(("groups", "pool"), "tp"),
            P(("groups", "pool"), None, None, "tp"),
            P(("groups", "pool"), None, None, "tp"),
            P(("groups", "pool"), "tp"),
            P(("groups", "pool"), None),
            P(("groups", "pool"), None),
            P(("groups", "pool")),
            P(("groups", "pool"), None),
            P(("groups", "pool"), None),
            P(("groups", "pool")),
        ),
        out_specs=(P(("groups", "pool"), "tp"), P(("groups", "pool"), "tp")),
        check_vma=False,
    )
```

```python
import functools

import jax
import jax.numpy as jnp
from jax import lax
from jax.experimental import pallas as pl
from jax.experimental.pallas import tpu as pltpu
from jax.sharding import PartitionSpec as P

GROUP = 8
HD = 128
LOG2E = 1.4426950408889634
CEXP = HD**-0.5 * LOG2E
NEG = -1e30
HUGE = 2.0**90
VMEM_LIMIT = 12 << 20
POOL_LIMIT = 56 << 20
FIRST_LIMIT = 20 << 20


NT = (((1,), (1,)), ((), ()))
VM = pl.BlockSpec(memory_space=pltpu.VMEM)
SM = pl.BlockSpec(memory_space=pltpu.SMEM)
ANY = pl.BlockSpec(memory_space=pl.ANY)
HBM = pl.BlockSpec(memory_space=pltpu.HBM)
PARAMS = pltpu.CompilerParams(vmem_limit_bytes=VMEM_LIMIT)


def head_at(i):
    return pl.ds(pl.multiple_of(i * HD, HD), HD)


def partner(i, k, size):
    return i ^ k if size & (size - 1) == 0 else lax.rem(i + k, size)


def source(i, k, size):
    return i ^ k if size & (size - 1) == 0 else lax.rem(i - k + size, size)


def gather_pages(kv_pool, fresh_kv, fetch_slots, suffix_route, entries, size, after, halves):
    _, _, page, width = kv_pool.shape
    n = len(entries)
    part = width // halves
    cap, caps = fetch_slots.shape[1] // size, suffix_route.shape[1] // size
    each = cap + caps

    def body(slots_ref, routes_ref, pool_ref, fresh_ref, *rest):
        outs, sem = rest[-n - 1 : -1], rest[-1]
        me = lax.axis_index("pool")
        for i, (k, half) in enumerate(entries):
            dest = partner(me, k, size)
            cols = slice(None) if half is None else slice(half * part, (half + 1) * part)
            for c in range(cap):
                pltpu.make_async_copy(
                    pool_ref.at[slots_ref[0, dest * cap + c], :, :, cols], outs[i].at[:, c], sem.at[i]
                ).start()
            for c in range(caps):
                pltpu.make_async_copy(
                    fresh_ref.at[routes_ref[0, dest * caps + c], :, :, cols], outs[i].at[:, cap + c], sem.at[i]
                ).start()
        for i in range(n):
            pltpu.make_async_copy(outs[i], outs[i], sem.at[i]).wait()

    shapes = [(2, each, page, width if half is None else part) for _, half in entries]
    return pl.pallas_call(
        body,
        out_shape=[pltpu.VMEM(shape, kv_pool.dtype) for shape in shapes],
        in_specs=[SM, SM, HBM, HBM] + [ANY] * len(after),
        out_specs=[VM] * n,
        scratch_shapes=[pltpu.SemaphoreType.DMA((n,))],
        compiler_params=pltpu.CompilerParams(vmem_limit_bytes=POOL_LIMIT),
        cost_estimate=pl.CostEstimate(
            flops=0, transcendentals=0, bytes_accessed=2 * n * each * 2 * page * width * 2
        ),
        name="gather_pages",
    )(fetch_slots, suffix_route, kv_pool, fresh_kv, *after)


def mark_visible(vis_ref, at, k, cap, page, pages_ref, plen_ref, size):
    wanted = pages_ref[...]
    keys = cap * page
    order = lax.broadcasted_iota(jnp.int32, (keys, wanted.shape[1]), 1)
    token = lax.broadcasted_iota(jnp.int32, (keys, 1), 0)
    name = source(lax.axis_index("pool"), k, size) * cap + token // page
    place = jnp.sum(jnp.where(wanted == name, order, 0), axis=1, keepdims=True)
    seen = place * page + token % page < plen_ref[0]
    vis_ref[at : at + keys, :] = jnp.broadcast_to(jnp.where(seen, 1.0, 0.0), (keys, HD))


def place_keys(k_ref, v_ref, vis_ref, vis_at, at, column, piece, stand_in, cap, page):
    keys = cap * page
    rows = slice(at, at + keys)
    seen = vis_ref[vis_at : vis_at + keys, :] > 0
    key = piece[0, 0:cap, :, head_at(column)].reshape(keys, HD).astype(jnp.float32)
    val = piece[1, 0:cap, :, head_at(column)].reshape(keys, HD).astype(jnp.float32)
    k_ref[rows, 0:HD] = jnp.where(seen, key, stand_in).astype(jnp.bfloat16)
    v_ref[rows, 0:HD] = jnp.where(seen, val, 0.0).astype(jnp.bfloat16)


def fetch_pages(piece_refs, held, sem, cap):
    copies = [
        pltpu.make_async_copy(ref.at[:, 0:cap], held.at[i], sem.at[i]) for i, ref in enumerate(piece_refs)
    ]
    for copy in copies:
        copy.start()
    return copies


def prefill_first(q, fresh, pieces, ks, pages, plen, after, cap, size):
    tokens, qwidth = q.shape
    page, width = fresh.shape[2:]
    rows = min(256, tokens)
    n = len(pieces)
    each = cap * page
    held = n * each

    def body(*refs):
        plen_ref, pages_ref, q_ref, f_ref = refs[:4]
        piece_refs = refs[4 : 4 + n]
        _, m_ref, acc_ref, l_ref, got_ref, sem, vis_ref, k_ref, v_ref = refs[4 + n :]
        copies = fetch_pages(piece_refs, got_ref, sem, cap)
        for i, k in enumerate(ks):
            mark_visible(vis_ref, i * each, k, cap, page, pages_ref, plen_ref, size)
        v_ref[0:held, HD:] = vis_ref[...].astype(jnp.bfloat16)
        v_ref[held:, HD:] = jnp.ones((tokens, HD), jnp.bfloat16)
        k_lane = lax.broadcasted_iota(jnp.int32, (held + tokens, HD), 1)
        k_ref[:, HD:] = jnp.where(k_lane == 0, -1.0, 0.0).astype(jnp.bfloat16)
        row = lax.broadcasted_iota(jnp.int32, (rows, rows), 0)
        col = lax.broadcasted_iota(jnp.int32, (rows, rows), 1)
        lane = lax.broadcasted_iota(jnp.int32, (tokens, HD), 1)
        for copy in copies:
            copy.wait()

        def group(g, carry):
            key = f_ref[:, 0, :, head_at(g)].reshape(tokens, HD)
            k_ref[held:, 0:HD] = key
            v_ref[held:, 0:HD] = f_ref[:, 1, :, head_at(g)].reshape(tokens, HD)
            key = key.astype(jnp.float32)
            for i in range(n):
                at = i * each
                place_keys(k_ref, v_ref, vis_ref, at, at, g, got_ref.at[i], key[0:1], cap, page)
            for h in range(GROUP):
                cols = head_at(g * GROUP + h)
                own = jnp.sum(q_ref[:, cols].astype(jnp.float32) * key, axis=1, keepdims=True)
                m_ref[:, cols] = jnp.where(lane == 0, own, 0.0).astype(jnp.bfloat16)
            for h in range(GROUP):
                cols = head_at(g * GROUP + h)
                for r in range(0, tokens, rows):
                    rs = slice(r, r + rows)
                    shown = held + r + rows
                    lhs = jnp.concatenate([q_ref[rs, cols], m_ref[rs, cols]], 1)
                    s = lax.dot_general(lhs, k_ref[0:shown, :], NT, preferred_element_type=jnp.float32)
                    diag = jnp.where(col <= row, s[:, held + r :], NEG)
                    s = jnp.concatenate([s[:, : held + r], diag], 1)
                    p = jnp.exp2(s * CEXP).astype(jnp.bfloat16)
                    new = jnp.dot(p, v_ref[0:shown, :], preferred_element_type=jnp.float32)
                    acc_ref[rs, cols] = new[:, :HD]
                    l_ref[rs, cols] = new[:, HD:]
            return carry

        lax.fori_loop(0, width // HD, group, 0)

    wide = pltpu.VMEM((tokens, qwidth), jnp.float32)
    work = tokens * (tokens // 2 + held) * (qwidth // HD)
    return pl.pallas_call(
        body,
        out_shape=[pltpu.VMEM((tokens, qwidth), jnp.bfloat16), wide, wide],
        in_specs=[SM, VM, VM, VM] + [ANY] * n + [SM],
        out_specs=[VM] * 3,
        scratch_shapes=[
            pltpu.VMEM((n, 2, cap, page, width), q.dtype),
            pltpu.SemaphoreType.DMA((n,)),
            pltpu.VMEM((held, HD), jnp.float32),
            pltpu.VMEM((held + tokens, 2 * HD), jnp.bfloat16),
            pltpu.VMEM((held + tokens, 2 * HD), jnp.bfloat16),
        ],
        compiler_params=pltpu.CompilerParams(vmem_limit_bytes=FIRST_LIMIT),
        cost_estimate=pl.CostEstimate(flops=8 * HD * work, transcendentals=work, bytes_accessed=8 * work // HD),
        name="prefill_first",
    )(plen, pages, q, fresh, *pieces, after)


def add_pages(k_ref, v_ref, q_ref, m_ref, g, emit):
    for h in range(GROUP):
        cols = head_at(g * GROUP + h)
        lhs = jnp.concatenate([q_ref[:, cols], m_ref[:, cols]], 1)
        s = lax.dot_general(lhs, k_ref[...], NT, preferred_element_type=jnp.float32)
        p = jnp.exp2(s * CEXP).astype(jnp.bfloat16)
        new = jnp.dot(p, v_ref[...], preferred_element_type=jnp.float32)
        emit(cols, new[:, :HD], new[:, HD:])


def start_pages(vis_ref, k_ref, v_ref, pages_ref, plen_ref, ks, cap, page, size):
    keys = k_ref.shape[0]
    for i, k in enumerate(ks):
        mark_visible(vis_ref, i * cap * page, k, cap, page, pages_ref, plen_ref, size)
    lane = lax.broadcasted_iota(jnp.int32, (keys, HD), 1)
    k_ref[:, HD:] = jnp.where(lane == 0, -1.0, 0.0).astype(jnp.bfloat16)
    v_ref[:, HD:] = vis_ref[...].astype(jnp.bfloat16)


def prefill_more(q, fresh, pieces, ks, pages, plen, state, cap, size, lo, hi):
    tokens, qwidth = q.shape
    page, width = fresh.shape[2:]
    n = len(pieces)
    piece_width = pieces[0].shape[3]
    base = lo if piece_width < width else 0
    keys = n * cap * page

    def body(*refs):
        plen_ref, pages_ref, q_ref, f_ref = refs[:4]
        piece_refs = refs[4 : 4 + n]
        m_ref, acc_in, l_in, acc_ref, l_ref, got_ref, sem, vis_ref, k_ref, v_ref = refs[4 + n :]
        copies = fetch_pages(piece_refs, got_ref, sem, cap)
        start_pages(vis_ref, k_ref, v_ref, pages_ref, plen_ref, ks, cap, page, size)
        for copy in copies:
            copy.wait()

        def group(g, carry):
            stand_in = f_ref[0, 0, :, head_at(g)][0:1].astype(jnp.float32)
            for i in range(n):
                at = i * cap * page
                place_keys(k_ref, v_ref, vis_ref, at, at, g - base, got_ref.at[i], stand_in, cap, page)

            def emit(cols, acc, total):
                acc_ref[:, cols] = acc_in[:, cols] + acc
                l_ref[:, cols] = l_in[:, cols] + total

            add_pages(k_ref, v_ref, q_ref, m_ref, g, emit)
            return carry

        lax.fori_loop(lo, hi, group, 0)

    work = tokens * keys * (hi - lo) * GROUP
    wide = pltpu.VMEM((tokens, qwidth), jnp.float32)
    return pl.pallas_call(
        body,
        out_shape=[wide, wide],
        in_specs=[SM, VM, VM, VM] + [ANY] * n + [VM] * 3,
        out_specs=[VM, VM],
        input_output_aliases={5 + n: 0, 6 + n: 1},
        scratch_shapes=[
            pltpu.VMEM((n, 2, cap, page, piece_width), q.dtype),
            pltpu.SemaphoreType.DMA((n,)),
            pltpu.VMEM((keys, HD), jnp.float32),
            pltpu.VMEM((keys, 2 * HD), jnp.bfloat16),
            pltpu.VMEM((keys, 2 * HD), jnp.bfloat16),
        ],
        compiler_params=PARAMS,
        cost_estimate=pl.CostEstimate(
            flops=8 * HD * work, transcendentals=work, bytes_accessed=8 * work // HD
        ),
        name="prefill_more",
    )(plen, pages, q, fresh, *pieces, *state)


def token_counts(full, part, rest, page):
    pages = full.shape[1]
    key = lax.broadcasted_iota(jnp.int32, (pages, pages * page), 1) // page
    row = lax.broadcasted_iota(jnp.int32, (pages, pages * page), 0)
    spread = jnp.where(key == row, 1.0, 0.0).astype(jnp.bfloat16)
    times = jnp.dot(full, spread, preferred_element_type=jnp.float32)
    edge = jnp.dot(part, spread, preferred_element_type=jnp.float32)
    token = lax.broadcasted_iota(jnp.int32, times.shape, 1) % page
    return times + jnp.where(token < rest, edge, 0.0)


def decode_fold(q_ref, g, key, val, times, m_old, l_old, acc_old):
    requests = times.shape[0]
    q = jnp.concatenate(
        [q_ref[:, (g * GROUP + h) * HD : (g * GROUP + h + 1) * HD] for h in range(GROUP)], 0
    )
    s = lax.dot_general(q, key, NT, preferred_element_type=jnp.float32)
    keys = s.shape[1]
    s = s.reshape(GROUP, requests, keys)
    s = jnp.where((times > 0)[None], s, NEG).reshape(GROUP * requests, keys)
    m = jnp.maximum(jnp.max(s, axis=1, keepdims=True), m_old)
    p = jnp.exp2((s - m) * CEXP).reshape(GROUP, requests, keys) * times[None]
    p = p.reshape(GROUP * requests, keys)
    total = jnp.sum(p, axis=1, keepdims=True)
    new = jnp.dot(p.astype(jnp.bfloat16), val, preferred_element_type=jnp.float32)
    alpha = jnp.exp2((m_old - m) * CEXP)
    return m, l_old * alpha + total, acc_old * alpha + new


def decode_pool(dec_q, kv_pool, full, part, rest):
    slots, _, page, width = kv_pool.shape
    requests = dec_q.shape[0]
    heads_kv = width // HD
    block = 128 if slots % 128 == 0 else slots
    steps = slots // block

    def body(q_ref, kv_ref, full_ref, part_ref, rest_ref, acc_ref, m_ref, l_ref, token_ref):
        token_ref[0] = 0

        @pl.when(pl.program_id(0) == 0)
        def _():
            acc_ref[...] = jnp.zeros_like(acc_ref)
            m_ref[...] = jnp.full_like(m_ref, NEG)
            l_ref[...] = jnp.zeros_like(l_ref)

        times = token_counts(full_ref[...], part_ref[...], rest_ref[...], page)
        for g in range(heads_kv):
            cols = slice(g * HD, (g + 1) * HD)
            key = kv_ref[:, 0, :, cols].reshape(block * page, HD)
            val = kv_ref[:, 1, :, cols].reshape(block * page, HD)
            m, l, acc = decode_fold(
                q_ref, g, key, val, times, m_ref[g, :, 0:1], l_ref[g, :, 0:1], acc_ref[g]
            )
            m_ref[g] = jnp.broadcast_to(m, m_ref.shape[1:])
            l_ref[g] = jnp.broadcast_to(l, l_ref.shape[1:])
            acc_ref[g] = acc

    shape = (heads_kv, GROUP * requests, HD)
    whole = pl.BlockSpec(shape, lambda i: (0, 0, 0))
    return pl.pallas_call(
        body,
        grid=(steps,),
        out_shape=[jax.ShapeDtypeStruct(shape, jnp.float32)] * 3 + [jax.ShapeDtypeStruct((1,), jnp.int32)],
        in_specs=[
            pl.BlockSpec(dec_q.shape, lambda i: (0, 0)),
            pl.BlockSpec((block, 2, page, width), lambda i: (i, 0, 0, 0)),
            pl.BlockSpec((requests, block), lambda i: (0, i)),
            pl.BlockSpec((requests, block), lambda i: (0, i)),
            pl.BlockSpec(rest.shape, lambda i: (0, 0)),
        ],
        out_specs=[whole] * 3 + [SM],
        compiler_params=pltpu.CompilerParams(vmem_limit_bytes=POOL_LIMIT),
        cost_estimate=pl.CostEstimate(
            flops=4 * HD * heads_kv * GROUP * requests * slots * page,
            transcendentals=heads_kv * GROUP * requests * slots * page,
            bytes_accessed=slots * 2 * page * width * 2,
        ),
        name="decode_pool",
    )(dec_q, kv_pool, full, part, rest)


def fresh_rows(piece, which, cap, cols):
    rows = piece[which, cap:, :, cols]
    return rows.reshape(rows.shape[0] * rows.shape[1], HD)


def decode_fresh(dec_q, pieces, state, full, part, rest, cap):
    page, width = pieces[0].shape[2:]
    caps = pieces[0].shape[1] - cap
    n = len(pieces)
    heads_kv = width // HD
    rows = state[0].shape[1]

    def body(*refs):
        q_ref, acc_in, m_in, l_in, full_ref, part_ref, rest_ref = refs[:7]
        piece_refs = refs[7 : 7 + n]
        acc_ref, m_ref, l_ref = refs[7 + n :]
        times = token_counts(full_ref[...], part_ref[...], rest_ref[...], page)
        for g in range(heads_kv):
            cols = slice(g * HD, (g + 1) * HD)
            key = jnp.concatenate([fresh_rows(p, 0, 0, cols) for p in piece_refs], 0)
            val = jnp.concatenate([fresh_rows(p, 1, 0, cols) for p in piece_refs], 0)
            m, l, acc = decode_fold(
                q_ref, g, key, val, times, m_in[g, :, 0:1], l_in[g, :, 0:1], acc_in[g]
            )
            m_ref[g] = jnp.broadcast_to(m, m_ref.shape[1:])
            l_ref[g] = jnp.broadcast_to(l, l_ref.shape[1:])
            acc_ref[g] = acc

    whole = lambda a: pl.BlockSpec(a.shape, lambda i: (0,) * a.ndim)
    each = pieces[0].shape[1]
    return pl.pallas_call(
        body,
        grid=(1,),
        out_shape=[jax.ShapeDtypeStruct(a.shape, a.dtype) for a in state],
        in_specs=[whole(a) for a in (dec_q, *state, full, part, rest)]
        + [pl.BlockSpec((2, caps, page, width), lambda i: (0, each // caps - 1, 0, 0))] * n,
        out_specs=[whole(a) for a in state],
        compiler_params=PARAMS,
        cost_estimate=pl.CostEstimate(
            flops=4 * HD * heads_kv * rows * n * caps * page,
            transcendentals=heads_kv * rows * n * caps * page,
            bytes_accessed=n * caps * 2 * page * width * 2,
        ),
        name="decode_fresh",
    )(dec_q, *state, full, part, rest, *pieces)


def finish(dec_q, dec_state, times, q, fresh, pages, plen, state, sums, split, tail, lo, hi, before, arrived, cap, size):
    page, width = fresh.shape[2:]
    ks = list(split)
    piece_width = split[ks[0]].shape[3]
    caps = split[ks[0]].shape[1] - cap
    requests = dec_q.shape[0]
    heads_kv = width // HD
    tokens, _ = q.shape
    n = len(ks)
    keys = cap * page
    rows = min(128, tokens)
    last = before is not None or hi - lo == heads_kv
    names = list(arrived) if last else []
    distances = sorted({k for k, _ in names})
    held = len(distances) * keys
    span = GROUP * HD

    def body(*refs):
        dq_ref, dacc_ref, dm_ref, dl_ref, times_ref, q_ref, f_ref, pages_ref, plen_ref = refs[:9]
        m_ref, acc_ref, l_ref, sums_ref = refs[9:13]
        split_refs = refs[13 : 13 + n]
        piece_refs = dict(zip(names, refs[13 + n : 13 + n + len(names)]))
        refs = refs[13 + n + len(names) + (0 if before is None else 2) :]
        dec_hbm, out_hbm, sums_out, dec_ref, out_ref, sem, got_ref, got_sem, vis_ref, k_ref, v_ref = refs[:11]
        copies = fetch_pages(split_refs, got_ref, got_sem, cap + caps)
        start_pages(vis_ref, k_ref, v_ref, pages_ref, plen_ref, tail, cap, page, size)
        for copy in copies:
            copy.wait()

        def out_copy(g):
            mine = pl.ds(pl.multiple_of((g - lo) * span, span), span)
            cols = pl.ds(pl.multiple_of(g * span, span), span)
            return pltpu.make_async_copy(out_ref.at[:, mine], out_hbm.at[:, cols], sem.at[g - lo])

        def group(g, sums):
            stand_in = f_ref[0, 0, :, head_at(g)][0:1].astype(jnp.float32)
            for i, k in enumerate(tail):
                place_keys(
                    k_ref, v_ref, vis_ref, i * keys, i * keys, g - lo, got_ref.at[ks.index(k)], stand_in, cap, page
                )
            partial = []

            def emit(cols, acc, total):
                mine = head_at((g - lo) * GROUP + len(partial))
                total = l_ref[:, cols] + total
                out_ref[:, mine] = ((acc_ref[:, cols] + acc) * pl.reciprocal(total)).astype(out_ref.dtype)
                partial.append(jnp.sum(total.reshape(-1, 8, HD), axis=0))

            add_pages(k_ref, v_ref, q_ref, m_ref, g, emit)
            out_copy(g).start()
            return sum(partial, sums)

        sums = lax.fori_loop(lo, hi, group, sums_ref[...])
        sums_out[...] = sums

        times = times_ref[...]
        for g in range(lo, hi):
            cols = slice((g - lo) * HD, (g - lo + 1) * HD)
            key = jnp.concatenate([fresh_rows(got_ref.at[i], 0, cap, cols) for i in range(n)], 0)
            val = jnp.concatenate([fresh_rows(got_ref.at[i], 1, cap, cols) for i in range(n)], 0)
            _, l, acc = decode_fold(
                dq_ref, g, key, val, times, dm_ref[g, :, 0:1], dl_ref[g, :, 0:1], dacc_ref[g]
            )
            done = (acc / l).astype(dec_ref.dtype)
            for h in range(GROUP):
                at = ((g - lo) * GROUP + h) * HD
                dec_ref[:, at : at + HD] = done[h * requests : (h + 1) * requests]
        dec_copy = pltpu.make_async_copy(dec_ref, dec_hbm.at[:, lo * span : hi * span], sem.at[hi - lo])
        dec_copy.start()
        dec_copy.wait()
        for g in range(lo, hi):
            out_copy(g).wait()
        if not last:
            return
        all_vis, all_k, all_v, page_ref, half_ref, block_ref = refs[11:]

        @pl.when(jnp.logical_not(jnp.sum(sums) <= HUGE))
        def _():
            for i, k in enumerate(distances):
                mark_visible(all_vis, i * keys, k, cap, page, pages_ref, plen_ref, size)
            all_v[0:tokens, HD:] = jnp.ones((tokens, HD), jnp.bfloat16)
            all_v[tokens:, HD:] = all_vis[...].astype(jnp.bfloat16)
            col = lax.broadcasted_iota(jnp.int32, (rows, tokens), 1)
            row = lax.broadcasted_iota(jnp.int32, (rows, tokens), 0)
            step = hi - lo

            def again(half, g, carry):
                all_k[0:tokens, :] = f_ref[:, 0, :, head_at(g)].reshape(tokens, HD)
                all_v[0:tokens, 0:HD] = f_ref[:, 1, :, head_at(g)].reshape(tokens, HD)
                stand_in = f_ref[0, 0, :, head_at(g)][0:1].astype(jnp.float32)
                for i, k in enumerate(distances):
                    whole = (k, None) in piece_refs
                    ref = piece_refs[(k, None if whole else half)]
                    into = page_ref if whole else half_ref
                    pltpu.sync_copy(ref.at[:, 0:cap], into)
                    column = g if whole else g - half * step
                    place_keys(all_k, all_v, all_vis, i * keys, tokens + i * keys, column, into, stand_in, cap, page)

                def block(b, carry):
                    r = pl.multiple_of((b % (tokens // rows)) * rows, rows)
                    cols = head_at(g * GROUP + b // (tokens // rows))
                    qb = q_ref[pl.ds(r, rows), cols]
                    s = lax.dot_general(qb, all_k[...], NT, preferred_element_type=jnp.float32)
                    own = jnp.where(col <= row + r, s[:, :tokens], NEG)
                    s = jnp.concatenate([own, s[:, tokens:]], 1)
                    m = jnp.max(s, axis=1, keepdims=True)
                    p = jnp.exp2((s - m) * CEXP).astype(jnp.bfloat16)
                    new = jnp.dot(p, all_v[...], preferred_element_type=jnp.float32)
                    block_ref[...] = (new[:, :HD] / new[:, HD:]).astype(block_ref.dtype)
                    pltpu.sync_copy(block_ref, out_hbm.at[pl.ds(r, rows), cols])
                    return carry

                lax.fori_loop(0, GROUP * (tokens // rows), block, 0)
                return carry

            for half in range(heads_kv // step):
                lax.fori_loop(half * step, (half + 1) * step, functools.partial(again, half), 0)

    work = tokens * len(tail) * keys * (hi - lo) * GROUP
    scratch = [
        pltpu.VMEM((requests, (hi - lo) * span), dec_q.dtype),
        pltpu.VMEM((tokens, (hi - lo) * span), q.dtype),
        pltpu.SemaphoreType.DMA((hi - lo + 1,)),
        pltpu.VMEM((n, 2, cap + caps, page, piece_width), q.dtype),
        pltpu.SemaphoreType.DMA((n,)),
        pltpu.VMEM((len(tail) * keys, HD), jnp.float32),
        pltpu.VMEM((len(tail) * keys, 2 * HD), jnp.bfloat16),
        pltpu.VMEM((len(tail) * keys, 2 * HD), jnp.bfloat16),
    ]
    if last:
        scratch += [
            pltpu.VMEM((held, HD), jnp.float32),
            pltpu.VMEM((tokens + held, HD), jnp.bfloat16),
            pltpu.VMEM((tokens + held, 2 * HD), jnp.bfloat16),
            pltpu.VMEM((2, cap, page, width), q.dtype),
            pltpu.VMEM((2, cap, page, piece_width), q.dtype),
            pltpu.VMEM((rows, HD), q.dtype),
        ]
    operands = [dec_q, *dec_state, times, q, fresh, pages, plen, *state, sums, *split.values()]
    operands += [arrived[name] for name in names]
    aliases = {}
    if before is not None:
        aliases = {len(operands): 0, len(operands) + 1: 1}
        operands += list(before)
    return pl.pallas_call(
        body,
        out_shape=[
            jax.ShapeDtypeStruct(dec_q.shape, dec_q.dtype),
            jax.ShapeDtypeStruct(q.shape, q.dtype),
            jax.ShapeDtypeStruct(sums.shape, sums.dtype),
        ],
        in_specs=[VM] * 8 + [SM] + [VM] * 4 + [ANY] * (len(operands) - 13),
        out_specs=[ANY, ANY, VM],
        input_output_aliases=aliases,
        scratch_shapes=scratch,
        compiler_params=PARAMS,
        cost_estimate=pl.CostEstimate(
            flops=8 * HD * work, transcendentals=work, bytes_accessed=8 * work // HD
        ),
        name="finish",
    )(*operands)


def halves_of(width):
    return 2 if (width // HD) % 2 == 0 else 1


def send_order(size):
    if size == 16:
        return [12, 8, 1, 2, 3, 4, 13, 5, 9, 6, 7], [14, 10, 15, 11]
    cut = size - max(1, size // 4)
    return list(range(1, cut)), list(range(cut, size))


def send_entries(size, halves):
    sends, split = send_order(size)
    return [(k, None) for k in sends] + [(k, half) for half in range(halves) for k in split]


def shards(
    size,
    suffix_q,
    fresh_kv,
    kv_pool,
    dec_q,
    fetch_slots,
    prefix_pages,
    prefix_len,
    suffix_route,
    dec_pages,
    dec_len,
):
    page = kv_pool.shape[2]
    slots = kv_pool.shape[0]
    cap = fetch_slots.shape[1] // size
    caps = suffix_route.shape[1] // size
    halves = halves_of(kv_pool.shape[3])
    sends, split = send_order(size)
    entries = send_entries(size, halves)
    lead = max(1, size // 8)
    batches = [entries[:lead], entries[lead:] + [(0, None)]]
    outgoing, after = {}, []
    for batch in batches:
        outs = gather_pages(kv_pool, fresh_kv, fetch_slots, suffix_route, batch, size, after, halves)
        after = outs[:1]
        outgoing |= dict(zip(batch, outs, strict=True))
    arrived = {(0, None): outgoing[(0, None)]}
    for k, half in entries:
        pairs = [(i, i ^ k if size & (size - 1) == 0 else (i + k) % size) for i in range(size)]
        arrived[(k, half)] = lax.ppermute(outgoing[(k, half)], "pool", pairs)

    context = dec_pages.shape[1]
    position = jnp.arange(context, dtype=jnp.int32)[None, :]
    whole_pages = (position + 1) * page <= dec_len[:, None]
    edge_page = position == dec_len[:, None] // page
    rest = (dec_len % page)[:, None]

    def counts(names):
        same = dec_pages[:, :, None] == names[None, None, :]
        full = jnp.sum((same & whole_pages[:, :, None]).astype(jnp.float32), 1).astype(jnp.bfloat16)
        part = jnp.sum((same & edge_page[:, :, None]).astype(jnp.float32), 1).astype(jnp.bfloat16)
        return full, part

    groups = arrival_groups(sends)
    early, last = [k for ks in groups for k in ks], split
    me = lax.axis_index("pool")

    def fresh_names(ks):
        srcs = source(jnp.full((len(ks),), me, jnp.int32), jnp.asarray(ks, jnp.int32), size)
        return slots + jnp.repeat(srcs, caps) * caps + jnp.tile(jnp.arange(caps, dtype=jnp.int32), len(ks))

    last_names = jnp.repeat(fresh_names(last), page)[None, None, :]
    last_token = (jnp.arange(last_names.shape[2], dtype=jnp.int32) % page)[None, None, :]
    last_seen = position[:, :, None] * page + last_token < dec_len[:, None, None]
    last_times = jnp.sum(((dec_pages[:, :, None] == last_names) & last_seen).astype(jnp.float32), 1)

    *dec_state, token = decode_pool(dec_q, kv_pool, *counts(jnp.arange(slots, dtype=jnp.int32)), rest)
    state = prefill_first(
        suffix_q,
        fresh_kv,
        [arrived[(k, None)] for k in groups[0]],
        groups[0],
        prefix_pages,
        prefix_len,
        token,
        cap,
        size,
    )

    def more(state, ks, half, lo, hi):
        pieces = [arrived[(k, half)] for k in ks]
        new = prefill_more(
            suffix_q, fresh_kv, pieces, ks, prefix_pages, prefix_len, state, cap, size, lo, hi
        )
        return (state[0], *new)

    heads_kv = kv_pool.shape[3] // HD
    for ks in groups[1:]:
        state = more(state, ks, None, 0, heads_kv)
    dec_state = decode_fresh(
        dec_q, [arrived[(k, None)] for k in early], dec_state, *counts(fresh_names(early)), rest, cap
    )
    before, sums = None, jnp.zeros((8, HD), jnp.float32)
    per = heads_kv // halves
    for half in range(halves):
        lo, hi = half * per, (half + 1) * per
        tail = split
        if half == halves - 1 and len(split) > 1:
            tail = split[len(split) // 2 :]
            state = more(state, split[: len(split) // 2], half, lo, hi)
        *before, sums = finish(
            dec_q,
            dec_state,
            last_times,
            suffix_q,
            fresh_kv,
            prefix_pages,
            prefix_len,
            state,
            sums,
            {k: arrived[(k, half)] for k in split},
            tail,
            lo,
            hi,
            before,
            arrived,
            cap,
            size,
        )
    decode_out, suffix_out = before
    return (suffix_out, decode_out)


def arrival_groups(sends):
    if len(sends) == 11:
        return [[0, 1, 2, 3, 12, 4, 8, 5], [13, 6, 9, 7]]
    order = [0] + sends
    cut = 2 * len(order) // 3
    return [order[:cut], order[cut:]]


def solution(mesh):
    size = mesh.shape["pool"]
    return jax.shard_map(
        functools.partial(shards, size),
        mesh=mesh,
        in_specs=(
            P(("groups", "pool"), "tp"),
            P(("groups", "pool"), None, None, "tp"),
            P(("groups", "pool"), None, None, "tp"),
            P(("groups", "pool"), "tp"),
            P(("groups", "pool"), None),
            P(("groups", "pool"), None),
            P(("groups", "pool")),
            P(("groups", "pool"), None),
            P(("groups", "pool"), None),
            P(("groups", "pool")),
        ),
        out_specs=(P(("groups", "pool"), "tp"), P(("groups", "pool"), "tp")),
        check_vma=False,
    )
```
